256 devices in a mesh: theta: 128 (over z, y_lo, x, core), gz: 2 (over y_hi).
Axes of the slice: x: 4, y: 4 (y_hi: 2, y_lo: 2; y = y_hi * 2 + y_lo), z: 8, core: 2. Of those that a mesh axis runs over, the one named last changes fastest.
Arguments:
- velocity: float32 [3, 2048, 16, 512], P(None, 'theta', 'gz'), may hold values from -2 to 3.5
- radial_op: float32 [512, 544], replicated, may hold values from -0.25 to 0.25
- azimuth_stencil: float32 [21], replicated, may hold values from -1.25 to 1.25
- viscous_factor: float32 [1], replicated, may hold values from 1000000 to 10000000
Outputs:
- new_velocity: float32 [3, 2048, 16, 512], P(None, 'theta', 'gz')
- nonlinear: float32 [3, 2048, 16, 512], P(None, 'theta', 'gz')
The draws below stay inside these ranges and needn't reach their ends.
All inputs are finite; a program needn't handle non-finite values.
Results may differ from the reference program's by a relative error of at most 0.000098.
Values sent between devices are 32-bit elements; how exact they have to be, the bound alone decides.
A program may use at most 64 MiB of HBM per device.

```python
import math
import jax
import jax.numpy as jnp
from jax import lax

NR = 512
RT = 32
AZ_REACH = 10
NT = 2048
NZ = 16


def draw_velocity(key, part):
    radius = (jnp.arange(NR).astype(jnp.float32) + 0.5) / NR
    profile = 1.5 * (1.0 - radius * radius)
    fluctuation = 0.5 * jax.random.truncated_normal(key, -4.0, 4.0, (3, NT, NZ, NR), jnp.float32)
    mean_flow = jnp.stack([jnp.zeros_like(profile), jnp.zeros_like(profile), profile])
    return fluctuation + mean_flow[:, None, None, :]


def scatter_about(rng, shape, spread, reach, held_as=jnp.bfloat16):
    return jnp.clip(spread * jax.random.normal(rng, shape, jnp.float32), -reach, reach).astype(held_as)


def setup_inputs(seed: int = 0) -> dict:
    streams_of = jax.random.split(jax.random.key(seed), 5)
    return {
        "velocity": draw_velocity(jax.random.fold_in(streams_of[4], 71), 0),
        "radial_op": scatter_about(streams_of[1], (NR, NR + RT), (NR + RT) ** -0.5, 0.25, jnp.float32),
        "azimuth_stencil": scatter_about(streams_of[2], (2 * AZ_REACH + 1,), (2 * AZ_REACH + 1) ** -0.5, 1.25, jnp.float32),
        "viscous_factor": jnp.clip(jnp.exp(jax.random.uniform(streams_of[3], (1,), jnp.float32, math.log(1000000), math.log(10000000))), 1000000, 10000000),
    }


AXIAL_WEIGHTS = (0.75, -0.15, 1.0 / 60.0)
STEP_WEIGHT = 0.2
MIRROR_SIGNS = (-1.0, -1.0, 1.0)


def reference(velocity, radial_op, azimuth_stencil, viscous_factor):
    highest = lax.Precision.HIGHEST
    radius = jnp.arange(NR).astype(jnp.float32) + 0.5
    inverse_r = 1.0 / radius
    sign_flip = jnp.array(MIRROR_SIGNS, jnp.float32).reshape(3, 1, 1, 1)
    mirror = sign_flip * jnp.roll(velocity[:, :, :, :RT], -(NT // 2), axis=1)
    radial_grad = jnp.einsum("ctzj,ij->ctzi", velocity, radial_op[:, :NR], precision=highest)
    radial_grad = radial_grad + jnp.einsum("ctzj,ij->ctzi", mirror, radial_op[:, NR:], precision=highest)
    theta_grad = jnp.zeros_like(velocity)
    for shift_by in range(-AZ_REACH, AZ_REACH + 1):
        theta_grad = theta_grad + azimuth_stencil[shift_by + AZ_REACH] * jnp.roll(velocity, -shift_by, axis=1)
    axial_grad = jnp.zeros_like(velocity)
    for position, weight in enumerate(AXIAL_WEIGHTS):
        shift_by = position + 1
        axial_grad = axial_grad + weight * (jnp.roll(velocity, -shift_by, axis=2) - jnp.roll(velocity, shift_by, axis=2))
    radial_vel = velocity[0]
    azimuth_vel = velocity[1]
    axial_vel = velocity[2]
    convective = radial_vel[None] * radial_grad + (azimuth_vel * inverse_r)[None] * theta_grad + axial_vel[None] * axial_grad
    metric = jnp.stack([-azimuth_vel * azimuth_vel * inverse_r, radial_vel * azimuth_vel * inverse_r, jnp.zeros_like(axial_vel)])
    nonlinear = convective + metric
    right_side = velocity - STEP_WEIGHT * nonlinear
    implicit_coef = viscous_factor[0] * inverse_r * inverse_r
    spectrum = jnp.fft.rfft(right_side, axis=1)
    wavenumber = jnp.arange(NT // 2 + 1).astype(jnp.float32)
    half_sine = jnp.sin(jnp.pi * wavenumber / NT)
    eigenvalue = 1.0 + 4.0 * implicit_coef[None, :] * (half_sine * half_sine)[:, None]
    new_velocity = jnp.fft.irfft(spectrum / eigenvalue[None, :, None, :], n=NT, axis=1).astype(jnp.float32)
    return (new_velocity, nonlinear)
```

```python
import functools

import jax
import jax.numpy as jnp
from jax import lax
from jax.experimental import pallas as pl
from jax.experimental.pallas import tpu as pltpu
from jax.sharding import PartitionSpec as P

AXIAL_WEIGHTS = (0.75, -0.15, 1.0 / 60.0)
STEP_WEIGHT = 0.2
MIRROR_SIGNS = (-1.0, -1.0, 1.0)
MESH = pl.DeviceIdType.MESH
F32 = jnp.float32
BF16 = jnp.bfloat16
REACH = 10
PTS = 16
NR = 512
RT = 32
LANES = 128
TILES = NR // LANES
GROUP = 8
SECTORS = 128
BLOCKS = SECTORS // GROUP
NT_DOT = (((1,), (1,)), ((), ()))


def split(x):
    high = x.astype(BF16)
    return high, (x - high.astype(F32)).astype(BF16)


def dot3(x, w_high, w_low):
    high, low = split(x)
    out = lax.dot_general(high, w_low, NT_DOT, preferred_element_type=F32)
    out = out + lax.dot_general(low, w_high, NT_DOT, preferred_element_type=F32)
    return out + lax.dot_general(high, w_high, NT_DOT, preferred_element_type=F32)


def sublane(shape):
    return lax.broadcasted_iota(jnp.int32, shape, len(shape) - 2)


def lane(shape):
    return lax.broadcasted_iota(jnp.int32, shape, len(shape) - 1)


def doubled(q):
    return q * (2.0 - q)


def kernel(
    v_hbm, op_hbm, sten, visc, new_hbm, non_hbm,
    ext, op_v, wh, wl, gsend, grecv, msend, mrecv, part, rhs, loc,
    rho_t, inv_t, pw_t, w_t, big_t, inv_n, fb, up_in, tot, car,
    in_sem, halo_s, halo_r, gz_s, gz_r, mir_s, mir_r, p1_s, p1_r, p2_s, p2_r, p3_s, p3_r, out_sem,
):
    p = lax.axis_index("theta")
    g = lax.axis_index("gz")
    me = p % GROUP
    block = p // GROUP
    backward = me // TILES
    my_tile = me % TILES

    reads = [
        pltpu.make_async_copy(v_hbm.at[c], ext.at[c, pl.ds(REACH, PTS)], in_sem.at[c]) for c in range(3)
    ]
    reads.append(pltpu.make_async_copy(op_hbm, op_v, in_sem.at[3]))
    for r in reads:
        r.start()

    after = (p + 1) % SECTORS
    before = (p + SECTORS - 1) % SECTORS
    across = (p + SECTORS // 2) % SECTORS
    group_peers = [block * GROUP + (me + k) % GROUP for k in range(1, GROUP)]
    block_peers = [((block + k) % BLOCKS) * GROUP + me for k in range(1, BLOCKS)]
    barrier = pltpu.get_barrier_semaphore()
    greeted = [(p, 1 - g), (after, g), (before, g)]
    greeted += [(q, g) for q in group_peers + block_peers]
    for who in greeted:
        pl.semaphore_signal(barrier, inc=1, device_id=who, device_id_type=MESH)

    for c in range(3):
        reads[c].wait()

    sub = sublane((8, NR))
    middle = (sub == 3) | (sub == 4)

    def pack(i, carry):
        for c in range(3):
            x = [ext[c, REACH + 4 * i + j] for j in range(4)]
            gsend[c, 3 * i] = jnp.where(middle, pltpu.roll(x[3], 3, 0), x[0])
            gsend[c, 3 * i + 1] = jnp.where(
                sub == 3, pltpu.roll(x[3], 1, 0), jnp.where(sub == 4, pltpu.roll(x[3], 7, 0), x[1])
            )
            gsend[c, 3 * i + 2] = jnp.where(middle, pltpu.roll(x[3], 5, 0), x[2])
            quarter = lane((8, LANES)) // RT
            line = x[0][:, :LANES]
            for j in range(1, 4):
                line = jnp.where(quarter == j, pltpu.roll(x[j][:, :LANES], RT * j, 1), line)
            msend[c, i] = MIRROR_SIGNS[c] * line
        return carry

    lax.fori_loop(0, 4, pack, 0)

    pl.semaphore_wait(barrier, len(greeted))

    def remote(src, dst, s_sem, r_sem, who):
        return pltpu.make_async_remote_copy(
            src_ref=src, dst_ref=dst, send_sem=s_sem, recv_sem=r_sem, device_id=who, device_id_type=MESH
        )

    halos, planes, mirrors = [], [], []
    for c in range(3):
        planes.append(remote(gsend.at[c], grecv.at[c], gz_s.at[c], gz_r.at[c], (p, 1 - g)))
        halos.append(
            (
                remote(
                    ext.at[c, pl.ds(PTS, REACH)], ext.at[c, pl.ds(0, REACH)],
                    halo_s.at[c, 0], halo_r.at[c, 0], (after, g),
                ),
                remote(
                    ext.at[c, pl.ds(REACH, REACH)], ext.at[c, pl.ds(REACH + PTS, REACH)],
                    halo_s.at[c, 1], halo_r.at[c, 1], (before, g),
                ),
            )
        )
        mirrors.append(remote(msend.at[c], mrecv.at[c], mir_s.at[c], mir_r.at[c], (across, g)))
        mirrors[c].start()
        halos[c][0].start()
        halos[c][1].start()
        planes[c].start()

    radius = lane((8, NR)).astype(F32) + 0.5
    inverse_r = 1.0 / radius
    inv_t[...] = inverse_r
    coef = visc[0] * inverse_r * inverse_r
    half = 0.5 / coef
    gap = jnp.sqrt(half * (2.0 + half)) - half
    rho = 1.0 - gap
    rho_t[...] = rho
    scale = 1.0 / jnp.sqrt(1.0 + 4.0 * coef)
    power = scale
    for j in range(PTS):
        power = power * rho
        pw_t[j] = power
    gap16 = doubled(doubled(doubled(doubled(gap))))
    gap128 = doubled(doubled(doubled(gap16)))
    whole = doubled(doubled(doubled(doubled(gap128))))
    for t in range(TILES):
        cols = slice(t * LANES, (t + 1) * LANES)
        w_t[t] = 1.0 - gap16[:, cols]
        big_t[t] = 1.0 - gap128[:, cols]
        inv_n[t] = 1.0 / whole[:, cols]

    reads[3].wait()
    op_high, op_low = split(op_v[...])
    wh[...] = op_high
    wl[...] = op_low
    for c in range(3):
        lines = ext[c, pl.ds(REACH, PTS)].reshape(PTS * 8, NR)
        part[c] = dot3(lines, wh[:, :NR], wl[:, :NR]).reshape(PTS, 8, NR)

    def first_half(c):
        mirrors[c].wait_recv()

        def unpack(i, carry):
            packed = mrecv[c, i]
            lines = [packed[:, :RT]] + [pltpu.roll(packed, LANES - RT * j, 1)[:, :RT] for j in range(1, 4)]
            lines = jnp.concatenate(lines, axis=0)
            more = dot3(lines, wh[:, NR:], wl[:, NR:]).reshape(4, 8, NR)
            rows = pl.ds(4 * i, 4)
            part[c, rows] = part[c, rows] + more
            return carry

        lax.fori_loop(0, 4, unpack, 0)
        halos[c][0].wait_recv()
        halos[c][1].wait_recv()

        def azimuth(i, carry):
            inv = inv_t[...]
            for t in range(4):
                row = 4 * i + t
                grad = sten[0] * ext[c, row]
                for m in range(1, 2 * REACH + 1):
                    grad = grad + sten[m] * ext[c, row + m]
                a, b = ext[0, REACH + row], ext[1, REACH + row]
                turn = b * inv
                term = a * part[c, row] + turn * grad
                if c == 0:
                    term = term - b * turn
                if c == 1:
                    term = term + a * turn
                part[c, row] = term
            return carry

        lax.fori_loop(0, 4, azimuth, 0)

    def second_half(c):
        planes[c].wait_recv()

        def axial(i, left):
            packed = [grecv[c, 3 * i + j] for j in range(3)]
            other = packed + [
                jnp.where(
                    sub < 2,
                    pltpu.roll(packed[0], 5, 0),
                    jnp.where(
                        sub == 2,
                        pltpu.roll(packed[1], 7, 0),
                        jnp.where(sub == 5, pltpu.roll(packed[1], 1, 0), pltpu.roll(packed[2], 3, 0)),
                    ),
                )
            ]
            rho = rho_t[...]
            for t in range(4):
                row = 4 * i + t
                own, far = ext[c, REACH + row], other[t]
                grad = jnp.zeros_like(own)
                for m, weight in enumerate(AXIAL_WEIGHTS, 1):
                    upper = pltpu.roll(jnp.where(sub < m, far, own), 8 - m, 0)
                    lower = pltpu.roll(jnp.where(sub >= 8 - m, far, own), m, 0)
                    grad = grad + weight * (upper - lower)
                term = part[c, row] + ext[2, REACH + row] * grad
                part[c, row] = term
                right = own - STEP_WEIGHT * term
                rhs[c, row] = right
                left = right + rho * left
                loc[c, row] = left - right
            return left

        left = lax.fori_loop(0, 4, axial, jnp.zeros((8, NR), F32))

        def back(i, carry):
            rho = rho_t[...]
            for t in range(4):
                row = PTS - 1 - 4 * i - t
                carry = rhs[c, row] + rho * carry
                loc[c, row] = loc[c, row] + carry
            return carry

        back_sum = lax.fori_loop(0, 4, back, jnp.zeros((8, NR), F32))
        for t in range(TILES):
            cols = slice(t * LANES, (t + 1) * LANES)
            fb[c, t] = left[:, cols]
            fb[c, TILES + t] = back_sum[:, cols]

    def start_group(c):
        copies = []
        for k in range(1, GROUP):
            other = (me + k) % GROUP
            cp = remote(
                fb.at[c, other], up_in.at[c, me], p1_s.at[c, k - 1], p1_r.at[c, k - 1],
                (block * GROUP + other, g),
            )
            cp.start()
            copies.append(cp)
        up_in[c, me] = fb[c, me]
        return copies

    def entry(c, k):
        return up_in[c, k + backward * (GROUP - 1 - 2 * k)]

    def start_blocks(c, arrivals):
        for cp in arrivals:
            cp.wait_recv()
        w = w_t[my_tile]
        run = entry(c, 0)
        for k in range(1, GROUP):
            run = entry(c, k) + w * run
        tot[c, block] = run
        copies = []
        for k in range(1, BLOCKS):
            cp = remote(
                tot.at[c, block], tot.at[c, block], p2_s.at[c, k - 1], p2_r.at[c, k - 1],
                (((block + k) % BLOCKS) * GROUP + me, g),
            )
            cp.start()
            copies.append(cp)
        return copies

    def start_return(c, arrivals):
        for cp in arrivals:
            cp.wait_recv()
        big = big_t[my_tile]
        run = tot[c, block]
        for m in range(BLOCKS - 1, 0, -1):
            run = tot[c, (block + (2 * backward - 1) * m + BLOCKS) % BLOCKS] + big * run
        run = run * inv_n[my_tile]
        w = w_t[my_tile]
        out = up_in
        for k in range(GROUP):
            here = k + backward * (GROUP - 1 - 2 * k)
            value = up_in[c, here]
            out[c, here] = run
            run = value + w * run
        copies = []
        for k in range(1, GROUP):
            other = (me + k) % GROUP
            cp = remote(
                up_in.at[c, other], car.at[c, me], p3_s.at[c, k - 1], p3_r.at[c, k - 1],
                (block * GROUP + other, g),
            )
            cp.start()
            copies.append(cp)
        car[c, me] = up_in[c, me]
        return copies

    def finish(c, arrivals):
        for cp in arrivals:
            cp.wait_recv()
        scale = 1.0 / jnp.sqrt(1.0 + 4.0 * (visc[0] * inv_t[...] * inv_t[...]))
        from_left = jnp.concatenate([car[c, t] for t in range(TILES)], axis=1)
        from_right = jnp.concatenate([car[c, TILES + t] for t in range(TILES)], axis=1)

        def last(i, carry):
            for t in range(4):
                row = 4 * i + t
                loc[c, row] = (
                    scale * loc[c, row] + pw_t[row] * from_left + pw_t[PTS - 1 - row] * from_right
                )
            return carry

        lax.fori_loop(0, 4, last, 0)

    def write(c, src, dst, k):
        cp = pltpu.make_async_copy(src.at[c], dst.at[c], out_sem.at[k, c])
        cp.start()
        return cp

    writes = []
    first_half(0)
    second_half(0)
    one = [start_group(0), None, None]
    writes.append(write(0, part, non_hbm, 1))
    first_half(1)
    second_half(1)
    one[1] = start_group(1)
    two = [start_blocks(0, one[0]), None, None]
    writes.append(write(1, part, non_hbm, 1))
    first_half(2)
    second_half(2)
    one[2] = start_group(2)
    two[1] = start_blocks(1, one[1])
    three = [start_return(0, two[0]), None, None]
    writes.append(write(2, part, non_hbm, 1))
    two[2] = start_blocks(2, one[2])
    three[1] = start_return(1, two[1])
    finish(0, three[0])
    writes.append(write(0, loc, new_hbm, 0))
    three[2] = start_return(2, two[2])
    finish(1, three[1])
    writes.append(write(1, loc, new_hbm, 0))
    finish(2, three[2])
    writes.append(write(2, loc, new_hbm, 0))
    for c in range(3):
        for cp in (planes[c], mirrors[c], *halos[c], *one[c], *two[c], *three[c]):
            cp.wait_send()
    for cp in writes:
        cp.wait()


def local(velocity, radial_op, azimuth_stencil, viscous_factor):
    dma = pltpu.SemaphoreType.DMA
    block = velocity.shape
    any_space = pl.BlockSpec(memory_space=pl.ANY)
    scalars = pl.BlockSpec(memory_space=pltpu.SMEM)
    tile = (8, LANES)
    return pl.pallas_call(
        kernel,
        name="substep",
        out_shape=(jax.ShapeDtypeStruct(block, F32), jax.ShapeDtypeStruct(block, F32)),
        in_specs=[any_space, any_space, scalars, scalars],
        out_specs=(any_space, any_space),
        scratch_shapes=[
            pltpu.VMEM((3, PTS + 2 * REACH, 8, NR), F32),
            pltpu.VMEM((NR, NR + RT), F32),
            pltpu.VMEM((NR, NR + RT), BF16),
            pltpu.VMEM((NR, NR + RT), BF16),
            pltpu.VMEM((3, 12, 8, NR), F32),
            pltpu.VMEM((3, 12, 8, NR), F32),
            pltpu.VMEM((3, 4, *tile), F32),
            pltpu.VMEM((3, 4, *tile), F32),
            pltpu.VMEM(block, F32),
            pltpu.VMEM(block, F32),
            pltpu.VMEM(block, F32),
            pltpu.VMEM((8, NR), F32),
            pltpu.VMEM((8, NR), F32),
            pltpu.VMEM((PTS, 8, NR), F32),
            pltpu.VMEM((TILES, *tile), F32),
            pltpu.VMEM((TILES, *tile), F32),
            pltpu.VMEM((TILES, *tile), F32),
            pltpu.VMEM((3, GROUP, *tile), F32),
            pltpu.VMEM((3, GROUP, *tile), F32),
            pltpu.VMEM((3, BLOCKS, *tile), F32),
            pltpu.VMEM((3, GROUP, *tile), F32),
            dma((4,)),
            dma((3, 2)), dma((3, 2)),
            dma((3,)), dma((3,)),
            dma((3,)), dma((3,)),
            dma((3, GROUP - 1)), dma((3, GROUP - 1)),
            dma((3, BLOCKS - 1)), dma((3, BLOCKS - 1)),
            dma((3, GROUP - 1)), dma((3, GROUP - 1)),
            dma((2, 3)),
        ],
        compiler_params=pltpu.CompilerParams(
            collective_id=0, has_side_effects=True, vmem_limit_bytes=40 << 20
        ),
    )(velocity, radial_op, azimuth_stencil, viscous_factor)


def solution(mesh):
    spec = P(None, "theta", "gz", None)
    return jax.shard_map(
        local, mesh=mesh, in_specs=(spec, P(), P(), P()), out_specs=(spec, spec), check_vma=False
    )
```

```python
import jax
import jax.numpy as jnp
from jax import lax
from jax.experimental import pallas as pl
from jax.experimental.pallas import tpu as pltpu
from jax.sharding import PartitionSpec as P

AXIAL_WEIGHTS = (0.75, -0.15, 1.0 / 60.0)
STEP_WEIGHT = 0.2
MIRROR_SIGNS = (-1.0, -1.0, 1.0)
MESH = pl.DeviceIdType.MESH
F32 = jnp.float32
BF16 = jnp.bfloat16
REACH = 10
PTS = 16
NR = 512
RT = 32
LANES = 128
TILES = NR // LANES
GROUP = 8
SECTORS = 128
BLOCKS = SECTORS // GROUP
PLAIN_DOT = (((1,), (0,)), ((), ()))


def split(x):
    high = x.astype(BF16)
    return high, (x - high.astype(F32)).astype(BF16)


def dot3(x, w_high, w_low):
    high, low = split(x)
    out = lax.dot_general(high, w_low, PLAIN_DOT, preferred_element_type=F32)
    out = out + lax.dot_general(low, w_high, PLAIN_DOT, preferred_element_type=F32)
    return out + lax.dot_general(high, w_high, PLAIN_DOT, preferred_element_type=F32)


def rows_of(shape):
    return lax.broadcasted_iota(jnp.int32, shape, len(shape) - 2)


def lane(shape):
    return lax.broadcasted_iota(jnp.int32, shape, len(shape) - 1)


def doubled(q):
    return q * (2.0 - q)


def pack4(x, sub):
    middle = (sub == 3) | (sub == 4)
    return (
        jnp.where(middle, pltpu.roll(x[3], 3, 0), x[0]),
        jnp.where(sub == 3, pltpu.roll(x[3], 1, 0), jnp.where(sub == 4, pltpu.roll(x[3], 7, 0), x[1])),
        jnp.where(middle, pltpu.roll(x[3], 5, 0), x[2]),
    )


def unpack4(y, sub):
    fourth = jnp.where(
        sub < 2,
        pltpu.roll(y[0], 5, 0),
        jnp.where(
            sub == 2,
            pltpu.roll(y[1], 7, 0),
            jnp.where(sub == 5, pltpu.roll(y[1], 1, 0), pltpu.roll(y[2], 3, 0)),
        ),
    )
    return (y[0], y[1], y[2], fourth)


def axial_parts(x, sub):
    own = far = None
    for m, weight in enumerate(AXIAL_WEIGHTS, 1):
        upper = weight * pltpu.roll(x, 8 - m, 0)
        lower = weight * pltpu.roll(x, m, 0)
        inside = jnp.where(sub < 8 - m, upper, 0.0) - jnp.where(sub >= m, lower, 0.0)
        outside = jnp.where(sub < 8 - m, 0.0, upper) - jnp.where(sub >= m, 0.0, lower)
        own = inside if own is None else own + inside
        far = outside if far is None else far + outside
    return own, far


def kernel(
    v_hbm, op_hbm, sten, visc, new_hbm, non_hbm,
    ext, op_v, wh, wl, esend, erecv, gsend, grecv, msend, mrecv, part, own_ax, far_ax, loc,
    inv_t, pow_t, scale_t, w_t, big_t, inv_n, ssend, srecv, fb, up_in, ret, tot, car,
    in_sem, e_sem, mir_sem, up_sem, down_sem, g_sem, sum_sem, p1_s, p1_r, p2_s, p2_r, p3_s, p3_r, out_sem,
):
    p = lax.axis_index("theta")
    g = lax.axis_index("gz")
    me = p % GROUP
    block = p // GROUP
    backward = me // TILES
    my_tile = me % TILES
    sub = rows_of((8, LANES))

    reads = [
        pltpu.make_async_copy(v_hbm, ext.at[:, pl.ds(REACH, PTS)], in_sem.at[0]),
        pltpu.make_async_copy(op_hbm, op_v, in_sem.at[1]),
    ]
    for r in reads:
        r.start()

    after = (p + 1) % SECTORS
    before = (p + SECTORS - 1) % SECTORS
    across = (p + SECTORS // 2) % SECTORS
    barrier = pltpu.get_barrier_semaphore()
    greeted = [(p, 1 - g), (after, g), (before, g)]
    greeted += [(block * GROUP + (me + k) % GROUP, g) for k in range(1, GROUP)]
    greeted += [(((block + k) % BLOCKS) * GROUP + me, g) for k in range(1, BLOCKS)]
    for who in greeted:
        pl.semaphore_signal(barrier, inc=1, device_id=who, device_id_type=MESH)

    def cols(t):
        return pl.ds(pl.multiple_of(t * LANES, LANES), LANES)

    reads[0].wait()

    def pack_axial(t, carry):
        for i in range(PTS // 4):
            x = [ext[2, REACH + 4 * i + j, :, cols(t)] for j in range(4)]
            for j, y in enumerate(pack4(x, sub)):
                esend[3 * i + j, :, cols(t)] = y
        return carry

    lax.fori_loop(0, TILES, pack_axial, 0)
    quarter = lane((8, LANES)) // RT
    for c in range(3):
        for i in range(PTS // 4):
            line = ext[c, REACH + 4 * i, :, :LANES]
            for j in range(1, 4):
                line = jnp.where(quarter == j, pltpu.roll(ext[c, REACH + 4 * i + j, :, :LANES], RT * j, 1), line)
            msend[c, i] = MIRROR_SIGNS[c] * line

    pl.semaphore_wait(barrier, len(greeted))

    def remote(src, dst, s_sem, r_sem, who):
        return pltpu.make_async_remote_copy(
            src_ref=src, dst_ref=dst, send_sem=s_sem, recv_sem=r_sem, device_id=who, device_id_type=MESH
        )

    def pair(src, dst, sem, who):
        return remote(src, dst, sem.at[0], sem.at[1], who)

    planes_e = pair(esend, erecv, e_sem, (p, 1 - g))
    halo_up = pair(ext.at[:, pl.ds(PTS, REACH)], ext.at[:, pl.ds(0, REACH)], up_sem, (after, g))
    halo_down = pair(ext.at[:, pl.ds(REACH, REACH)], ext.at[:, pl.ds(REACH + PTS, REACH)], down_sem, (before, g))
    mirror = pair(msend, mrecv, mir_sem, (across, g))
    sums = pair(ssend, srecv, sum_sem, (p, 1 - g))
    planes = [
        remote(gsend.at[c], grecv.at[c], g_sem.at[0, c], g_sem.at[1, c], (p, 1 - g)) for c in range(2)
    ]
    planes_e.start()
    halo_up.start()
    halo_down.start()
    mirror.start()

    radius = lane((8, NR)).astype(F32) + 0.5
    inverse_r = 1.0 / radius
    coef = visc[0] * inverse_r * inverse_r
    half = 0.5 / coef
    gap = jnp.sqrt(half * (2.0 + half)) - half
    rho = 1.0 - gap
    scale = 1.0 / jnp.sqrt(1.0 + 4.0 * coef)
    gap16 = doubled(doubled(doubled(doubled(gap))))
    gap128 = doubled(doubled(doubled(gap16)))
    whole = doubled(doubled(doubled(doubled(gap128))))
    for t in range(TILES):
        here = slice(t * LANES, (t + 1) * LANES)
        inv_t[t] = inverse_r[:, here]
        scale_t[t] = scale[:, here]
        w_t[t] = 1.0 - gap16[:, here]
        big_t[t] = 1.0 - gap128[:, here]
        inv_n[t] = 1.0 / whole[:, here]
        power = jnp.ones((8, LANES), F32)
        for j in range(PTS + 1):
            pow_t[t, j] = power
            power = power * rho[:, here]

    def spread(t, carry):
        for c in range(3):
            for i in range(PTS // 4):
                far = []
                for j in range(4):
                    row = 4 * i + j
                    inside, outside = axial_parts(ext[c, REACH + row, :, cols(t)], sub)
                    own_ax[c, row, :, cols(t)] = inside
                    far_ax[c, row, :, cols(t)] = outside
                    far.append(outside)
                if c < 2:
                    for j, y in enumerate(pack4(far, sub)):
                        gsend[c, 3 * i + j, :, cols(t)] = y
        return carry

    lax.fori_loop(0, TILES, spread, 0)

    reads[1].wait()
    op_high, op_low = split(op_v[...])
    wh[...] = op_high
    wl[...] = op_low
    for c in range(3):
        lines = ext[c, pl.ds(REACH, PTS)].reshape(PTS * 8, NR)
        part[c] = dot3(lines, wh[pl.ds(0, NR)], wl[pl.ds(0, NR)]).reshape(PTS, 8, NR)

    planes_e.wait_recv()

    def partner_sums(t, carry):
        rho = pow_t[t, 1]
        e = []
        for i in range(PTS // 4):
            e += unpack4([erecv[3 * i + j, :, cols(t)] for j in range(3)], sub)
        for c in range(3):
            ahead = back = None
            for row in range(PTS):
                x = e[row] * far_ax[c, row, :, cols(t)]
                ahead = x if row == 0 else rho * ahead + x
                back = x if row == 0 else back + pow_t[t, row] * x
            ssend[t, c] = ahead
            ssend[TILES + t, c] = back
        return carry

    lax.fori_loop(0, TILES, partner_sums, 0)
    sums.start()
    for cp in planes:
        cp.start()

    mirror.wait_recv()

    def across_axis(i, carry):
        lines = []
        for c in range(3):
            packed = mrecv[c, i]
            lines += [packed[:, :RT]] + [pltpu.roll(packed, LANES - RT * j, 1)[:, :RT] for j in range(1, 4)]
        more = dot3(jnp.concatenate(lines, axis=0), wh[pl.ds(NR, RT)], wl[pl.ds(NR, RT)]).reshape(3, 4, 8, NR)
        rows = pl.ds(4 * i, 4)
        for c in range(3):
            part[c, rows] = part[c, rows] + more[c]
        return carry

    lax.fori_loop(0, PTS // 4, across_axis, 0)
    halo_up.wait_recv()
    halo_down.wait_recv()

    def azimuth(t, carry):
        inv, rho = inv_t[t], pow_t[t, 1]
        for c in range(3):
            x = [ext[c, k, :, cols(t)] for k in range(PTS + 2 * REACH)]
            ahead = back = None
            for row in range(PTS):
                grad = sten[0] * x[row]
                for m in range(1, 2 * REACH + 1):
                    grad = grad + sten[m] * x[row + m]
                a = ext[0, REACH + row, :, cols(t)]
                b = ext[1, REACH + row, :, cols(t)]
                e = ext[2, REACH + row, :, cols(t)]
                turn = b * inv
                if c == 0:
                    grad = grad - b
                if c == 1:
                    grad = grad + a
                term = a * part[c, row, :, cols(t)] + turn * grad + e * own_ax[c, row, :, cols(t)]
                part[c, row, :, cols(t)] = term
                right = x[REACH + row] - STEP_WEIGHT * term
                ahead = right if row == 0 else rho * ahead + right
                back = right if row == 0 else back + pow_t[t, row] * right
            fb[t, c] = ahead
            fb[TILES + t, c] = back
        return carry

    lax.fori_loop(0, TILES, azimuth, 0)

    sums.wait_recv()
    for k in range(GROUP):
        fb[k] = fb[k] - STEP_WEIGHT * srecv[k]

    one, two, three = [], [], []
    for k in range(1, GROUP):
        other = (me + k) % GROUP
        cp = remote(fb.at[other], up_in.at[me], p1_s.at[k - 1], p1_r.at[k - 1], (block * GROUP + other, g))
        cp.start()
        one.append(cp)
    up_in[me] = fb[me]

    def finish_term(c):
        def body(t, carry):
            rho = pow_t[t, 1]
            right = []
            left = []
            for i in range(PTS // 4):
                if c < 2:
                    far = unpack4([grecv[c, 3 * i + j, :, cols(t)] for j in range(3)], sub)
                else:
                    far = unpack4([erecv[3 * i + j, :, cols(t)] for j in range(3)], sub)
                for j in range(4):
                    row = 4 * i + j
                    grad = far[j]
                    if c == 2:
                        grad = axial_parts(grad, sub)[1]
                    else:
                        grad = jnp.where((sub == 3) | (sub == 4), 0.0, grad)
                    term = part[c, row, :, cols(t)] + ext[2, REACH + row, :, cols(t)] * grad
                    part[c, row, :, cols(t)] = term
                    right.append(ext[c, REACH + row, :, cols(t)] - STEP_WEIGHT * term)
                    left.append(right[row] if row == 0 else right[row] + rho * left[row - 1])
            run = None
            for row in range(PTS - 1, -1, -1):
                if run is None:
                    loc[c, row, :, cols(t)] = left[row]
                    run = right[row]
                else:
                    run = rho * run
                    loc[c, row, :, cols(t)] = left[row] + run
                    run = right[row] + run
            return carry

        lax.fori_loop(0, TILES, body, 0)

    def write(src, dst, k):
        cp = pltpu.make_async_copy(src, dst, out_sem.at[k])
        cp.start()
        return cp

    def entry(k):
        return k + backward * (GROUP - 1 - 2 * k)

    for cp in one:
        cp.wait_recv()
    w = w_t[my_tile]
    run = up_in[entry(0)]
    for k in range(1, GROUP):
        run = up_in[entry(k)] + w * run
    tot[block] = run
    for k in range(1, BLOCKS):
        cp = remote(
            tot.at[block], tot.at[block], p2_s.at[k - 1], p2_r.at[k - 1],
            (((block + k) % BLOCKS) * GROUP + me, g),
        )
        cp.start()
        two.append(cp)

    finish_term(2)
    writes = [write(part.at[2], non_hbm.at[2], 0)]

    for cp in two:
        cp.wait_recv()
    big = big_t[my_tile]
    run = tot[block]
    for m in range(BLOCKS - 1, 0, -1):
        run = tot[(block + (2 * backward - 1) * m + BLOCKS) % BLOCKS] + big * run
    run = run * inv_n[my_tile]
    for k in range(GROUP):
        ret[entry(k)] = run
        run = up_in[entry(k)] + w * run
    for k in range(1, GROUP):
        other = (me + k) % GROUP
        cp = remote(ret.at[other], car.at[me], p3_s.at[k - 1], p3_r.at[k - 1], (block * GROUP + other, g))
        cp.start()
        three.append(cp)
    car[me] = ret[me]

    for c in range(2):
        planes[c].wait_recv()
        finish_term(c)
        writes.append(write(part.at[c], non_hbm.at[c], 1 + c))

    for cp in three:
        cp.wait_recv()

    def last(t, carry):
        scale = scale_t[t]
        for c in range(3):
            from_left = scale * car[t, c]
            from_right = scale * car[TILES + t, c]
            for row in range(PTS):
                loc[c, row, :, cols(t)] = (
                    scale * loc[c, row, :, cols(t)]
                    + pow_t[t, row + 1] * from_left
                    + pow_t[t, PTS - row] * from_right
                )
        return carry

    lax.fori_loop(0, TILES, last, 0)
    writes.append(write(loc, new_hbm, 3))
    for cp in (planes_e, halo_up, halo_down, mirror, sums, *planes, *one, *two, *three):
        cp.wait_send()
    for cp in writes:
        cp.wait()


def local(velocity, radial_op, azimuth_stencil, viscous_factor):
    dma = pltpu.SemaphoreType.DMA
    block = velocity.shape
    any_space = pl.BlockSpec(memory_space=pl.ANY)
    scalars = pl.BlockSpec(memory_space=pltpu.SMEM)
    tile = (8, LANES)
    return pl.pallas_call(
        kernel,
        name="substep",
        out_shape=(jax.ShapeDtypeStruct(block, F32), jax.ShapeDtypeStruct(block, F32)),
        in_specs=[any_space, any_space, scalars, scalars],
        out_specs=(any_space, any_space),
        scratch_shapes=[
            pltpu.VMEM((3, PTS + 2 * REACH, 8, NR), F32),
            pltpu.VMEM((NR + RT, NR), F32),
            pltpu.VMEM((NR + RT, NR), BF16),
            pltpu.VMEM((NR + RT, NR), BF16),
            pltpu.VMEM((12, 8, NR), F32),
            pltpu.VMEM((12, 8, NR), F32),
            pltpu.VMEM((2, 12, 8, NR), F32),
            pltpu.VMEM((2, 12, 8, NR), F32),
            pltpu.VMEM((3, 4, *tile), F32),
            pltpu.VMEM((3, 4, *tile), F32),
            pltpu.VMEM(block, F32),
            pltpu.VMEM(block, F32),
            pltpu.VMEM(block, F32),
            pltpu.VMEM(block, F32),
            pltpu.VMEM((TILES, *tile), F32),
            pltpu.VMEM((TILES, PTS + 1, *tile), F32),
            pltpu.VMEM((TILES, *tile), F32),
            pltpu.VMEM((TILES, *tile), F32),
            pltpu.VMEM((TILES, *tile), F32),
            pltpu.VMEM((TILES, *tile), F32),
            pltpu.VMEM((GROUP, 3, *tile), F32),
            pltpu.VMEM((GROUP, 3, *tile), F32),
            pltpu.VMEM((GROUP, 3, *tile), F32),
            pltpu.VMEM((GROUP, 3, *tile), F32),
            pltpu.VMEM((GROUP, 3, *tile), F32),
            pltpu.VMEM((BLOCKS, 3, *tile), F32),
            pltpu.VMEM((GROUP, 3, *tile), F32),
            dma((2,)),
            dma((2,)), dma((2,)), dma((2,)), dma((2,)),
            dma((2, 2)), dma((2,)),
            dma((GROUP - 1,)), dma((GROUP - 1,)),
            dma((BLOCKS - 1,)), dma((BLOCKS - 1,)),
            dma((GROUP - 1,)), dma((GROUP - 1,)),
            dma((4,)),
        ],
        compiler_params=pltpu.CompilerParams(
            collective_id=0, has_side_effects=True, vmem_limit_bytes=40 << 20
        ),
    )(velocity, radial_op.T, azimuth_stencil, viscous_factor)


def solution(mesh):
    spec = P(None, "theta", "gz", None)
    return jax.shard_map(
        local, mesh=mesh, in_specs=(spec, P(), P(), P()), out_specs=(spec, spec), check_vma=False
    )
```

```python
import jax
import jax.numpy as jnp
from jax import lax
from jax.experimental import pallas as pl
from jax.experimental.pallas import tpu as pltpu
from jax.sharding import PartitionSpec as P

AXIAL_WEIGHTS = (0.75, -0.15, 1.0 / 60.0)
STEP_WEIGHT = 0.2
MIRROR_SIGNS = (-1.0, -1.0, 1.0)
MESH = pl.DeviceIdType.MESH
F32 = jnp.float32
BF16 = jnp.bfloat16
REACH = 10
PTS = 16
NR = 512
RT = 32
LANES = 128
TILES = NR // LANES
GROUP = 8
SECTORS = 128
BLOCKS = SECTORS // GROUP
ROWS = (range(0, REACH), range(PTS - REACH, PTS))
PLAIN_DOT = (((1,), (0,)), ((), ()))


def split(x):
    high = x.astype(BF16)
    return high, (x - high.astype(F32)).astype(BF16)


def dot3(x, w_high, w_low):
    high, low = split(x)
    out = lax.dot_general(high, w_low, PLAIN_DOT, preferred_element_type=F32)
    out = out + lax.dot_general(low, w_high, PLAIN_DOT, preferred_element_type=F32)
    return out + lax.dot_general(high, w_high, PLAIN_DOT, preferred_element_type=F32)


def rows_of(shape):
    return lax.broadcasted_iota(jnp.int32, shape, len(shape) - 2)


def lane(shape):
    return lax.broadcasted_iota(jnp.int32, shape, len(shape) - 1)


def doubled(q):
    return q * (2.0 - q)


def pack4(x, sub):
    middle = (sub == 3) | (sub == 4)
    return (
        jnp.where(middle, pltpu.roll(x[3], 3, 0), x[0]),
        jnp.where(sub == 3, pltpu.roll(x[3], 1, 0), jnp.where(sub == 4, pltpu.roll(x[3], 7, 0), x[1])),
        jnp.where(middle, pltpu.roll(x[3], 5, 0), x[2]),
    )


def unpack4(y, sub):
    fourth = jnp.where(
        sub < 2,
        pltpu.roll(y[0], 5, 0),
        jnp.where(
            sub == 2,
            pltpu.roll(y[1], 7, 0),
            jnp.where(sub == 5, pltpu.roll(y[1], 1, 0), pltpu.roll(y[2], 3, 0)),
        ),
    )
    return (y[0], y[1], y[2], fourth)


def axial_parts(x, sub):
    own = far = None
    for m, weight in enumerate(AXIAL_WEIGHTS, 1):
        upper = weight * pltpu.roll(x, 8 - m, 0)
        lower = weight * pltpu.roll(x, m, 0)
        inside = jnp.where(sub < 8 - m, upper, 0.0) - jnp.where(sub >= m, lower, 0.0)
        outside = jnp.where(sub < 8 - m, 0.0, upper) - jnp.where(sub >= m, 0.0, lower)
        own = inside if own is None else own + inside
        far = outside if far is None else far + outside
    return own, far


def kernel(
    v_hbm, op_hbm, sten, visc, new_hbm, non_hbm,
    ext, op_v, wh, wl, esend, erecv, gsend, grecv, msend, mrecv, part, own_ax, far_ax, loc,
    inv_t, pow_t, scale_t, w_t, big_t, inv_n, ssend, sum_in, hsend, halo_in, fb, up_in, ret, tot, car,
    in_sem, e_sem, mir_sem, up_sem, down_sem, g_sem, v_s, v_r, h_s, h_r,
    p1_s, p1_r, p2_s, p2_r, p3_s, p3_r, out_sem,
):
    p = lax.axis_index("theta")
    g = lax.axis_index("gz")
    me = p % GROUP
    block = p // GROUP
    backward = me // TILES
    my_tile = me % TILES
    sub = rows_of((8, LANES))

    reads = [
        pltpu.make_async_copy(v_hbm, ext.at[:, pl.ds(REACH, PTS)], in_sem.at[0]),
        pltpu.make_async_copy(op_hbm, op_v, in_sem.at[1]),
    ]
    for r in reads:
        r.start()

    after = (p + 1) % SECTORS
    before = (p + SECTORS - 1) % SECTORS
    across = (p + SECTORS // 2) % SECTORS
    barrier = pltpu.get_barrier_semaphore()
    greeted = [(after, g), (before, g)]
    greeted += [(block * GROUP + (me + k) % GROUP, g) for k in range(1, GROUP)]
    greeted += [(block * GROUP + (me + k) % GROUP, 1 - g) for k in range(GROUP)]
    greeted += [(((block + k) % BLOCKS) * GROUP + me, g) for k in range(1, BLOCKS)]
    greeted += [(((block + BLOCKS - 1) % BLOCKS) * GROUP + GROUP - 1, g), (((block + 1) % BLOCKS) * GROUP, g)]
    at_edge = me // (GROUP - 1) + (GROUP - 1 - me) // (GROUP - 1)
    for who in greeted:
        pl.semaphore_signal(barrier, inc=1, device_id=who, device_id_type=MESH)

    def cols(t):
        return pl.ds(pl.multiple_of(t * LANES, LANES), LANES)

    reads[0].wait()

    def pack_axial(t, carry):
        for i in range(PTS // 4):
            x = [ext[2, REACH + 4 * i + j, :, cols(t)] for j in range(4)]
            for j, y in enumerate(pack4(x, sub)):
                esend[3 * i + j, :, cols(t)] = y
        return carry

    lax.fori_loop(0, TILES, pack_axial, 0)
    quarter = lane((8, LANES)) // RT
    for c in range(3):
        for i in range(PTS // 4):
            line = ext[c, REACH + 4 * i, :, :LANES]
            for j in range(1, 4):
                line = jnp.where(quarter == j, pltpu.roll(ext[c, REACH + 4 * i + j, :, :LANES], RT * j, 1), line)
            msend[c, i] = MIRROR_SIGNS[c] * line

    pl.semaphore_wait(barrier, len(greeted) - 2 + GROUP * at_edge)

    def remote(src, dst, s_sem, r_sem, who):
        return pltpu.make_async_remote_copy(
            src_ref=src, dst_ref=dst, send_sem=s_sem, recv_sem=r_sem, device_id=who, device_id_type=MESH
        )

    def pair(src, dst, sem, who):
        return remote(src, dst, sem.at[0], sem.at[1], who)

    planes_e = pair(esend, erecv, e_sem, (p, 1 - g))
    halo_up, halo_down = [], []
    for c in range(3):
        halo_up.append(
            remote(ext.at[c, pl.ds(PTS, REACH)], ext.at[c, pl.ds(0, REACH)], up_sem.at[0, c], up_sem.at[1, c], (after, g))
        )
        halo_down.append(
            remote(
                ext.at[c, pl.ds(REACH, REACH)], ext.at[c, pl.ds(REACH + PTS, REACH)],
                down_sem.at[0, c], down_sem.at[1, c], (before, g),
            )
        )
    mirror = pair(msend, mrecv, mir_sem, (across, g))
    sums = []
    for k in range(GROUP):
        other = (me + k) % GROUP
        sums.append(
            remote(ssend.at[other], sum_in.at[me], v_s.at[k], v_r.at[k], (block * GROUP + other, 1 - g))
        )
    planes = [
        remote(gsend.at[c], grecv.at[c], g_sem.at[0, c], g_sem.at[1, c], (p, 1 - g)) for c in range(2)
    ]
    first, final = me == 0, me == GROUP - 1
    planes_e.start()
    halo_up[1].start()
    halo_down[1].start()
    mirror.start()

    @pl.when(me != GROUP - 1)
    def _():
        halo_up[0].start()
        halo_up[2].start()

    @pl.when(me != 0)
    def _():
        halo_down[0].start()
        halo_down[2].start()

    radius = lane((8, NR)).astype(F32) + 0.5
    inverse_r = 1.0 / radius
    coef = visc[0] * inverse_r * inverse_r
    half = 0.5 / coef
    gap = jnp.sqrt(half * (2.0 + half)) - half
    rho = 1.0 - gap
    scale = 1.0 / jnp.sqrt(1.0 + 4.0 * coef)
    gap16 = doubled(doubled(doubled(doubled(gap))))
    gap128 = doubled(doubled(doubled(gap16)))
    whole = doubled(doubled(doubled(doubled(gap128))))
    for t in range(TILES):
        here = slice(t * LANES, (t + 1) * LANES)
        inv_t[t] = inverse_r[:, here]
        scale_t[t] = scale[:, here]
        w_t[t] = 1.0 - gap16[:, here]
        big_t[t] = 1.0 - gap128[:, here]
        inv_n[t] = 1.0 / whole[:, here]
        power = jnp.ones((8, LANES), F32)
        for j in range(PTS + 1):
            pow_t[t, j] = power
            power = power * rho[:, here]

    def spread(t, carry):
        for c in range(3):
            for i in range(PTS // 4):
                far = []
                for j in range(4):
                    row = 4 * i + j
                    inside, outside = axial_parts(ext[c, REACH + row, :, cols(t)], sub)
                    own_ax[c, row, :, cols(t)] = inside
                    far_ax[c, row, :, cols(t)] = outside
                    far.append(outside)
                if c < 2:
                    for j, y in enumerate(pack4(far, sub)):
                        gsend[c, 3 * i + j, :, cols(t)] = y
        return carry

    lax.fori_loop(0, TILES, spread, 0)

    reads[1].wait()
    op_high, op_low = split(op_v[...])
    wh[...] = op_high
    wl[...] = op_low
    for c in range(3):
        lines = ext[c, pl.ds(REACH, PTS)].reshape(PTS * 8, NR)
        part[c] = dot3(lines, wh[pl.ds(0, NR)], wl[pl.ds(0, NR)]).reshape(PTS, 8, NR)

    def azimuth(t, carry):
        inv = inv_t[t]
        for c in range(3):
            x = [ext[c, REACH + k, :, cols(t)] for k in range(PTS)]
            for row in range(PTS):
                grad = None
                for k in range(max(0, row - REACH), min(PTS, row + REACH + 1)):
                    tap = sten[k - row + REACH] * x[k]
                    grad = tap if grad is None else grad + tap
                a = ext[0, REACH + row, :, cols(t)]
                b = ext[1, REACH + row, :, cols(t)]
                e = ext[2, REACH + row, :, cols(t)]
                if c == 0:
                    grad = grad - b
                if c == 1:
                    grad = grad + a
                part[c, row, :, cols(t)] = (
                    a * part[c, row, :, cols(t)] + (b * inv) * grad + e * own_ax[c, row, :, cols(t)]
                )
        return carry

    lax.fori_loop(0, TILES, azimuth, 0)

    planes_e.wait_recv()

    def partner_sums(t, carry):
        rho = pow_t[t, 1]
        e = []
        for i in range(PTS // 4):
            e += unpack4([erecv[3 * i + j, :, cols(t)] for j in range(3)], sub)
        for c in range(3):
            ahead = back = None
            for row in range(PTS):
                x = e[row] * far_ax[c, row, :, cols(t)]
                ahead = x if row == 0 else rho * ahead + x
                back = x if row == 0 else back + pow_t[t, row] * x
            ssend[t, c] = -STEP_WEIGHT * ahead
            ssend[TILES + t, c] = -STEP_WEIGHT * back
        return carry

    lax.fori_loop(0, TILES, partner_sums, 0)
    for cp in sums:
        cp.start()

    def halo_taps(t, c, row, shift):
        span = range(row, REACH) if shift[0] == 0 else range(REACH + PTS, row + 2 * REACH + 1)
        grad = None
        for k in span:
            tap = sten[k - row] * ext[c, k + shift[1], :, cols(t)]
            grad = tap if grad is None else grad + tap
        return grad

    def edge_sums(side):
        shift = (side, PTS if side == 0 else -PTS)
        theirs = REACH + PTS if side == 0 else REACH - PTS

        def body(t, carry):
            inv, rho = inv_t[t], pow_t[t, 1]
            for c in range(3):
                ahead = back = None
                for row in ROWS[side]:
                    x = (ext[1, row + theirs, :, cols(t)] * inv) * halo_taps(t, c, row, shift)
                    ahead = x if ahead is None else rho * ahead + x
                    x = pow_t[t, row] * x
                    back = x if back is None else back + x
                if side == 0:
                    ahead = ahead * pow_t[t, PTS - REACH]
                hsend[t, c] = -STEP_WEIGHT * ahead
                hsend[TILES + t, c] = -STEP_WEIGHT * back
            return carry

        lax.fori_loop(0, TILES, body, 0)

    def edge_copies(side):
        to = (block + 1) % BLOCKS if side == 0 else (block + BLOCKS - 1) % BLOCKS
        return [
            remote(hsend.at[k], halo_in.at[side], h_s.at[k], h_r.at[side], (to * GROUP + k, g)) for k in range(GROUP)
        ]

    edge = [edge_copies(0), edge_copies(1)]

    @pl.when(final)
    def _():
        halo_down[1].wait_recv()
        edge_sums(0)
        for cp in edge[0]:
            cp.start()

    @pl.when(first)
    def _():
        halo_up[1].wait_recv()
        edge_sums(1)
        for cp in edge[1]:
            cp.start()

    for cp in planes:
        cp.start()

    @pl.when(final)
    def _():
        halo_up[0].start()
        halo_up[2].start()

    @pl.when(first)
    def _():
        halo_down[0].start()
        halo_down[2].start()

    mirror.wait_recv()

    def across_axis(i, carry):
        lines = []
        for c in range(3):
            packed = mrecv[c, i]
            lines += [packed[:, :RT]] + [pltpu.roll(packed, LANES - RT * j, 1)[:, :RT] for j in range(1, 4)]
        more = dot3(jnp.concatenate(lines, axis=0), wh[pl.ds(NR, RT)], wl[pl.ds(NR, RT)]).reshape(3, 4, 8, NR)
        rows = pl.ds(4 * i, 4)
        for c in range(3):
            part[c, rows] = part[c, rows] + ext[0, pl.ds(REACH + 4 * i, 4)] * more[c]
        return carry

    lax.fori_loop(0, PTS // 4, across_axis, 0)

    def local_sums(t, carry):
        rho = pow_t[t, 1]
        for c in range(3):
            ahead = back = None
            for row in range(PTS):
                right = ext[c, REACH + row, :, cols(t)] - STEP_WEIGHT * part[c, row, :, cols(t)]
                ahead = right if row == 0 else rho * ahead + right
                back = right if row == 0 else back + pow_t[t, row] * right
            fb[t, c] = ahead
            fb[TILES + t, c] = back
        return carry

    lax.fori_loop(0, TILES, local_sums, 0)

    def add_halo(side, summed):
        def body(t, carry):
            inv, rho = inv_t[t], pow_t[t, 1]
            for c in range(3):
                ahead = back = None
                for row in ROWS[side]:
                    x = (ext[1, REACH + row, :, cols(t)] * inv) * halo_taps(t, c, row, (side, 0))
                    part[c, row, :, cols(t)] = part[c, row, :, cols(t)] + x
                    if summed:
                        ahead = x if ahead is None else rho * ahead + x
                        x = pow_t[t, row] * x
                        back = x if back is None else back + x
                if summed:
                    if side == 0:
                        ahead = ahead * pow_t[t, PTS - REACH]
                    fb[t, c] = fb[t, c] - STEP_WEIGHT * ahead
                    fb[TILES + t, c] = fb[TILES + t, c] - STEP_WEIGHT * back
            return carry

        lax.fori_loop(0, TILES, body, 0)

    @pl.when(me != 0)
    def _():
        for cp in (halo_up[1], halo_up[0], halo_up[2]):
            cp.wait_recv()
        add_halo(0, True)

    @pl.when(me != GROUP - 1)
    def _():
        for cp in (halo_down[1], halo_down[0], halo_down[2]):
            cp.wait_recv()
        add_halo(1, True)

    one, two, three = [], [], []
    for k in range(1, GROUP):
        other = (me + k) % GROUP
        cp = remote(fb.at[other], up_in.at[me], p1_s.at[k - 1], p1_r.at[k - 1], (block * GROUP + other, g))
        cp.start()
        one.append(cp)
    up_in[me] = fb[me]

    def finish_term(c):
        def body(t, carry):
            rho = pow_t[t, 1]
            right = []
            left = []
            for i in range(PTS // 4):
                if c < 2:
                    far = unpack4([grecv[c, 3 * i + j, :, cols(t)] for j in range(3)], sub)
                else:
                    far = unpack4([erecv[3 * i + j, :, cols(t)] for j in range(3)], sub)
                for j in range(4):
                    row = 4 * i + j
                    grad = far[j]
                    if c == 2:
                        grad = axial_parts(grad, sub)[1]
                    else:
                        grad = jnp.where((sub == 3) | (sub == 4), 0.0, grad)
                    term = part[c, row, :, cols(t)] + ext[2, REACH + row, :, cols(t)] * grad
                    part[c, row, :, cols(t)] = term
                    right.append(ext[c, REACH + row, :, cols(t)] - STEP_WEIGHT * term)
                    left.append(right[row] if row == 0 else right[row] + rho * left[row - 1])
            run = None
            for row in range(PTS - 1, -1, -1):
                if run is None:
                    loc[c, row, :, cols(t)] = left[row]
                    run = right[row]
                else:
                    run = rho * run
                    loc[c, row, :, cols(t)] = left[row] + run
                    run = right[row] + run
            return carry

        lax.fori_loop(0, TILES, body, 0)

    def write(src, dst, k):
        cp = pltpu.make_async_copy(src, dst, out_sem.at[k])
        cp.start()
        return cp

    def entry(k):
        return k + backward * (GROUP - 1 - 2 * k)

    for cp in (*one, *sums, edge[0][0], edge[1][0]):
        cp.wait_recv()
    for k in range(GROUP):
        total = up_in[k] + sum_in[k]
        if k == 0:
            total = total + halo_in[0]
        if k == GROUP - 1:
            total = total + halo_in[1]
        up_in[k] = total
    w = w_t[my_tile]
    run = up_in[entry(0)]
    for k in range(1, GROUP):
        run = up_in[entry(k)] + w * run
    tot[block] = run
    for k in range(1, BLOCKS):
        cp = remote(
            tot.at[block], tot.at[block], p2_s.at[k - 1], p2_r.at[k - 1],
            (((block + k) % BLOCKS) * GROUP + me, g),
        )
        cp.start()
        two.append(cp)

    @pl.when(first)
    def _():
        halo_up[0].wait_recv()
        halo_up[2].wait_recv()
        add_halo(0, False)

    @pl.when(final)
    def _():
        halo_down[0].wait_recv()
        halo_down[2].wait_recv()
        add_halo(1, False)

    finish_term(2)
    writes = [write(part.at[2], non_hbm.at[2], 0)]

    for cp in two:
        cp.wait_recv()
    big = big_t[my_tile]
    run = tot[block]
    for m in range(BLOCKS - 1, 0, -1):
        run = tot[(block + (2 * backward - 1) * m + BLOCKS) % BLOCKS] + big * run
    run = run * inv_n[my_tile]
    for k in range(GROUP):
        ret[entry(k)] = run
        run = up_in[entry(k)] + w * run
    for k in range(1, GROUP):
        other = (me + k) % GROUP
        cp = remote(ret.at[other], car.at[me], p3_s.at[k - 1], p3_r.at[k - 1], (block * GROUP + other, g))
        cp.start()
        three.append(cp)
    car[me] = ret[me]

    for c in range(2):
        planes[c].wait_recv()
        finish_term(c)
        writes.append(write(part.at[c], non_hbm.at[c], 1 + c))

    for cp in three:
        cp.wait_recv()

    def last(t, carry):
        scale = scale_t[t]
        for c in range(3):
            from_left = scale * car[t, c]
            from_right = scale * car[TILES + t, c]
            for row in range(PTS):
                loc[c, row, :, cols(t)] = (
                    scale * loc[c, row, :, cols(t)]
                    + pow_t[t, row + 1] * from_left
                    + pow_t[t, PTS - row] * from_right
                )
        return carry

    lax.fori_loop(0, TILES, last, 0)
    writes.append(write(loc, new_hbm, 3))
    for cp in (planes_e, *halo_up, *halo_down, mirror, *sums, *planes, *one, *two, *three):
        cp.wait_send()

    for side, here in ((0, final), (1, first)):

        @pl.when(here)
        def _(side=side):
            for cp in edge[side]:
                cp.wait_send()

    for cp in writes:
        cp.wait()


def local(velocity, radial_op, azimuth_stencil, viscous_factor):
    dma = pltpu.SemaphoreType.DMA
    block = velocity.shape
    any_space = pl.BlockSpec(memory_space=pl.ANY)
    scalars = pl.BlockSpec(memory_space=pltpu.SMEM)
    tile = (8, LANES)
    return pl.pallas_call(
        kernel,
        name="substep",
        out_shape=(jax.ShapeDtypeStruct(block, F32), jax.ShapeDtypeStruct(block, F32)),
        in_specs=[any_space, any_space, scalars, scalars],
        out_specs=(any_space, any_space),
        scratch_shapes=[
            pltpu.VMEM((3, PTS + 2 * REACH, 8, NR), F32),
            pltpu.VMEM((NR + RT, NR), F32),
            pltpu.VMEM((NR + RT, NR), BF16),
            pltpu.VMEM((NR + RT, NR), BF16),
            pltpu.VMEM((12, 8, NR), F32),
            pltpu.VMEM((12, 8, NR), F32),
            pltpu.VMEM((2, 12, 8, NR), F32),
            pltpu.VMEM((2, 12, 8, NR), F32),
            pltpu.VMEM((3, 4, *tile), F32),
            pltpu.VMEM((3, 4, *tile), F32),
            pltpu.VMEM(block, F32),
            pltpu.VMEM(block, F32),
            pltpu.VMEM(block, F32),
            pltpu.VMEM(block, F32),
            pltpu.VMEM((TILES, *tile), F32),
            pltpu.VMEM((TILES, PTS + 1, *tile), F32),
            pltpu.VMEM((TILES, *tile), F32),
            pltpu.VMEM((TILES, *tile), F32),
            pltpu.VMEM((TILES, *tile), F32),
            pltpu.VMEM((TILES, *tile), F32),
            pltpu.VMEM((GROUP, 3, *tile), F32),
            pltpu.VMEM((GROUP, 3, *tile), F32),
            pltpu.VMEM((GROUP, 3, *tile), F32),
            pltpu.VMEM((2, 3, *tile), F32),
            pltpu.VMEM((GROUP, 3, *tile), F32),
            pltpu.VMEM((GROUP, 3, *tile), F32),
            pltpu.VMEM((GROUP, 3, *tile), F32),
            pltpu.VMEM((BLOCKS, 3, *tile), F32),
            pltpu.VMEM((GROUP, 3, *tile), F32),
            dma((2,)),
            dma((2,)), dma((2,)), dma((2, 3)), dma((2, 3)),
            dma((2, 2)), dma((GROUP,)), dma((GROUP,)), dma((GROUP,)), dma((2,)),
            dma((GROUP - 1,)), dma((GROUP - 1,)),
            dma((BLOCKS - 1,)), dma((BLOCKS - 1,)),
            dma((GROUP - 1,)), dma((GROUP - 1,)),
            dma((4,)),
        ],
        compiler_params=pltpu.CompilerParams(
            collective_id=0, has_side_effects=True, vmem_limit_bytes=52 << 20
        ),
    )(velocity, radial_op.T, azimuth_stencil, viscous_factor)


def solution(mesh):
    spec = P(None, "theta", "gz", None)
    return jax.shard_map(
        local, mesh=mesh, in_specs=(spec, P(), P(), P()), out_specs=(spec, spec), check_vma=False
    )
```

```python
import jax
import jax.numpy as jnp
from jax import lax
from jax.experimental import pallas as pl
from jax.experimental.pallas import tpu as pltpu
from jax.sharding import PartitionSpec as P

AXIAL_WEIGHTS = (0.75, -0.15, 1.0 / 60.0)
STEP_WEIGHT = 0.2
MIRROR_SIGNS = (-1.0, -1.0, 1.0)
MESH = pl.DeviceIdType.MESH
F32 = jnp.float32
BF16 = jnp.bfloat16
REACH = 10
PTS = 16
NR = 512
RT = 32
LANES = 128
TILES = NR // LANES
GROUP = 8
SECTORS = 128
BLOCKS = SECTORS // GROUP
ROWS = (range(0, REACH), range(PTS - REACH, PTS))
PLAIN_DOT = (((1,), (0,)), ((), ()))


def split(x):
    high = x.astype(BF16)
    return high, (x - high.astype(F32)).astype(BF16)


def dot3(x, w_high, w_low):
    high, low = split(x)
    out = lax.dot_general(high, w_low, PLAIN_DOT, preferred_element_type=F32)
    out = out + lax.dot_general(low, w_high, PLAIN_DOT, preferred_element_type=F32)
    return out + lax.dot_general(high, w_high, PLAIN_DOT, preferred_element_type=F32)


def rows_of(shape):
    return lax.broadcasted_iota(jnp.int32, shape, len(shape) - 2)


def lane(shape):
    return lax.broadcasted_iota(jnp.int32, shape, len(shape) - 1)


def doubled(q):
    return q * (2.0 - q)


def pack4(x, sub):
    middle = (sub == 3) | (sub == 4)
    return (
        jnp.where(middle, pltpu.roll(x[3], 3, 0), x[0]),
        jnp.where(sub == 3, pltpu.roll(x[3], 1, 0), jnp.where(sub == 4, pltpu.roll(x[3], 7, 0), x[1])),
        jnp.where(middle, pltpu.roll(x[3], 5, 0), x[2]),
    )


def unpack4(y, sub):
    fourth = jnp.where(
        sub < 2,
        pltpu.roll(y[0], 5, 0),
        jnp.where(
            sub == 2,
            pltpu.roll(y[1], 7, 0),
            jnp.where(sub == 5, pltpu.roll(y[1], 1, 0), pltpu.roll(y[2], 3, 0)),
        ),
    )
    return (y[0], y[1], y[2], fourth)


def axial_parts(x, sub):
    own = far = None
    for m, weight in enumerate(AXIAL_WEIGHTS, 1):
        upper = weight * pltpu.roll(x, 8 - m, 0)
        lower = weight * pltpu.roll(x, m, 0)
        inside = jnp.where(sub < 8 - m, upper, 0.0) - jnp.where(sub >= m, lower, 0.0)
        outside = jnp.where(sub < 8 - m, 0.0, upper) - jnp.where(sub >= m, 0.0, lower)
        own = inside if own is None else own + inside
        far = outside if far is None else far + outside
    return own, far


def kernel(
    v_hbm, op_hbm, sten_hbm, visc, new_hbm, non_hbm,
    sten,
    ext, op_v, wh, wl, esend, erecv, gsend, grecv, msend, mrecv, part, own_ax, far_ax, loc,
    inv_t, pow_t, scale_t, w_t, big_t, inv_n, ssend, sum_in, hsend, halo_in, fb, up_in, ret, tot, car,
    in_sem, e_sem, mir_sem, up_sem, down_sem, g_sem, v_s, v_r, h_s, h_r,
    p1_s, p1_r, p2_s, p2_r, p3_s, p3_r, out_sem, chain,
):
    p = lax.axis_index("theta")
    g = lax.axis_index("gz")
    me = p % GROUP
    block = p // GROUP
    backward = me // TILES
    my_tile = me % TILES
    sub = rows_of((8, LANES))

    reads = [
        pltpu.make_async_copy(v_hbm, ext.at[:, pl.ds(REACH, PTS)], in_sem.at[0]),
        pltpu.make_async_copy(op_hbm, op_v, in_sem.at[1]),
        pltpu.make_async_copy(sten_hbm, sten, in_sem.at[2]),
    ]
    for r in reads:
        r.start()

    after = (p + 1) % SECTORS
    before = (p + SECTORS - 1) % SECTORS
    across = (p + SECTORS // 2) % SECTORS
    barrier = pltpu.get_barrier_semaphore()
    greeted = [(after, g), (before, g)]
    greeted += [(block * GROUP + (me + k) % GROUP, g) for k in range(1, GROUP)]
    greeted += [(p, 1 - g)]
    hop = [((p + d) % SECTORS, g) for d in (2 * GROUP, SECTORS - 2 * GROUP, 4 * GROUP, SECTORS - 4 * GROUP)]
    side_block = (block + 1 - 2 * (block % 2)) * GROUP + me
    greeted += [*hop[:2], (side_block, g)]
    for who in greeted:
        pl.semaphore_signal(barrier, inc=1, device_id=who, device_id_type=MESH)

    def cols(t):
        return pl.ds(pl.multiple_of(t * LANES, LANES), LANES)

    reads[0].wait()

    def pack_axial(t, carry):
        for i in range(PTS // 4):
            x = [ext[2, REACH + 4 * i + j, :, cols(t)] for j in range(4)]
            for j, y in enumerate(pack4(x, sub)):
                esend[3 * i + j, :, cols(t)] = y
        return carry

    lax.fori_loop(0, TILES, pack_axial, 0)
    quarter = lane((8, LANES)) // RT
    for c in range(3):
        for i in range(PTS // 4):
            line = ext[c, REACH + 4 * i, :, :LANES]
            for j in range(1, 4):
                line = jnp.where(quarter == j, pltpu.roll(ext[c, REACH + 4 * i + j, :, :LANES], RT * j, 1), line)
            msend[c, i] = MIRROR_SIGNS[c] * line

    pl.semaphore_wait(barrier, len(greeted))

    def tell(stage, whom):
        for who in whom:
            pl.semaphore_signal(chain.at[stage], inc=1, device_id=who, device_id_type=MESH)

    tell(0, hop[:2])

    def remote(src, dst, s_sem, r_sem, who):
        return pltpu.make_async_remote_copy(
            src_ref=src, dst_ref=dst, send_sem=s_sem, recv_sem=r_sem, device_id=who, device_id_type=MESH
        )

    def pair(src, dst, sem, who):
        return remote(src, dst, sem.at[0], sem.at[1], who)

    planes_e = pair(esend, erecv, e_sem, (p, 1 - g))
    halo_up, halo_down = [], []
    for c in range(3):
        halo_up.append(
            remote(ext.at[c, pl.ds(PTS, REACH)], ext.at[c, pl.ds(0, REACH)], up_sem.at[0, c], up_sem.at[1, c], (after, g))
        )
        halo_down.append(
            remote(
                ext.at[c, pl.ds(REACH, REACH)], ext.at[c, pl.ds(REACH + PTS, REACH)],
                down_sem.at[0, c], down_sem.at[1, c], (before, g),
            )
        )
    mirror = pair(msend, mrecv, mir_sem, (across, g))
    sums = []
    for k in range(GROUP):
        other = (me + k) % GROUP
        sums.append(
            remote(ssend.at[other], sum_in.at[me], v_s.at[k], v_r.at[k], (block * GROUP + other, 1 - g))
        )
    planes = [
        remote(gsend.at[c], grecv.at[c], g_sem.at[0, c], g_sem.at[1, c], (p, 1 - g)) for c in range(2)
    ]
    first, final = me == 0, me == GROUP - 1
    planes_e.start()
    halo_up[1].start()
    halo_down[1].start()

    @pl.when(me != GROUP - 1)
    def _():
        halo_up[0].start()
        halo_up[2].start()

    @pl.when(me != 0)
    def _():
        halo_down[0].start()
        halo_down[2].start()

    reads[2].wait()
    radius = lane((8, NR)).astype(F32) + 0.5
    inverse_r = 1.0 / radius
    coef = visc[0] * inverse_r * inverse_r
    half = 0.5 / coef
    gap = jnp.sqrt(half * (2.0 + half)) - half
    rho = 1.0 - gap
    scale = 1.0 / jnp.sqrt(1.0 + 4.0 * coef)
    gap16 = doubled(doubled(doubled(doubled(gap))))
    gap128 = doubled(doubled(doubled(gap16)))
    whole = doubled(doubled(doubled(doubled(gap128))))
    for t in range(TILES):
        here = slice(t * LANES, (t + 1) * LANES)
        inv_t[t] = inverse_r[:, here]
        scale_t[t] = scale[:, here]
        w_t[t] = 1.0 - gap16[:, here]
        big_t[t] = 1.0 - gap128[:, here]
        inv_n[t] = 1.0 / whole[:, here]
        power = jnp.ones((8, LANES), F32)
        for j in range(PTS + 1):
            pow_t[t, j] = power
            power = power * rho[:, here]

    def spread(t, carry):
        for c in range(3):
            for i in range(PTS // 4):
                far = []
                for j in range(4):
                    row = 4 * i + j
                    inside, outside = axial_parts(ext[c, REACH + row, :, cols(t)], sub)
                    own_ax[c, row, :, cols(t)] = inside
                    far_ax[c, row, :, cols(t)] = outside
                    far.append(outside)
                if c < 2:
                    for j, y in enumerate(pack4(far, sub)):
                        gsend[c, 3 * i + j, :, cols(t)] = y
        return carry

    lax.fori_loop(0, TILES, spread, 0)

    pl.semaphore_wait(chain.at[0], 2)
    tell(1, hop[2:])

    reads[1].wait()
    op_high, op_low = split(op_v[...])
    wh[...] = op_high
    wl[...] = op_low
    for c in range(3):
        lines = ext[c, pl.ds(REACH, PTS)].reshape(PTS * 8, NR)
        part[c] = dot3(lines, wh[pl.ds(0, NR)], wl[pl.ds(0, NR)]).reshape(PTS, 8, NR)

    pl.semaphore_wait(chain.at[1], 2)
    mirror.start()
    tell(2, [(side_block, g)])

    def azimuth(t, carry):
        inv = inv_t[t]
        for c in range(3):
            x = [ext[c, REACH + k, :, cols(t)] for k in range(PTS)]
            for row in range(PTS):
                grad = None
                for k in range(max(0, row - REACH), min(PTS, row + REACH + 1)):
                    tap = sten[k - row + REACH] * x[k]
                    grad = tap if grad is None else grad + tap
                a = ext[0, REACH + row, :, cols(t)]
                b = ext[1, REACH + row, :, cols(t)]
                e = ext[2, REACH + row, :, cols(t)]
                if c == 0:
                    grad = grad - b
                if c == 1:
                    grad = grad + a
                part[c, row, :, cols(t)] = (
                    a * part[c, row, :, cols(t)] + (b * inv) * grad + e * own_ax[c, row, :, cols(t)]
                )
        return carry

    lax.fori_loop(0, TILES, azimuth, 0)

    planes_e.wait_recv()

    def partner_sums(t, carry):
        rho = pow_t[t, 1]
        e = []
        for i in range(PTS // 4):
            e += unpack4([erecv[3 * i + j, :, cols(t)] for j in range(3)], sub)
        for c in range(3):
            ahead = back = None
            for row in range(PTS):
                x = e[row] * far_ax[c, row, :, cols(t)]
                ahead = x if row == 0 else rho * ahead + x
                back = x if row == 0 else back + pow_t[t, row] * x
            ssend[t, c] = -STEP_WEIGHT * ahead
            ssend[TILES + t, c] = -STEP_WEIGHT * back
        return carry

    lax.fori_loop(0, TILES, partner_sums, 0)
    for cp in sums:
        cp.start()

    def halo_taps(t, c, row, shift):
        span = range(row, REACH) if shift[0] == 0 else range(REACH + PTS, row + 2 * REACH + 1)
        grad = None
        for k in span:
            tap = sten[k - row] * ext[c, k + shift[1], :, cols(t)]
            grad = tap if grad is None else grad + tap
        return grad

    def edge_sums(side):
        shift = (side, PTS if side == 0 else -PTS)
        theirs = REACH + PTS if side == 0 else REACH - PTS

        def body(t, carry):
            inv, rho = inv_t[t], pow_t[t, 1]
            for c in range(3):
                ahead = back = None
                for row in ROWS[side]:
                    x = (ext[1, row + theirs, :, cols(t)] * inv) * halo_taps(t, c, row, shift)
                    ahead = x if ahead is None else rho * ahead + x
                    x = pow_t[t, row] * x
                    back = x if back is None else back + x
                if side == 0:
                    ahead = ahead * pow_t[t, PTS - REACH]
                hsend[t, c] = -STEP_WEIGHT * ahead
                hsend[TILES + t, c] = -STEP_WEIGHT * back
            return carry

        lax.fori_loop(0, TILES, body, 0)

    def edge_copies(side):
        to = (block + 1) % BLOCKS if side == 0 else (block + BLOCKS - 1) % BLOCKS
        return [
            remote(hsend.at[k], halo_in.at[side], h_s.at[k], h_r.at[side], (to * GROUP + k, g)) for k in range(GROUP)
        ]

    edge = [edge_copies(0), edge_copies(1)]

    @pl.when(final)
    def _():
        halo_down[1].wait_recv()
        edge_sums(0)
        for cp in edge[0]:
            cp.start()

    @pl.when(first)
    def _():
        halo_up[1].wait_recv()
        edge_sums(1)
        for cp in edge[1]:
            cp.start()

    for cp in planes:
        cp.start()

    @pl.when(final)
    def _():
        halo_up[0].start()
        halo_up[2].start()

    @pl.when(first)
    def _():
        halo_down[0].start()
        halo_down[2].start()

    mirror.wait_recv()

    def across_axis(i, carry):
        lines = []
        for c in range(3):
            packed = mrecv[c, i]
            lines += [packed[:, :RT]] + [pltpu.roll(packed, LANES - RT * j, 1)[:, :RT] for j in range(1, 4)]
        more = dot3(jnp.concatenate(lines, axis=0), wh[pl.ds(NR, RT)], wl[pl.ds(NR, RT)]).reshape(3, 4, 8, NR)
        rows = pl.ds(4 * i, 4)
        for c in range(3):
            part[c, rows] = part[c, rows] + ext[0, pl.ds(REACH + 4 * i, 4)] * more[c]
        return carry

    lax.fori_loop(0, PTS // 4, across_axis, 0)

    def local_sums(t, carry):
        rho = pow_t[t, 1]
        for c in range(3):
            ahead = back = None
            for row in range(PTS):
                right = ext[c, REACH + row, :, cols(t)] - STEP_WEIGHT * part[c, row, :, cols(t)]
                ahead = right if row == 0 else rho * ahead + right
                back = right if row == 0 else back + pow_t[t, row] * right
            fb[t, c] = ahead
            fb[TILES + t, c] = back
        return carry

    lax.fori_loop(0, TILES, local_sums, 0)

    def add_halo(side, summed):
        def body(t, carry):
            inv, rho = inv_t[t], pow_t[t, 1]
            for c in range(3):
                ahead = back = None
                for row in ROWS[side]:
                    x = (ext[1, REACH + row, :, cols(t)] * inv) * halo_taps(t, c, row, (side, 0))
                    part[c, row, :, cols(t)] = part[c, row, :, cols(t)] + x
                    if summed:
                        ahead = x if ahead is None else rho * ahead + x
                        x = pow_t[t, row] * x
                        back = x if back is None else back + x
                if summed:
                    if side == 0:
                        ahead = ahead * pow_t[t, PTS - REACH]
                    fb[t, c] = fb[t, c] - STEP_WEIGHT * ahead
                    fb[TILES + t, c] = fb[TILES + t, c] - STEP_WEIGHT * back
            return carry

        lax.fori_loop(0, TILES, body, 0)

    @pl.when(me != 0)
    def _():
        for cp in (halo_up[1], halo_up[0], halo_up[2]):
            cp.wait_recv()
        add_halo(0, True)

    @pl.when(me != GROUP - 1)
    def _():
        for cp in (halo_down[1], halo_down[0], halo_down[2]):
            cp.wait_recv()
        add_halo(1, True)

    one, two, three = [], [], []
    for k in sorted(range(1, GROUP), key=lambda k: abs(k - GROUP // 2)):
        other = (me + k) % GROUP
        cp = remote(fb.at[other], up_in.at[me], p1_s.at[k - 1], p1_r.at[k - 1], (block * GROUP + other, g))
        cp.start()
        one.append(cp)
    up_in[me] = fb[me]

    def finish_term(c):
        def body(t, carry):
            rho = pow_t[t, 1]
            right = []
            left = []
            for i in range(PTS // 4):
                if c < 2:
                    far = unpack4([grecv[c, 3 * i + j, :, cols(t)] for j in range(3)], sub)
                else:
                    far = unpack4([erecv[3 * i + j, :, cols(t)] for j in range(3)], sub)
                for j in range(4):
                    row = 4 * i + j
                    grad = far[j]
                    if c == 2:
                        grad = axial_parts(grad, sub)[1]
                    else:
                        grad = jnp.where((sub == 3) | (sub == 4), 0.0, grad)
                    term = part[c, row, :, cols(t)] + ext[2, REACH + row, :, cols(t)] * grad
                    part[c, row, :, cols(t)] = term
                    right.append(ext[c, REACH + row, :, cols(t)] - STEP_WEIGHT * term)
                    left.append(right[row] if row == 0 else right[row] + rho * left[row - 1])
            run = None
            for row in range(PTS - 1, -1, -1):
                if run is None:
                    loc[c, row, :, cols(t)] = left[row]
                    run = right[row]
                else:
                    run = rho * run
                    loc[c, row, :, cols(t)] = left[row] + run
                    run = right[row] + run
            return carry

        lax.fori_loop(0, TILES, body, 0)

    def write(src, dst, k):
        cp = pltpu.make_async_copy(src, dst, out_sem.at[k])
        cp.start()
        return cp

    def entry(k):
        return k + backward * (GROUP - 1 - 2 * k)

    pl.semaphore_wait(chain.at[2], 1)
    for cp in (*one, *sums, edge[0][0], edge[1][0]):
        cp.wait_recv()
    for k in range(GROUP):
        total = up_in[k] + sum_in[k]
        if k == 0:
            total = total + halo_in[0]
        if k == GROUP - 1:
            total = total + halo_in[1]
        up_in[k] = total
    w = w_t[my_tile]
    run = up_in[entry(0)]
    for k in range(1, GROUP):
        run = up_in[entry(k)] + w * run
    tot[block] = run
    for k in sorted(range(1, BLOCKS), key=lambda k: abs(k - BLOCKS // 2)):
        cp = remote(
            tot.at[block], tot.at[block], p2_s.at[k - 1], p2_r.at[k - 1],
            (((block + k) % BLOCKS) * GROUP + me, g),
        )
        cp.start()
        two.append(cp)

    @pl.when(first)
    def _():
        halo_up[0].wait_recv()
        halo_up[2].wait_recv()
        add_halo(0, False)

    @pl.when(final)
    def _():
        halo_down[0].wait_recv()
        halo_down[2].wait_recv()
        add_halo(1, False)

    finish_term(2)
    writes = [write(part.at[2], non_hbm.at[2], 0)]

    for cp in two:
        cp.wait_recv()
    big = big_t[my_tile]
    run = tot[block]
    for m in range(BLOCKS - 1, 0, -1):
        run = tot[(block + (2 * backward - 1) * m + BLOCKS) % BLOCKS] + big * run
    run = run * inv_n[my_tile]
    for k in range(GROUP):
        ret[entry(k)] = run
        run = up_in[entry(k)] + w * run
    for k in sorted(range(1, GROUP), key=lambda k: abs(k - GROUP // 2)):
        other = (me + k) % GROUP
        cp = remote(ret.at[other], car.at[me], p3_s.at[k - 1], p3_r.at[k - 1], (block * GROUP + other, g))
        cp.start()
        three.append(cp)
    car[me] = ret[me]

    for c in range(2):
        planes[c].wait_recv()
        finish_term(c)
        writes.append(write(part.at[c], non_hbm.at[c], 1 + c))

    for cp in three:
        cp.wait_recv()

    def last(t, carry):
        scale = scale_t[t]
        for c in range(3):
            from_left = scale * car[t, c]
            from_right = scale * car[TILES + t, c]
            for row in range(PTS):
                loc[c, row, :, cols(t)] = (
                    scale * loc[c, row, :, cols(t)]
                    + pow_t[t, row + 1] * from_left
                    + pow_t[t, PTS - row] * from_right
                )
        return carry

    lax.fori_loop(0, TILES, last, 0)
    writes.append(write(loc, new_hbm, 3))
    for cp in (planes_e, *halo_up, *halo_down, mirror, *sums, *planes, *one, *two, *three):
        cp.wait_send()

    for side, here in ((0, final), (1, first)):

        @pl.when(here)
        def _(side=side):
            for cp in edge[side]:
                cp.wait_send()

    for cp in writes:
        cp.wait()


def write_out(new_in, non_in, new_out, non_out, sem):
    copies = []
    for k, (src, dst) in enumerate(((new_in, new_out), (non_in, non_out))):
        for c in range(3):
            copies.append(pltpu.make_async_copy(src.at[c], dst.at[c], sem.at[k, c]))
    for cp in copies:
        cp.start()
    for cp in copies:
        cp.wait()


def local(velocity, radial_op, azimuth_stencil, viscous_factor):
    dma = pltpu.SemaphoreType.DMA
    block = velocity.shape
    any_space = pl.BlockSpec(memory_space=pl.ANY)
    in_place = [
        pltpu.with_memory_space_constraint(x, pltpu.HBM) for x in (velocity, radial_op.T, azimuth_stencil)
    ]
    tile = (8, LANES)
    shapes = (jax.ShapeDtypeStruct(block, F32), jax.ShapeDtypeStruct(block, F32))
    outs = pl.pallas_call(
        kernel,
        name="substep",
        out_shape=shapes,
        in_specs=[any_space] * 3 + [pl.BlockSpec(memory_space=pltpu.SMEM)],
        out_specs=(any_space, any_space),
        scratch_shapes=[
            pltpu.SMEM((2 * REACH + 1,), F32),
            pltpu.VMEM((3, PTS + 2 * REACH, 8, NR), F32),
            pltpu.VMEM((NR + RT, NR), F32),
            pltpu.VMEM((NR + RT, NR), BF16),
            pltpu.VMEM((NR + RT, NR), BF16),
            pltpu.VMEM((12, 8, NR), F32),
            pltpu.VMEM((12, 8, NR), F32),
            pltpu.VMEM((2, 12, 8, NR), F32),
            pltpu.VMEM((2, 12, 8, NR), F32),
            pltpu.VMEM((3, 4, *tile), F32),
            pltpu.VMEM((3, 4, *tile), F32),
            pltpu.VMEM(block, F32),
            pltpu.VMEM(block, F32),
            pltpu.VMEM(block, F32),
            pltpu.VMEM(block, F32),
            pltpu.VMEM((TILES, *tile), F32),
            pltpu.VMEM((TILES, PTS + 1, *tile), F32),
            pltpu.VMEM((TILES, *tile), F32),
            pltpu.VMEM((TILES, *tile), F32),
            pltpu.VMEM((TILES, *tile), F32),
            pltpu.VMEM((TILES, *tile), F32),
            pltpu.VMEM((GROUP, 3, *tile), F32),
            pltpu.VMEM((GROUP, 3, *tile), F32),
            pltpu.VMEM((GROUP, 3, *tile), F32),
            pltpu.VMEM((2, 3, *tile), F32),
            pltpu.VMEM((GROUP, 3, *tile), F32),
            pltpu.VMEM((GROUP, 3, *tile), F32),
            pltpu.VMEM((GROUP, 3, *tile), F32),
            pltpu.VMEM((BLOCKS, 3, *tile), F32),
            pltpu.VMEM((GROUP, 3, *tile), F32),
            dma((4,)),
            dma((2,)), dma((2,)), dma((2, 3)), dma((2, 3)),
            dma((2, 2)), dma((GROUP,)), dma((GROUP,)), dma((GROUP,)), dma((2,)),
            dma((GROUP - 1,)), dma((GROUP - 1,)),
            dma((BLOCKS - 1,)), dma((BLOCKS - 1,)),
            dma((GROUP - 1,)), dma((GROUP - 1,)),
            dma((4,)),
            pltpu.SemaphoreType.REGULAR((3,)),
        ],
        compiler_params=pltpu.CompilerParams(
            collective_id=0, has_side_effects=True, vmem_limit_bytes=40 << 20
        ),
    )(*in_place, viscous_factor)
    return pl.pallas_call(
        write_out,
        name="write_out",
        out_shape=(pltpu.HBM(block, F32), pltpu.HBM(block, F32)),
        in_specs=[pl.BlockSpec(memory_space=pltpu.VMEM)] * 2,
        out_specs=(any_space, any_space),
        scratch_shapes=[dma((2, 3))],
    )(*[pltpu.with_memory_space_constraint(x, pltpu.VMEM) for x in outs])


def solution(mesh):
    spec = P(None, "theta", "gz", None)
    return jax.shard_map(
        local, mesh=mesh, in_specs=(spec, P(), P(), P()), out_specs=(spec, spec), check_vma=False
    )
```

```python
import jax
import jax.numpy as jnp
from jax import lax
from jax.experimental import pallas as pl
from jax.experimental.pallas import tpu as pltpu
from jax.sharding import PartitionSpec as P

AXIAL_WEIGHTS = (0.75, -0.15, 1.0 / 60.0)
STEP_WEIGHT = 0.2
MIRROR_SIGNS = (-1.0, -1.0, 1.0)
MESH = pl.DeviceIdType.MESH
F32 = jnp.float32
BF16 = jnp.bfloat16
REACH = 10
PTS = 16
NR = 512
RT = 32
LANES = 128
TILES = NR // LANES
GROUP = 8
SECTORS = 128
BLOCKS = SECTORS // GROUP
ROWS = (range(0, REACH), range(PTS - REACH, PTS))
RELAY = (5, 2)
PLAIN_DOT = (((1,), (0,)), ((), ()))


def split(x):
    high = x.astype(BF16)
    return high, (x - high.astype(F32)).astype(BF16)


def dot3(x, w_high, w_low):
    high, low = split(x)
    out = lax.dot_general(high, w_low, PLAIN_DOT, preferred_element_type=F32)
    out = out + lax.dot_general(low, w_high, PLAIN_DOT, preferred_element_type=F32)
    return out + lax.dot_general(high, w_high, PLAIN_DOT, preferred_element_type=F32)


def rows_of(shape):
    return lax.broadcasted_iota(jnp.int32, shape, len(shape) - 2)


def lane(shape):
    return lax.broadcasted_iota(jnp.int32, shape, len(shape) - 1)


def doubled(q):
    return q * (2.0 - q)


def pack4(x, sub):
    middle = (sub == 3) | (sub == 4)
    return (
        jnp.where(middle, pltpu.roll(x[3], 3, 0), x[0]),
        jnp.where(sub == 3, pltpu.roll(x[3], 1, 0), jnp.where(sub == 4, pltpu.roll(x[3], 7, 0), x[1])),
        jnp.where(middle, pltpu.roll(x[3], 5, 0), x[2]),
    )


def unpack4(y, sub):
    fourth = jnp.where(
        sub < 2,
        pltpu.roll(y[0], 5, 0),
        jnp.where(
            sub == 2,
            pltpu.roll(y[1], 7, 0),
            jnp.where(sub == 5, pltpu.roll(y[1], 1, 0), pltpu.roll(y[2], 3, 0)),
        ),
    )
    return (y[0], y[1], y[2], fourth)


def axial_parts(x, sub):
    own = far = None
    for m, weight in enumerate(AXIAL_WEIGHTS, 1):
        upper = weight * pltpu.roll(x, 8 - m, 0)
        lower = weight * pltpu.roll(x, m, 0)
        inside = jnp.where(sub < 8 - m, upper, 0.0) - jnp.where(sub >= m, lower, 0.0)
        outside = jnp.where(sub < 8 - m, 0.0, upper) - jnp.where(sub >= m, 0.0, lower)
        own = inside if own is None else own + inside
        far = outside if far is None else far + outside
    return own, far


def kernel(
    v_hbm, op_hbm, sten_hbm, visc, loc, part, ends, pow_t, scale_t,
    sten,
    ext, op_v, wh, wl, esend, erecv, gsend, grecv, msend, mrecv, own_ax, far_ax,
    inv_t, w_t, big_t, inv_n, ssend, sum_in, hsend, halo_in, fb, up_in, ret, tot, car,
    in_sem, e_sem, mir_sem, up_sem, down_sem, g_sem, v_s, v_r, h_s, h_r,
    p1_s, p1_r, p2_s, p2_r, p3_s, p3_r, relay_in, relay_out, passing, chain,
):
    p = lax.axis_index("theta")
    g = lax.axis_index("gz")
    me = p % GROUP
    block = p // GROUP
    backward = me // TILES
    my_tile = me % TILES
    sub = rows_of((8, LANES))

    reads = [
        pltpu.make_async_copy(v_hbm, ext.at[:, pl.ds(REACH, PTS)], in_sem.at[0]),
        pltpu.make_async_copy(op_hbm, op_v, in_sem.at[1]),
        pltpu.make_async_copy(sten_hbm, sten, in_sem.at[2]),
    ]
    for r in reads:
        r.start()

    after = (p + 1) % SECTORS
    before = (p + SECTORS - 1) % SECTORS
    across = (p + SECTORS // 2) % SECTORS
    barrier = pltpu.get_barrier_semaphore()
    greeted = [(after, g), (before, g)]
    greeted += [(block * GROUP + (me + k) % GROUP, g) for k in range(1, GROUP)]
    greeted += [(p, 1 - g)]
    hop = [((p + d) % SECTORS, g) for d in (2 * GROUP, SECTORS - 2 * GROUP, 4 * GROUP, SECTORS - 4 * GROUP)]
    side_block = (block + 1 - 2 * (block % 2)) * GROUP + me
    greeted += [*hop[:2], (side_block, g)]
    for who in greeted:
        pl.semaphore_signal(barrier, inc=1, device_id=who, device_id_type=MESH)

    def cols(t):
        return pl.ds(pl.multiple_of(t * LANES, LANES), LANES)

    reads[0].wait()

    def pack_axial(t, carry):
        for i in range(PTS // 4):
            x = [ext[2, REACH + 4 * i + j, :, cols(t)] for j in range(4)]
            for j, y in enumerate(pack4(x, sub)):
                esend[3 * i + j, :, cols(t)] = y
        return carry

    lax.fori_loop(0, TILES, pack_axial, 0)
    quarter = lane((8, LANES)) // RT
    for c in range(3):
        for i in range(PTS // 4):
            line = ext[c, REACH + 4 * i, :, :LANES]
            for j in range(1, 4):
                line = jnp.where(quarter == j, pltpu.roll(ext[c, REACH + 4 * i + j, :, :LANES], RT * j, 1), line)
            msend[c, i] = MIRROR_SIGNS[c] * line

    pl.semaphore_wait(barrier, len(greeted))

    def tell(stage, whom):
        for who in whom:
            pl.semaphore_signal(chain.at[stage], inc=1, device_id=who, device_id_type=MESH)

    tell(0, hop[:2])

    def remote(src, dst, s_sem, r_sem, who):
        return pltpu.make_async_remote_copy(
            src_ref=src, dst_ref=dst, send_sem=s_sem, recv_sem=r_sem, device_id=who, device_id_type=MESH
        )

    def pair(src, dst, sem, who):
        return remote(src, dst, sem.at[0], sem.at[1], who)

    planes_e = pair(esend, erecv, e_sem, (p, 1 - g))
    halo_up, halo_down = [], []
    for c in range(3):
        halo_up.append(
            remote(ext.at[c, pl.ds(PTS, REACH)], ext.at[c, pl.ds(0, REACH)], up_sem.at[0, c], up_sem.at[1, c], (after, g))
        )
        halo_down.append(
            remote(
                ext.at[c, pl.ds(REACH, REACH)], ext.at[c, pl.ds(REACH + PTS, REACH)],
                down_sem.at[0, c], down_sem.at[1, c], (before, g),
            )
        )
    next_block, last_block = (block + 1) % BLOCKS, (block + BLOCKS - 1) % BLOCKS
    halo_up_last, halo_down_last = ext.at[0, pl.ds(PTS, REACH)], ext.at[0, pl.ds(REACH, REACH)]
    to_relay = [
        pair(halo_up_last, passing, relay_in, (next_block * GROUP + RELAY[0], g)),
        pair(halo_down_last, passing, relay_in, (last_block * GROUP + RELAY[1], g)),
    ]
    relayed = [
        pair(passing, ext.at[0, pl.ds(0, REACH)], relay_out, (block * GROUP, g)),
        pair(passing, ext.at[0, pl.ds(REACH + PTS, REACH)], relay_out, (block * GROUP + GROUP - 1, g)),
    ]
    mirror = pair(msend, mrecv, mir_sem, (across, g))
    sums = []
    for k in range(GROUP):
        other = (me + k) % GROUP
        sums.append(
            remote(ssend.at[other], sum_in.at[me], v_s.at[k], v_r.at[k], (block * GROUP + other, 1 - g))
        )
    planes = [
        remote(gsend.at[c], grecv.at[c], g_sem.at[0, c], g_sem.at[1, c], (p, 1 - g)) for c in range(2)
    ]
    first, final = me == 0, me == GROUP - 1
    planes_e.start()
    halo_up[1].start()
    halo_down[1].start()

    @pl.when(me != GROUP - 1)
    def _():
        halo_up[0].start()
        halo_up[2].start()

    @pl.when(me != 0)
    def _():
        halo_down[0].start()
        halo_down[2].start()

    reads[2].wait()
    radius = lane((8, NR)).astype(F32) + 0.5
    inverse_r = 1.0 / radius
    coef = visc[0] * inverse_r * inverse_r
    half = 0.5 / coef
    gap = jnp.sqrt(half * (2.0 + half)) - half
    rho = 1.0 - gap
    scale = 1.0 / jnp.sqrt(1.0 + 4.0 * coef)
    gap16 = doubled(doubled(doubled(doubled(gap))))
    gap128 = doubled(doubled(doubled(gap16)))
    whole = doubled(doubled(doubled(doubled(gap128))))
    for t in range(TILES):
        here = slice(t * LANES, (t + 1) * LANES)
        inv_t[t] = inverse_r[:, here]
        scale_t[t] = scale[:, here]
        w_t[t] = 1.0 - gap16[:, here]
        big_t[t] = 1.0 - gap128[:, here]
        inv_n[t] = 1.0 / whole[:, here]
        power = jnp.ones((8, LANES), F32)
        for j in range(PTS + 1):
            pow_t[t, j] = power
            power = power * rho[:, here]

    def spread(t, carry):
        for c in range(3):
            for i in range(PTS // 4):
                far = []
                for j in range(4):
                    row = 4 * i + j
                    inside, outside = axial_parts(ext[c, REACH + row, :, cols(t)], sub)
                    own_ax[c, row, :, cols(t)] = inside
                    far_ax[c, row, :, cols(t)] = outside
                    far.append(outside)
                if c < 2:
                    for j, y in enumerate(pack4(far, sub)):
                        gsend[c, 3 * i + j, :, cols(t)] = y
        return carry

    lax.fori_loop(0, TILES, spread, 0)

    pl.semaphore_wait(chain.at[0], 2)
    tell(1, hop[2:])

    reads[1].wait()
    op_high, op_low = split(op_v[...])
    wh[...] = op_high
    wl[...] = op_low
    for c in range(3):
        lines = ext[c, pl.ds(REACH, PTS)].reshape(PTS * 8, NR)
        part[c] = dot3(lines, wh[pl.ds(0, NR)], wl[pl.ds(0, NR)]).reshape(PTS, 8, NR)

    pl.semaphore_wait(chain.at[1], 2)
    mirror.start()
    tell(2, [(side_block, g)])

    def azimuth(t, carry):
        inv = inv_t[t]
        for c in range(3):
            x = [ext[c, REACH + k, :, cols(t)] for k in range(PTS)]
            for row in range(PTS):
                grad = None
                for k in range(max(0, row - REACH), min(PTS, row + REACH + 1)):
                    tap = sten[k - row + REACH] * x[k]
                    grad = tap if grad is None else grad + tap
                a = ext[0, REACH + row, :, cols(t)]
                b = ext[1, REACH + row, :, cols(t)]
                e = ext[2, REACH + row, :, cols(t)]
                if c == 0:
                    grad = grad - b
                if c == 1:
                    grad = grad + a
                part[c, row, :, cols(t)] = (
                    a * part[c, row, :, cols(t)] + (b * inv) * grad + e * own_ax[c, row, :, cols(t)]
                )
        return carry

    lax.fori_loop(0, TILES, azimuth, 0)

    def local_sums(t, carry):
        rho = pow_t[t, 1]
        for c in range(3):
            ahead = back = None
            for row in range(PTS):
                right = ext[c, REACH + row, :, cols(t)] - STEP_WEIGHT * part[c, row, :, cols(t)]
                ahead = right if row == 0 else rho * ahead + right
                back = right if row == 0 else back + pow_t[t, row] * right
            fb[t, c] = ahead
            fb[TILES + t, c] = back
        return carry

    lax.fori_loop(0, TILES, local_sums, 0)

    planes_e.wait_recv()

    def partner_sums(t, carry):
        rho = pow_t[t, 1]
        e = []
        for i in range(PTS // 4):
            e += unpack4([erecv[3 * i + j, :, cols(t)] for j in range(3)], sub)
        for c in range(3):
            ahead = back = None
            for row in range(PTS):
                x = e[row] * far_ax[c, row, :, cols(t)]
                ahead = x if row == 0 else rho * ahead + x
                back = x if row == 0 else back + pow_t[t, row] * x
            ssend[t, c] = -STEP_WEIGHT * ahead
            ssend[TILES + t, c] = -STEP_WEIGHT * back
        return carry

    lax.fori_loop(0, TILES, partner_sums, 0)
    for cp in sums:
        cp.start()

    def halo_taps(t, c, row, shift):
        span = range(row, REACH) if shift[0] == 0 else range(REACH + PTS, row + 2 * REACH + 1)
        grad = None
        for k in span:
            tap = sten[k - row] * ext[c, k + shift[1], :, cols(t)]
            grad = tap if grad is None else grad + tap
        return grad

    def edge_sums(side):
        shift = (side, PTS if side == 0 else -PTS)
        theirs = REACH + PTS if side == 0 else REACH - PTS

        def body(t, carry):
            inv, rho = inv_t[t], pow_t[t, 1]
            for c in range(3):
                ahead = back = None
                for row in ROWS[side]:
                    x = (ext[1, row + theirs, :, cols(t)] * inv) * halo_taps(t, c, row, shift)
                    ahead = x if ahead is None else rho * ahead + x
                    x = pow_t[t, row] * x
                    back = x if back is None else back + x
                if side == 0:
                    ahead = ahead * pow_t[t, PTS - REACH]
                hsend[t, c] = -STEP_WEIGHT * ahead
                hsend[TILES + t, c] = -STEP_WEIGHT * back
            return carry

        lax.fori_loop(0, TILES, body, 0)

    def edge_copies(side):
        to = (block + 1) % BLOCKS if side == 0 else (block + BLOCKS - 1) % BLOCKS
        return [
            remote(hsend.at[k], halo_in.at[side], h_s.at[k], h_r.at[side], (to * GROUP + k, g)) for k in range(GROUP)
        ]

    edge = [edge_copies(0), edge_copies(1)]

    @pl.when(final)
    def _():
        halo_down[1].wait_recv()
        edge_sums(0)
        for cp in edge[0]:
            cp.start()

    @pl.when(first)
    def _():
        halo_up[1].wait_recv()
        edge_sums(1)
        for cp in edge[1]:
            cp.start()

    for cp in planes:
        cp.start()

    @pl.when(final)
    def _():
        to_relay[0].start()
        halo_up[2].start()

    @pl.when(first)
    def _():
        to_relay[1].start()
        halo_down[2].start()

    def add_halo(side, summed):
        def body(t, carry):
            inv, rho = inv_t[t], pow_t[t, 1]
            for c in range(3):
                ahead = back = None
                for row in ROWS[side]:
                    x = (ext[1, REACH + row, :, cols(t)] * inv) * halo_taps(t, c, row, (side, 0))
                    part[c, row, :, cols(t)] = part[c, row, :, cols(t)] + x
                    if summed:
                        ahead = x if ahead is None else rho * ahead + x
                        x = pow_t[t, row] * x
                        back = x if back is None else back + x
                if summed:
                    if side == 0:
                        ahead = ahead * pow_t[t, PTS - REACH]
                    fb[t, c] = fb[t, c] - STEP_WEIGHT * ahead
                    fb[TILES + t, c] = fb[TILES + t, c] - STEP_WEIGHT * back
            return carry

        lax.fori_loop(0, TILES, body, 0)

    @pl.when(me != 0)
    def _():
        for cp in (halo_up[1], halo_up[0], halo_up[2]):
            cp.wait_recv()
        add_halo(0, True)

    @pl.when(me != GROUP - 1)
    def _():
        for cp in (halo_down[1], halo_down[0], halo_down[2]):
            cp.wait_recv()
        add_halo(1, True)

    mirror.wait_recv()
    for i in range(PTS // 4):
        lines = []
        for c in range(3):
            packed = mrecv[c, i]
            lines += [packed[:, :RT]] + [pltpu.roll(packed, LANES - RT * j, 1)[:, :RT] for j in range(1, 4)]
        more = dot3(jnp.concatenate(lines, axis=0), wh[pl.ds(NR, RT)], wl[pl.ds(NR, RT)]).reshape(3, 4, 8, NR)
        for t in range(TILES):
            here = slice(t * LANES, (t + 1) * LANES)
            for c in range(3):
                ahead, back = fb[t, c], fb[TILES + t, c]
                for j in range(4):
                    row = 4 * i + j
                    x = ext[0, REACH + row, :, here] * more[c, j, :, here]
                    part[c, row, :, here] = part[c, row, :, here] + x
                    x = -STEP_WEIGHT * x
                    ahead = ahead + pow_t[t, PTS - 1 - row] * x
                    back = back + pow_t[t, row] * x
                fb[t, c] = ahead
                fb[TILES + t, c] = back

    one, two, three = [], [], []
    for k in sorted(range(1, GROUP), key=lambda k: abs(k - GROUP // 2)):
        other = (me + k) % GROUP
        cp = remote(fb.at[other], up_in.at[me], p1_s.at[k - 1], p1_r.at[k - 1], (block * GROUP + other, g))
        cp.start()
        one.append(cp)
    up_in[me] = fb[me]

    def finish_term(c):
        def body(t, carry):
            rho = pow_t[t, 1]
            right = []
            left = []
            for i in range(PTS // 4):
                if c < 2:
                    far = unpack4([grecv[c, 3 * i + j, :, cols(t)] for j in range(3)], sub)
                else:
                    far = unpack4([erecv[3 * i + j, :, cols(t)] for j in range(3)], sub)
                for j in range(4):
                    row = 4 * i + j
                    grad = far[j]
                    if c == 2:
                        grad = axial_parts(grad, sub)[1]
                    else:
                        grad = jnp.where((sub == 3) | (sub == 4), 0.0, grad)
                    term = part[c, row, :, cols(t)] + ext[2, REACH + row, :, cols(t)] * grad
                    part[c, row, :, cols(t)] = term
                    right.append(ext[c, REACH + row, :, cols(t)] - STEP_WEIGHT * term)
                    left.append(right[row] if row == 0 else right[row] + rho * left[row - 1])
            run = None
            for row in range(PTS - 1, -1, -1):
                if run is None:
                    loc[c, row, :, cols(t)] = left[row]
                    run = right[row]
                else:
                    run = rho * run
                    loc[c, row, :, cols(t)] = left[row] + run
                    run = right[row] + run
            return carry

        lax.fori_loop(0, TILES, body, 0)

    def entry(k):
        return k + backward * (GROUP - 1 - 2 * k)

    pl.semaphore_wait(chain.at[2], 1)
    for cp in (*one, *sums, edge[0][0], edge[1][0]):
        cp.wait_recv()
    for k in range(GROUP):
        total = up_in[k] + sum_in[k]
        if k == 0:
            total = total + halo_in[0]
        if k == GROUP - 1:
            total = total + halo_in[1]
        up_in[k] = total
    w = w_t[my_tile]
    run = up_in[entry(0)]
    for k in range(1, GROUP):
        run = up_in[entry(k)] + w * run
    tot[block] = run
    for k in sorted(range(1, BLOCKS), key=lambda k: abs(k - BLOCKS // 2)):
        cp = remote(
            tot.at[block], tot.at[block], p2_s.at[k - 1], p2_r.at[k - 1],
            (((block + k) % BLOCKS) * GROUP + me, g),
        )
        cp.start()
        two.append(cp)


    for side in range(2):

        @pl.when(me == RELAY[side])
        def _(side=side):
            to_relay[side].wait_recv()
            relayed[side].start()

    for cp in two:
        cp.wait_recv()
    big = big_t[my_tile]
    run = tot[block]
    for m in range(BLOCKS - 1, 0, -1):
        run = tot[(block + (2 * backward - 1) * m + BLOCKS) % BLOCKS] + big * run
    run = run * inv_n[my_tile]
    for k in range(GROUP):
        ret[entry(k)] = run
        run = up_in[entry(k)] + w * run
    for k in sorted(range(1, GROUP), key=lambda k: abs(k - GROUP // 2)):
        other = (me + k) % GROUP
        cp = remote(ret.at[other], car.at[me], p3_s.at[k - 1], p3_r.at[k - 1], (block * GROUP + other, g))
        cp.start()
        three.append(cp)
    car[me] = ret[me]

    @pl.when(first)
    def _():
        relayed[0].wait_recv()
        halo_up[2].wait_recv()
        add_halo(0, False)

    @pl.when(final)
    def _():
        relayed[1].wait_recv()
        halo_down[2].wait_recv()
        add_halo(1, False)

    finish_term(2)
    for c in range(2):
        planes[c].wait_recv()
        finish_term(c)

    for cp in three:
        cp.wait_recv()

    for t in range(TILES):
        ends[t] = scale_t[t] * car[t]
        ends[TILES + t] = scale_t[t] * car[TILES + t]
    for cp in (planes_e, *halo_up[1:], *halo_down[1:], mirror, *sums, *planes, *one, *two, *three):
        cp.wait_send()

    @pl.when(me != GROUP - 1)
    def _():
        halo_up[0].wait_send()

    @pl.when(me != 0)
    def _():
        halo_down[0].wait_send()

    for side in range(2):

        @pl.when(me == RELAY[side])
        def _(side=side):
            relayed[side].wait_send()

    for side, here in ((0, final), (1, first)):

        @pl.when(here)
        def _(side=side):
            for cp in (*edge[side], to_relay[side]):
                cp.wait_send()


def write_out(loc, part, ends, pow_t, scale_t, new_out, non_out, new, sem):
    def copy(src, dst, k, c):
        cp = pltpu.make_async_copy(src.at[c], dst.at[c], sem.at[k, c])
        cp.start()
        return cp

    copies = [copy(part, non_out, 1, c) for c in range(3)]
    for c in range(3):
        for t in range(TILES):
            here = slice(t * LANES, (t + 1) * LANES)
            for row in range(PTS):
                new[c, row, :, here] = (
                    scale_t[t] * loc[c, row, :, here]
                    + pow_t[t, row + 1] * ends[t, c]
                    + pow_t[t, PTS - row] * ends[TILES + t, c]
                )
        copies.append(copy(new, new_out, 0, c))
    for cp in copies:
        cp.wait()


def local(velocity, radial_op, azimuth_stencil, viscous_factor):
    dma = pltpu.SemaphoreType.DMA
    block = velocity.shape
    any_space = pl.BlockSpec(memory_space=pl.ANY)
    in_place = [
        pltpu.with_memory_space_constraint(x, pltpu.HBM) for x in (velocity, radial_op.T, azimuth_stencil)
    ]
    tile = (8, LANES)
    kept = tuple(
        jax.ShapeDtypeStruct(shape, F32)
        for shape in (block, block, (GROUP, 3, *tile), (TILES, PTS + 1, *tile), (TILES, *tile))
    )
    outs = pl.pallas_call(
        kernel,
        name="substep",
        out_shape=kept,
        in_specs=[any_space] * 3 + [pl.BlockSpec(memory_space=pltpu.SMEM)],
        out_specs=(pl.BlockSpec(memory_space=pltpu.VMEM),) * len(kept),
        scratch_shapes=[
            pltpu.SMEM((2 * REACH + 1,), F32),
            pltpu.VMEM((3, PTS + 2 * REACH, 8, NR), F32),
            pltpu.VMEM((NR + RT, NR), F32),
            pltpu.VMEM((NR + RT, NR), BF16),
            pltpu.VMEM((NR + RT, NR), BF16),
            pltpu.VMEM((12, 8, NR), F32),
            pltpu.VMEM((12, 8, NR), F32),
            pltpu.VMEM((2, 12, 8, NR), F32),
            pltpu.VMEM((2, 12, 8, NR), F32),
            pltpu.VMEM((3, 4, *tile), F32),
            pltpu.VMEM((3, 4, *tile), F32),
            pltpu.VMEM(block, F32),
            pltpu.VMEM(block, F32),
            pltpu.VMEM((TILES, *tile), F32),
            pltpu.VMEM((TILES, *tile), F32),
            pltpu.VMEM((TILES, *tile), F32),
            pltpu.VMEM((TILES, *tile), F32),
            pltpu.VMEM((GROUP, 3, *tile), F32),
            pltpu.VMEM((GROUP, 3, *tile), F32),
            pltpu.VMEM((GROUP, 3, *tile), F32),
            pltpu.VMEM((2, 3, *tile), F32),
            pltpu.VMEM((GROUP, 3, *tile), F32),
            pltpu.VMEM((GROUP, 3, *tile), F32),
            pltpu.VMEM((GROUP, 3, *tile), F32),
            pltpu.VMEM((BLOCKS, 3, *tile), F32),
            pltpu.VMEM((GROUP, 3, *tile), F32),
            dma((4,)),
            dma((2,)), dma((2,)), dma((2, 3)), dma((2, 3)),
            dma((2, 2)), dma((GROUP,)), dma((GROUP,)), dma((GROUP,)), dma((2,)),
            dma((GROUP - 1,)), dma((GROUP - 1,)),
            dma((BLOCKS - 1,)), dma((BLOCKS - 1,)),
            dma((GROUP - 1,)), dma((GROUP - 1,)),
            dma((2,)), dma((2,)),
            pltpu.VMEM((REACH, 8, NR), F32),
            pltpu.SemaphoreType.REGULAR((3,)),
        ],
        compiler_params=pltpu.CompilerParams(
            collective_id=0, has_side_effects=True, vmem_limit_bytes=40 << 20
        ),
    )(*in_place, viscous_factor)
    return pl.pallas_call(
        write_out,
        name="write_out",
        out_shape=(pltpu.HBM(block, F32), pltpu.HBM(block, F32)),
        in_specs=[pl.BlockSpec(memory_space=pltpu.VMEM)] * len(kept),
        out_specs=(any_space, any_space),
        scratch_shapes=[pltpu.VMEM(block, F32), dma((2, 3))],
    )(*[pltpu.with_memory_space_constraint(x, pltpu.VMEM) for x in outs])


def solution(mesh):
    spec = P(None, "theta", "gz", None)
    return jax.shard_map(
        local, mesh=mesh, in_specs=(spec, P(), P(), P()), out_specs=(spec, spec), check_vma=False
    )
```

```python
import jax
import jax.numpy as jnp
from jax import lax
from jax.experimental import pallas as pl
from jax.experimental.pallas import tpu as pltpu
from jax.sharding import PartitionSpec as P

AXIAL_WEIGHTS = (0.75, -0.15, 1.0 / 60.0)
STEP_WEIGHT = 0.2
MIRROR_SIGNS = (-1.0, -1.0, 1.0)
MESH = pl.DeviceIdType.MESH
F32 = jnp.float32
BF16 = jnp.bfloat16
REACH = 10
PTS = 16
NR = 512
RT = 32
LANES = 128
TILES = NR // LANES
GROUP = 8
SECTORS = 128
BLOCKS = SECTORS // GROUP
ROWS = (range(0, REACH), range(PTS - REACH, PTS))
RELAY = (5, 2)
PLAIN_DOT = (((1,), (0,)), ((), ()))


def split(x):
    high = x.astype(BF16)
    return high, (x - high.astype(F32)).astype(BF16)


def dot3(x, w_high, w_low):
    high, low = split(x)
    out = lax.dot_general(high, w_low, PLAIN_DOT, preferred_element_type=F32)
    out = out + lax.dot_general(low, w_high, PLAIN_DOT, preferred_element_type=F32)
    return out + lax.dot_general(high, w_high, PLAIN_DOT, preferred_element_type=F32)


def rows_of(shape):
    return lax.broadcasted_iota(jnp.int32, shape, len(shape) - 2)


def lane(shape):
    return lax.broadcasted_iota(jnp.int32, shape, len(shape) - 1)


def doubled(q):
    return q * (2.0 - q)


def pack4(x, sub):
    middle = (sub == 3) | (sub == 4)
    return (
        jnp.where(middle, pltpu.roll(x[3], 3, 0), x[0]),
        jnp.where(sub == 3, pltpu.roll(x[3], 1, 0), jnp.where(sub == 4, pltpu.roll(x[3], 7, 0), x[1])),
        jnp.where(middle, pltpu.roll(x[3], 5, 0), x[2]),
    )


def unpack4(y, sub):
    fourth = jnp.where(
        sub < 2,
        pltpu.roll(y[0], 5, 0),
        jnp.where(
            sub == 2,
            pltpu.roll(y[1], 7, 0),
            jnp.where(sub == 5, pltpu.roll(y[1], 1, 0), pltpu.roll(y[2], 3, 0)),
        ),
    )
    return (y[0], y[1], y[2], fourth)


def axial_parts(x, sub):
    own = far = None
    for m, weight in enumerate(AXIAL_WEIGHTS, 1):
        upper = weight * pltpu.roll(x, 8 - m, 0)
        lower = weight * pltpu.roll(x, m, 0)
        inside = jnp.where(sub < 8 - m, upper, 0.0) - jnp.where(sub >= m, lower, 0.0)
        outside = jnp.where(sub < 8 - m, 0.0, upper) - jnp.where(sub >= m, 0.0, lower)
        own = inside if own is None else own + inside
        far = outside if far is None else far + outside
    return own, far


def kernel(
    v_hbm, op_hbm, sten_hbm, visc, loc, part, ends, pow_t, scale_t,
    sten,
    ext, op_v, wh, wl, esend, erecv, gsend, grecv, msend, mrecv, own_ax, far_ax,
    inv_t, w_t, big_t, inv_n, ssend, sum_in, hsend, halo_in, fb, up_in, ret, tot, car,
    in_sem, e_sem, mir_sem, up_sem, down_sem, g_sem, v_s, v_r, h_s, h_r,
    p1_s, p1_r, p2_s, p2_r, p3_s, p3_r, relay_in, relay_out, passing, chain,
):
    p = lax.axis_index("theta")
    g = lax.axis_index("gz")
    me = p % GROUP
    block = p // GROUP
    backward = me // TILES
    my_tile = me % TILES
    sub = rows_of((8, LANES))

    reads = [
        pltpu.make_async_copy(v_hbm, ext.at[:, pl.ds(REACH, PTS)], in_sem.at[0]),
        pltpu.make_async_copy(op_hbm, op_v, in_sem.at[1]),
        pltpu.make_async_copy(sten_hbm, sten, in_sem.at[2]),
    ]
    for r in reads:
        r.start()

    after = (p + 1) % SECTORS
    before = (p + SECTORS - 1) % SECTORS
    across = (p + SECTORS // 2) % SECTORS
    barrier = pltpu.get_barrier_semaphore()
    greeted = [(after, g), (before, g)]
    greeted += [(block * GROUP + (me + k) % GROUP, g) for k in range(1, GROUP)]
    greeted += [(p, 1 - g)]
    hop = [((p + d) % SECTORS, g) for d in (2 * GROUP, SECTORS - 2 * GROUP, 4 * GROUP, SECTORS - 4 * GROUP)]
    side_block = (block + 1 - 2 * (block % 2)) * GROUP + me
    greeted += [*hop[:2], (side_block, g)]
    for who in greeted:
        pl.semaphore_signal(barrier, inc=1, device_id=who, device_id_type=MESH)

    def cols(t):
        return pl.ds(pl.multiple_of(t * LANES, LANES), LANES)

    reads[0].wait()

    def pack_axial(t, carry):
        for i in range(PTS // 4):
            x = [ext[2, REACH + 4 * i + j, :, cols(t)] for j in range(4)]
            for j, y in enumerate(pack4(x, sub)):
                esend[3 * i + j, :, cols(t)] = y
        return carry

    lax.fori_loop(0, TILES, pack_axial, 0)
    quarter = lane((8, LANES)) // RT
    for c in range(3):
        for i in range(PTS // 4):
            line = ext[c, REACH + 4 * i, :, :LANES]
            for j in range(1, 4):
                line = jnp.where(quarter == j, pltpu.roll(ext[c, REACH + 4 * i + j, :, :LANES], RT * j, 1), line)
            msend[c, i] = MIRROR_SIGNS[c] * line

    pl.semaphore_wait(barrier, len(greeted))

    def tell(stage, whom):
        for who in whom:
            pl.semaphore_signal(chain.at[stage], inc=1, device_id=who, device_id_type=MESH)

    tell(0, hop[:2])

    def remote(src, dst, s_sem, r_sem, who):
        return pltpu.make_async_remote_copy(
            src_ref=src, dst_ref=dst, send_sem=s_sem, recv_sem=r_sem, device_id=who, device_id_type=MESH
        )

    def pair(src, dst, sem, who):
        return remote(src, dst, sem.at[0], sem.at[1], who)

    planes_e = pair(esend, erecv, e_sem, (p, 1 - g))
    halo_up, halo_down = [], []
    for c in range(3):
        halo_up.append(
            remote(ext.at[c, pl.ds(PTS, REACH)], ext.at[c, pl.ds(0, REACH)], up_sem.at[0, c], up_sem.at[1, c], (after, g))
        )
        halo_down.append(
            remote(
                ext.at[c, pl.ds(REACH, REACH)], ext.at[c, pl.ds(REACH + PTS, REACH)],
                down_sem.at[0, c], down_sem.at[1, c], (before, g),
            )
        )
    next_block, last_block = (block + 1) % BLOCKS, (block + BLOCKS - 1) % BLOCKS
    halo_up_last, halo_down_last = ext.at[0, pl.ds(PTS, REACH)], ext.at[0, pl.ds(REACH, REACH)]
    to_relay = [
        pair(halo_up_last, passing, relay_in, (next_block * GROUP + RELAY[0], g)),
        pair(halo_down_last, passing, relay_in, (last_block * GROUP + RELAY[1], g)),
    ]
    relayed = [
        pair(passing, ext.at[0, pl.ds(0, REACH)], relay_out, (block * GROUP, g)),
        pair(passing, ext.at[0, pl.ds(REACH + PTS, REACH)], relay_out, (block * GROUP + GROUP - 1, g)),
    ]
    mirror = pair(msend, mrecv, mir_sem, (across, g))
    planes = [
        remote(gsend.at[c], grecv.at[c], g_sem.at[0, c], g_sem.at[1, c], (p, 1 - g)) for c in range(2)
    ]
    first, final = me == 0, me == GROUP - 1
    planes_e.start()
    halo_up[1].start()
    halo_down[1].start()

    @pl.when(me != GROUP - 1)
    def _():
        halo_up[0].start()
        halo_up[2].start()

    @pl.when(me != 0)
    def _():
        halo_down[0].start()
        halo_down[2].start()

    reads[2].wait()
    radius = lane((8, NR)).astype(F32) + 0.5
    inverse_r = 1.0 / radius
    coef = visc[0] * inverse_r * inverse_r
    half = 0.5 / coef
    gap = jnp.sqrt(half * (2.0 + half)) - half
    rho = 1.0 - gap
    scale = 1.0 / jnp.sqrt(1.0 + 4.0 * coef)
    gap16 = doubled(doubled(doubled(doubled(gap))))
    gap128 = doubled(doubled(doubled(gap16)))
    whole = doubled(doubled(doubled(doubled(gap128))))
    for t in range(TILES):
        here = slice(t * LANES, (t + 1) * LANES)
        inv_t[t] = inverse_r[:, here]
        scale_t[t] = scale[:, here]
        w_t[t] = 1.0 - gap16[:, here]
        big_t[t] = 1.0 - gap128[:, here]
        inv_n[t] = 1.0 / whole[:, here]
        power = jnp.ones((8, LANES), F32)
        for j in range(PTS + 1):
            pow_t[t, j] = power
            power = power * rho[:, here]

    def spread(t, carry):
        for c in range(3):
            for i in range(PTS // 4):
                far = []
                for j in range(4):
                    row = 4 * i + j
                    inside, outside = axial_parts(ext[c, REACH + row, :, cols(t)], sub)
                    own_ax[c, row, :, cols(t)] = inside
                    far_ax[c, row, :, cols(t)] = outside
                    far.append(outside)
                if c < 2:
                    for j, y in enumerate(pack4(far, sub)):
                        gsend[c, 3 * i + j, :, cols(t)] = y
        return carry

    lax.fori_loop(0, TILES, spread, 0)

    pl.semaphore_wait(chain.at[0], 2)
    tell(1, hop[2:])

    reads[1].wait()
    op_high, op_low = split(op_v[...])
    wh[...] = op_high
    wl[...] = op_low
    for c in range(3):
        lines = ext[c, pl.ds(REACH, PTS)].reshape(PTS * 8, NR)
        part[c] = dot3(lines, wh[pl.ds(0, NR)], wl[pl.ds(0, NR)]).reshape(PTS, 8, NR)

    pl.semaphore_wait(chain.at[1], 2)
    mirror.start()
    tell(2, [(side_block, g)])

    def azimuth(t, carry):
        inv = inv_t[t]
        for c in range(3):
            x = [ext[c, REACH + k, :, cols(t)] for k in range(PTS)]
            for row in range(PTS):
                grad = None
                for k in range(max(0, row - REACH), min(PTS, row + REACH + 1)):
                    tap = sten[k - row + REACH] * x[k]
                    grad = tap if grad is None else grad + tap
                a = ext[0, REACH + row, :, cols(t)]
                b = ext[1, REACH + row, :, cols(t)]
                e = ext[2, REACH + row, :, cols(t)]
                if c == 0:
                    grad = grad - b
                if c == 1:
                    grad = grad + a
                part[c, row, :, cols(t)] = (
                    a * part[c, row, :, cols(t)] + (b * inv) * grad + e * own_ax[c, row, :, cols(t)]
                )
        return carry

    lax.fori_loop(0, TILES, azimuth, 0)

    def local_sums(t, carry):
        rho = pow_t[t, 1]
        for c in range(3):
            ahead = back = None
            for row in range(PTS):
                right = ext[c, REACH + row, :, cols(t)] - STEP_WEIGHT * part[c, row, :, cols(t)]
                ahead = right if row == 0 else rho * ahead + right
                back = right if row == 0 else back + pow_t[t, row] * right
            fb[t, c] = ahead
            fb[TILES + t, c] = back
        return carry

    lax.fori_loop(0, TILES, local_sums, 0)

    @pl.when(final)
    def _():
        halo_down[1].wait_recv()
        to_relay[0].start()

    @pl.when(first)
    def _():
        halo_up[1].wait_recv()
        to_relay[1].start()

    planes_e.wait_recv()

    sums = []
    for turn in range(TILES):
        t = (my_tile + turn) % TILES
        rho = pow_t[t, 1]
        e = []
        for i in range(PTS // 4):
            e += unpack4([erecv[3 * i + j, :, cols(t)] for j in range(3)], sub)
        for c in range(3):
            ahead = back = None
            for row in range(PTS):
                x = e[row] * far_ax[c, row, :, cols(t)]
                ahead = x if row == 0 else rho * ahead + x
                back = x if row == 0 else back + pow_t[t, row] * x
            ssend[t, c] = -STEP_WEIGHT * ahead
            ssend[TILES + t, c] = -STEP_WEIGHT * back
        for k in (t, TILES + t):
            cp = remote(
                ssend.at[k], sum_in.at[me], v_s.at[len(sums)], v_r.at[0], (block * GROUP + k, 1 - g)
            )
            cp.start()
            sums.append(cp)

    def halo_taps(t, c, row, shift):
        span = range(row, REACH) if shift[0] == 0 else range(REACH + PTS, row + 2 * REACH + 1)
        grad = None
        for k in span:
            tap = sten[k - row] * ext[c, k + shift[1], :, cols(t)]
            grad = tap if grad is None else grad + tap
        return grad

    def edge_sums(side):
        shift = (side, PTS if side == 0 else -PTS)
        theirs = REACH + PTS if side == 0 else REACH - PTS

        def body(t, carry):
            inv, rho = inv_t[t], pow_t[t, 1]
            for c in range(3):
                ahead = back = None
                for row in ROWS[side]:
                    x = (ext[1, row + theirs, :, cols(t)] * inv) * halo_taps(t, c, row, shift)
                    ahead = x if ahead is None else rho * ahead + x
                    x = pow_t[t, row] * x
                    back = x if back is None else back + x
                if side == 0:
                    ahead = ahead * pow_t[t, PTS - REACH]
                hsend[t, c] = -STEP_WEIGHT * ahead
                hsend[TILES + t, c] = -STEP_WEIGHT * back
            return carry

        lax.fori_loop(0, TILES, body, 0)

    def edge_copies(side):
        to = (block + 1) % BLOCKS if side == 0 else (block + BLOCKS - 1) % BLOCKS
        return [
            remote(hsend.at[k], halo_in.at[side], h_s.at[k], h_r.at[side], (to * GROUP + k, g)) for k in range(GROUP)
        ]

    edge = [edge_copies(0), edge_copies(1)]

    @pl.when(final)
    def _():
        edge_sums(0)
        for cp in edge[0]:
            cp.start()

    @pl.when(first)
    def _():
        edge_sums(1)
        for cp in edge[1]:
            cp.start()

    for cp in planes:
        cp.start()

    @pl.when(final)
    def _():
        halo_up[2].start()

    @pl.when(first)
    def _():
        halo_down[2].start()

    def add_halo(side, summed):
        def body(t, carry):
            inv, rho = inv_t[t], pow_t[t, 1]
            for c in range(3):
                ahead = back = None
                for row in ROWS[side]:
                    x = (ext[1, REACH + row, :, cols(t)] * inv) * halo_taps(t, c, row, (side, 0))
                    part[c, row, :, cols(t)] = part[c, row, :, cols(t)] + x
                    if summed:
                        ahead = x if ahead is None else rho * ahead + x
                        x = pow_t[t, row] * x
                        back = x if back is None else back + x
                if summed:
                    if side == 0:
                        ahead = ahead * pow_t[t, PTS - REACH]
                    fb[t, c] = fb[t, c] - STEP_WEIGHT * ahead
                    fb[TILES + t, c] = fb[TILES + t, c] - STEP_WEIGHT * back
            return carry

        lax.fori_loop(0, TILES, body, 0)

    @pl.when(me != 0)
    def _():
        for cp in (halo_up[1], halo_up[0], halo_up[2]):
            cp.wait_recv()
        add_halo(0, True)

    @pl.when(me != GROUP - 1)
    def _():
        for cp in (halo_down[1], halo_down[0], halo_down[2]):
            cp.wait_recv()
        add_halo(1, True)

    mirror.wait_recv()
    for i in range(PTS // 4):
        lines = []
        for c in range(3):
            packed = mrecv[c, i]
            lines += [packed[:, :RT]] + [pltpu.roll(packed, LANES - RT * j, 1)[:, :RT] for j in range(1, 4)]
        more = dot3(jnp.concatenate(lines, axis=0), wh[pl.ds(NR, RT)], wl[pl.ds(NR, RT)]).reshape(3, 4, 8, NR)
        for t in range(TILES):
            here = slice(t * LANES, (t + 1) * LANES)
            for c in range(3):
                ahead, back = fb[t, c], fb[TILES + t, c]
                for j in range(4):
                    row = 4 * i + j
                    x = ext[0, REACH + row, :, here] * more[c, j, :, here]
                    part[c, row, :, here] = part[c, row, :, here] + x
                    x = -STEP_WEIGHT * x
                    ahead = ahead + pow_t[t, PTS - 1 - row] * x
                    back = back + pow_t[t, row] * x
                fb[t, c] = ahead
                fb[TILES + t, c] = back

    one, two, three = [], [], []
    for k in sorted(range(1, GROUP), key=lambda k: abs(k - GROUP // 2)):
        other = (me + k) % GROUP
        cp = remote(fb.at[other], up_in.at[me], p1_s.at[k - 1], p1_r.at[k - 1], (block * GROUP + other, g))
        cp.start()
        one.append(cp)
    up_in[me] = fb[me]

    def finish_term(c):
        def body(t, carry):
            rho = pow_t[t, 1]
            right = []
            left = []
            for i in range(PTS // 4):
                if c < 2:
                    far = unpack4([grecv[c, 3 * i + j, :, cols(t)] for j in range(3)], sub)
                else:
                    far = unpack4([erecv[3 * i + j, :, cols(t)] for j in range(3)], sub)
                for j in range(4):
                    row = 4 * i + j
                    grad = far[j]
                    if c == 2:
                        grad = axial_parts(grad, sub)[1]
                    else:
                        grad = jnp.where((sub == 3) | (sub == 4), 0.0, grad)
                    term = part[c, row, :, cols(t)] + ext[2, REACH + row, :, cols(t)] * grad
                    part[c, row, :, cols(t)] = term
                    right.append(ext[c, REACH + row, :, cols(t)] - STEP_WEIGHT * term)
                    left.append(right[row] if row == 0 else right[row] + rho * left[row - 1])
            run = None
            for row in range(PTS - 1, -1, -1):
                if run is None:
                    loc[c, row, :, cols(t)] = left[row]
                    run = right[row]
                else:
                    run = rho * run
                    loc[c, row, :, cols(t)] = left[row] + run
                    run = right[row] + run
            return carry

        lax.fori_loop(0, TILES, body, 0)

    def entry(k):
        return k + backward * (GROUP - 1 - 2 * k)

    pl.semaphore_wait(chain.at[2], 1)
    for cp in (*one, edge[0][0], edge[1][0]):
        cp.wait_recv()
    remote(ssend, sum_in, v_s.at[0], v_r.at[0], (p, 1 - g)).wait_recv()
    for k in range(GROUP):
        total = up_in[k] + sum_in[k]
        if k == 0:
            total = total + halo_in[0]
        if k == GROUP - 1:
            total = total + halo_in[1]
        up_in[k] = total
    w = w_t[my_tile]
    run = up_in[entry(0)]
    for k in range(1, GROUP):
        run = up_in[entry(k)] + w * run
    tot[block] = run
    for k in sorted(range(1, BLOCKS), key=lambda k: abs(k - BLOCKS // 2)):
        cp = remote(
            tot.at[block], tot.at[block], p2_s.at[k - 1], p2_r.at[k - 1],
            (((block + k) % BLOCKS) * GROUP + me, g),
        )
        cp.start()
        two.append(cp)


    for side in range(2):

        @pl.when(me == RELAY[side])
        def _(side=side):
            to_relay[side].wait_recv()
            relayed[side].start()

    for cp in two:
        cp.wait_recv()
    big = big_t[my_tile]
    run = tot[block]
    for m in range(BLOCKS - 1, 0, -1):
        run = tot[(block + (2 * backward - 1) * m + BLOCKS) % BLOCKS] + big * run
    run = run * inv_n[my_tile]
    for k in range(GROUP):
        ret[entry(k)] = run
        run = up_in[entry(k)] + w * run
    for k in sorted(range(1, GROUP), key=lambda k: abs(k - GROUP // 2)):
        other = (me + k) % GROUP
        cp = remote(ret.at[other], car.at[me], p3_s.at[k - 1], p3_r.at[k - 1], (block * GROUP + other, g))
        cp.start()
        three.append(cp)
    car[me] = ret[me]

    @pl.when(first)
    def _():
        relayed[0].wait_recv()
        halo_up[2].wait_recv()
        add_halo(0, False)

    @pl.when(final)
    def _():
        relayed[1].wait_recv()
        halo_down[2].wait_recv()
        add_halo(1, False)

    finish_term(2)
    for c in range(2):
        planes[c].wait_recv()
        finish_term(c)

    for cp in three:
        cp.wait_recv()

    for t in range(TILES):
        ends[t] = scale_t[t] * car[t]
        ends[TILES + t] = scale_t[t] * car[TILES + t]
    for cp in (planes_e, *halo_up[1:], *halo_down[1:], mirror, *sums, *planes, *one, *two, *three):
        cp.wait_send()

    @pl.when(me != GROUP - 1)
    def _():
        halo_up[0].wait_send()

    @pl.when(me != 0)
    def _():
        halo_down[0].wait_send()

    for side in range(2):

        @pl.when(me == RELAY[side])
        def _(side=side):
            relayed[side].wait_send()

    for side, here in ((0, final), (1, first)):

        @pl.when(here)
        def _(side=side):
            for cp in (*edge[side], to_relay[side]):
                cp.wait_send()


def write_out(loc, part, ends, pow_t, scale_t, new_out, non_out, new, sem):
    def copy(src, dst, k, c):
        cp = pltpu.make_async_copy(src.at[c], dst.at[c], sem.at[k, c])
        cp.start()
        return cp

    copies = [copy(part, non_out, 1, c) for c in range(3)]
    for c in range(3):
        for t in range(TILES):
            here = slice(t * LANES, (t + 1) * LANES)
            for row in range(PTS):
                new[c, row, :, here] = (
                    scale_t[t] * loc[c, row, :, here]
                    + pow_t[t, row + 1] * ends[t, c]
                    + pow_t[t, PTS - row] * ends[TILES + t, c]
                )
        copies.append(copy(new, new_out, 0, c))
    for cp in copies:
        cp.wait()


def local(velocity, radial_op, azimuth_stencil, viscous_factor):
    dma = pltpu.SemaphoreType.DMA
    block = velocity.shape
    any_space = pl.BlockSpec(memory_space=pl.ANY)
    in_place = [
        pltpu.with_memory_space_constraint(x, pltpu.HBM) for x in (velocity, radial_op.T, azimuth_stencil)
    ]
    tile = (8, LANES)
    kept = tuple(
        jax.ShapeDtypeStruct(shape, F32)
        for shape in (block, block, (GROUP, 3, *tile), (TILES, PTS + 1, *tile), (TILES, *tile))
    )
    outs = pl.pallas_call(
        kernel,
        name="substep",
        out_shape=kept,
        in_specs=[any_space] * 3 + [pl.BlockSpec(memory_space=pltpu.SMEM)],
        out_specs=(pl.BlockSpec(memory_space=pltpu.VMEM),) * len(kept),
        scratch_shapes=[
            pltpu.SMEM((2 * REACH + 1,), F32),
            pltpu.VMEM((3, PTS + 2 * REACH, 8, NR), F32),
            pltpu.VMEM((NR + RT, NR), F32),
            pltpu.VMEM((NR + RT, NR), BF16),
            pltpu.VMEM((NR + RT, NR), BF16),
            pltpu.VMEM((12, 8, NR), F32),
            pltpu.VMEM((12, 8, NR), F32),
            pltpu.VMEM((2, 12, 8, NR), F32),
            pltpu.VMEM((2, 12, 8, NR), F32),
            pltpu.VMEM((3, 4, *tile), F32),
            pltpu.VMEM((3, 4, *tile), F32),
            pltpu.VMEM(block, F32),
            pltpu.VMEM(block, F32),
            pltpu.VMEM((TILES, *tile), F32),
            pltpu.VMEM((TILES, *tile), F32),
            pltpu.VMEM((TILES, *tile), F32),
            pltpu.VMEM((TILES, *tile), F32),
            pltpu.VMEM((GROUP, 3, *tile), F32),
            pltpu.VMEM((GROUP, 3, *tile), F32),
            pltpu.VMEM((GROUP, 3, *tile), F32),
            pltpu.VMEM((2, 3, *tile), F32),
            pltpu.VMEM((GROUP, 3, *tile), F32),
            pltpu.VMEM((GROUP, 3, *tile), F32),
            pltpu.VMEM((GROUP, 3, *tile), F32),
            pltpu.VMEM((BLOCKS, 3, *tile), F32),
            pltpu.VMEM((GROUP, 3, *tile), F32),
            dma((4,)),
            dma((2,)), dma((2,)), dma((2, 3)), dma((2, 3)),
            dma((2, 2)), dma((GROUP,)), dma((1,)), dma((GROUP,)), dma((2,)),
            dma((GROUP - 1,)), dma((GROUP - 1,)),
            dma((BLOCKS - 1,)), dma((BLOCKS - 1,)),
            dma((GROUP - 1,)), dma((GROUP - 1,)),
            dma((2,)), dma((2,)),
            pltpu.VMEM((REACH, 8, NR), F32),
            pltpu.SemaphoreType.REGULAR((3,)),
        ],
        compiler_params=pltpu.CompilerParams(
            collective_id=0, has_side_effects=True, vmem_limit_bytes=40 << 20
        ),
    )(*in_place, viscous_factor)
    return pl.pallas_call(
        write_out,
        name="write_out",
        out_shape=(pltpu.HBM(block, F32), pltpu.HBM(block, F32)),
        in_specs=[pl.BlockSpec(memory_space=pltpu.VMEM)] * len(kept),
        out_specs=(any_space, any_space),
        scratch_shapes=[pltpu.VMEM(block, F32), dma((2, 3))],
    )(*[pltpu.with_memory_space_constraint(x, pltpu.VMEM) for x in outs])


def solution(mesh):
    spec = P(None, "theta", "gz", None)
    return jax.shard_map(
        local, mesh=mesh, in_specs=(spec, P(), P(), P()), out_specs=(spec, spec), check_vma=False
    )
```

```python
import jax
import jax.numpy as jnp
from jax import lax
from jax.experimental import pallas as pl
from jax.experimental.pallas import tpu as pltpu
from jax.sharding import PartitionSpec as P

AXIAL_WEIGHTS = (0.75, -0.15, 1.0 / 60.0)
STEP_WEIGHT = 0.2
MIRROR_SIGNS = (-1.0, -1.0, 1.0)
MESH = pl.DeviceIdType.MESH
F32 = jnp.float32
BF16 = jnp.bfloat16
REACH = 10
PTS = 16
NR = 512
RT = 32
LANES = 128
TILES = NR // LANES
GROUP = 8
SECTORS = 128
BLOCKS = SECTORS // GROUP
ROWS = (range(0, REACH), range(PTS - REACH, PTS))
RELAY = (5, 2)
PLAIN_DOT = (((1,), (0,)), ((), ()))


def split(x):
    high = x.astype(BF16)
    return high, (x - high.astype(F32)).astype(BF16)


def dot3(x, w_high, w_low):
    high, low = split(x)
    out = lax.dot_general(high, w_low, PLAIN_DOT, preferred_element_type=F32)
    out = out + lax.dot_general(low, w_high, PLAIN_DOT, preferred_element_type=F32)
    return out + lax.dot_general(high, w_high, PLAIN_DOT, preferred_element_type=F32)


def rows_of(shape):
    return lax.broadcasted_iota(jnp.int32, shape, len(shape) - 2)


def lane(shape):
    return lax.broadcasted_iota(jnp.int32, shape, len(shape) - 1)


def doubled(q):
    return q * (2.0 - q)


def pack4(x, sub):
    middle = (sub == 3) | (sub == 4)
    return (
        jnp.where(middle, pltpu.roll(x[3], 3, 0), x[0]),
        jnp.where(sub == 3, pltpu.roll(x[3], 1, 0), jnp.where(sub == 4, pltpu.roll(x[3], 7, 0), x[1])),
        jnp.where(middle, pltpu.roll(x[3], 5, 0), x[2]),
    )


def unpack4(y, sub):
    fourth = jnp.where(
        sub < 2,
        pltpu.roll(y[0], 5, 0),
        jnp.where(
            sub == 2,
            pltpu.roll(y[1], 7, 0),
            jnp.where(sub == 5, pltpu.roll(y[1], 1, 0), pltpu.roll(y[2], 3, 0)),
        ),
    )
    return (y[0], y[1], y[2], fourth)


def axial_parts(x, sub):
    own = far = None
    for m, weight in enumerate(AXIAL_WEIGHTS, 1):
        upper = weight * pltpu.roll(x, 8 - m, 0)
        lower = weight * pltpu.roll(x, m, 0)
        inside = jnp.where(sub < 8 - m, upper, 0.0) - jnp.where(sub >= m, lower, 0.0)
        outside = jnp.where(sub < 8 - m, 0.0, upper) - jnp.where(sub >= m, 0.0, lower)
        own = inside if own is None else own + inside
        far = outside if far is None else far + outside
    return own, far


def kernel(
    v_hbm, op_hbm, sten_hbm, visc, loc, part, ends, pow_t, scale_t,
    sten,
    ext, op_v, wh, wl, esend, erecv, gsend, grecv, msend, mrecv, own_ax, far_ax,
    inv_t, w_t, big_t, inv_n, ssend, sum_in, hsend, halo_in, fb, up_in, ret, tot, car,
    in_sem, e_sem, mir_sem, up_sem, down_sem, g_sem, v_s, v_r, h_s, h_r,
    p1_s, p1_r, p2_s, p2_r, p3_s, p3_r, relay_in, relay_out, passing, chain,
):
    p = lax.axis_index("theta")
    g = lax.axis_index("gz")
    me = p % GROUP
    block = p // GROUP
    backward = me // TILES
    my_tile = me % TILES
    sub = rows_of((8, LANES))

    reads = [
        pltpu.make_async_copy(v_hbm, ext.at[:, pl.ds(REACH, PTS)], in_sem.at[0]),
        pltpu.make_async_copy(op_hbm, op_v, in_sem.at[1]),
        pltpu.make_async_copy(sten_hbm, sten, in_sem.at[2]),
    ]
    for r in reads:
        r.start()

    after = (p + 1) % SECTORS
    before = (p + SECTORS - 1) % SECTORS
    across = (p + SECTORS // 2) % SECTORS
    barrier = pltpu.get_barrier_semaphore()
    greeted = [(after, g), (before, g)]
    greeted += [(block * GROUP + (me + k) % GROUP, g) for k in range(1, GROUP)]
    greeted += [(p, 1 - g)]
    hop = [((p + d) % SECTORS, g) for d in (2 * GROUP, SECTORS - 2 * GROUP, 4 * GROUP, SECTORS - 4 * GROUP)]
    side_block = (block + 1 - 2 * (block % 2)) * GROUP + me
    greeted += [*hop[:2], (side_block, g)]
    for who in greeted:
        pl.semaphore_signal(barrier, inc=1, device_id=who, device_id_type=MESH)

    def cols(t):
        return pl.ds(pl.multiple_of(t * LANES, LANES), LANES)

    reads[0].wait()

    def pack_axial(t, carry):
        for i in range(PTS // 4):
            x = [ext[2, REACH + 4 * i + j, :, cols(t)] for j in range(4)]
            for j, y in enumerate(pack4(x, sub)):
                esend[3 * i + j, :, cols(t)] = y
        return carry

    lax.fori_loop(0, TILES, pack_axial, 0)
    quarter = lane((8, LANES)) // RT
    for c in range(3):
        for i in range(PTS // 4):
            line = ext[c, REACH + 4 * i, :, :LANES]
            for j in range(1, 4):
                line = jnp.where(quarter == j, pltpu.roll(ext[c, REACH + 4 * i + j, :, :LANES], RT * j, 1), line)
            msend[c, i] = MIRROR_SIGNS[c] * line

    pl.semaphore_wait(barrier, len(greeted))

    def tell(stage, whom):
        for who in whom:
            pl.semaphore_signal(chain.at[stage], inc=1, device_id=who, device_id_type=MESH)

    tell(0, hop[:2])

    def remote(src, dst, s_sem, r_sem, who):
        return pltpu.make_async_remote_copy(
            src_ref=src, dst_ref=dst, send_sem=s_sem, recv_sem=r_sem, device_id=who, device_id_type=MESH
        )

    def pair(src, dst, sem, who):
        return remote(src, dst, sem.at[0], sem.at[1], who)

    planes_e = pair(esend, erecv, e_sem, (p, 1 - g))
    halo_up, halo_down = [], []
    for c in range(3):
        halo_up.append(
            remote(ext.at[c, pl.ds(PTS, REACH)], ext.at[c, pl.ds(0, REACH)], up_sem.at[0, c], up_sem.at[1, c], (after, g))
        )
        halo_down.append(
            remote(
                ext.at[c, pl.ds(REACH, REACH)], ext.at[c, pl.ds(REACH + PTS, REACH)],
                down_sem.at[0, c], down_sem.at[1, c], (before, g),
            )
        )
    next_block, last_block = (block + 1) % BLOCKS, (block + BLOCKS - 1) % BLOCKS
    halo_up_last, halo_down_last = ext.at[0, pl.ds(PTS, REACH)], ext.at[0, pl.ds(REACH, REACH)]
    to_relay = [
        pair(halo_up_last, passing, relay_in, (next_block * GROUP + RELAY[0], g)),
        pair(halo_down_last, passing, relay_in, (last_block * GROUP + RELAY[1], g)),
    ]
    relayed = [
        pair(passing, ext.at[0, pl.ds(0, REACH)], relay_out, (block * GROUP, g)),
        pair(passing, ext.at[0, pl.ds(REACH + PTS, REACH)], relay_out, (block * GROUP + GROUP - 1, g)),
    ]
    mirror = pair(msend, mrecv, mir_sem, (across, g))
    planes = [
        remote(gsend.at[c], grecv.at[c], g_sem.at[0, c], g_sem.at[1, c], (p, 1 - g)) for c in range(2)
    ]
    first, final = me == 0, me == GROUP - 1
    planes_e.start()
    halo_up[1].start()
    halo_down[1].start()

    @pl.when(me != GROUP - 1)
    def _():
        halo_up[0].start()
        halo_up[2].start()

    @pl.when(me != 0)
    def _():
        halo_down[0].start()
        halo_down[2].start()

    reads[2].wait()
    radius = lane((8, NR)).astype(F32) + 0.5
    inverse_r = 1.0 / radius
    coef = visc[0] * inverse_r * inverse_r
    half = 0.5 / coef
    gap = jnp.sqrt(half * (2.0 + half)) - half
    rho = 1.0 - gap
    scale = 1.0 / jnp.sqrt(1.0 + 4.0 * coef)
    gap16 = doubled(doubled(doubled(doubled(gap))))
    gap128 = doubled(doubled(doubled(gap16)))
    whole = doubled(doubled(doubled(doubled(gap128))))
    for t in range(TILES):
        here = slice(t * LANES, (t + 1) * LANES)
        inv_t[t] = inverse_r[:, here]
        scale_t[t] = scale[:, here]
        w_t[t] = 1.0 - gap16[:, here]
        big_t[t] = 1.0 - gap128[:, here]
        inv_n[t] = 1.0 / whole[:, here]
        power = jnp.ones((8, LANES), F32)
        for j in range(PTS + 1):
            pow_t[t, j] = power
            power = power * rho[:, here]

    pl.semaphore_wait(chain.at[0], 2)
    tell(1, hop[2:])

    def spread(t, carry):
        for c in range(3):
            for i in range(PTS // 4):
                far = []
                for j in range(4):
                    row = 4 * i + j
                    inside, outside = axial_parts(ext[c, REACH + row, :, cols(t)], sub)
                    own_ax[c, row, :, cols(t)] = inside
                    far_ax[c, row, :, cols(t)] = outside
                    far.append(outside)
                if c < 2:
                    for j, y in enumerate(pack4(far, sub)):
                        gsend[c, 3 * i + j, :, cols(t)] = y
        return carry

    lax.fori_loop(0, TILES, spread, 0)

    reads[1].wait()
    op_high, op_low = split(op_v[...])
    wh[...] = op_high
    wl[...] = op_low
    for c in range(3):
        lines = ext[c, pl.ds(REACH, PTS)].reshape(PTS * 8, NR)
        part[c] = dot3(lines, wh[pl.ds(0, NR)], wl[pl.ds(0, NR)]).reshape(PTS, 8, NR)

    pl.semaphore_wait(chain.at[1], 2)
    mirror.start()
    tell(2, [(side_block, g)])

    def azimuth(t, carry):
        inv = inv_t[t]
        for c in range(3):
            x = [ext[c, REACH + k, :, cols(t)] for k in range(PTS)]
            for row in range(PTS):
                grad = None
                for k in range(max(0, row - REACH), min(PTS, row + REACH + 1)):
                    tap = sten[k - row + REACH] * x[k]
                    grad = tap if grad is None else grad + tap
                a = ext[0, REACH + row, :, cols(t)]
                b = ext[1, REACH + row, :, cols(t)]
                e = ext[2, REACH + row, :, cols(t)]
                if c == 0:
                    grad = grad - b
                if c == 1:
                    grad = grad + a
                part[c, row, :, cols(t)] = (
                    a * part[c, row, :, cols(t)] + (b * inv) * grad + e * own_ax[c, row, :, cols(t)]
                )
        return carry

    lax.fori_loop(0, TILES, azimuth, 0)

    def local_sums(t, carry):
        rho = pow_t[t, 1]
        for c in range(3):
            ahead = back = None
            for row in range(PTS):
                right = ext[c, REACH + row, :, cols(t)] - STEP_WEIGHT * part[c, row, :, cols(t)]
                ahead = right if row == 0 else rho * ahead + right
                back = right if row == 0 else back + pow_t[t, row] * right
            fb[t, c] = ahead
            fb[TILES + t, c] = back
        return carry

    lax.fori_loop(0, TILES, local_sums, 0)

    @pl.when(final)
    def _():
        halo_down[1].wait_recv()
        to_relay[0].start()
        halo_up[2].start()

    @pl.when(first)
    def _():
        halo_up[1].wait_recv()
        to_relay[1].start()
        halo_down[2].start()

    planes_e.wait_recv()

    sums = []
    for turn in range(TILES):
        t = (my_tile + turn) % TILES
        rho = pow_t[t, 1]
        e = []
        for i in range(PTS // 4):
            e += unpack4([erecv[3 * i + j, :, cols(t)] for j in range(3)], sub)
        for c in range(3):
            ahead = back = None
            for row in range(PTS):
                x = e[row] * far_ax[c, row, :, cols(t)]
                ahead = x if row == 0 else rho * ahead + x
                back = x if row == 0 else back + pow_t[t, row] * x
            ssend[t, c] = -STEP_WEIGHT * ahead
            ssend[TILES + t, c] = -STEP_WEIGHT * back
        for k in (t, TILES + t):
            cp = remote(
                ssend.at[k], sum_in.at[me], v_s.at[len(sums)], v_r.at[0], (block * GROUP + k, 1 - g)
            )
            cp.start()
            sums.append(cp)

    def halo_taps(t, c, row, shift):
        span = range(row, REACH) if shift[0] == 0 else range(REACH + PTS, row + 2 * REACH + 1)
        grad = None
        for k in span:
            tap = sten[k - row] * ext[c, k + shift[1], :, cols(t)]
            grad = tap if grad is None else grad + tap
        return grad

    def edge_sums(side):
        shift = (side, PTS if side == 0 else -PTS)
        theirs = REACH + PTS if side == 0 else REACH - PTS

        def body(t, carry):
            inv, rho = inv_t[t], pow_t[t, 1]
            for c in range(3):
                ahead = back = None
                for row in ROWS[side]:
                    x = (ext[1, row + theirs, :, cols(t)] * inv) * halo_taps(t, c, row, shift)
                    ahead = x if ahead is None else rho * ahead + x
                    x = pow_t[t, row] * x
                    back = x if back is None else back + x
                if side == 0:
                    ahead = ahead * pow_t[t, PTS - REACH]
                hsend[t, c] = -STEP_WEIGHT * ahead
                hsend[TILES + t, c] = -STEP_WEIGHT * back
            return carry

        lax.fori_loop(0, TILES, body, 0)

    def edge_copies(side):
        to = (block + 1) % BLOCKS if side == 0 else (block + BLOCKS - 1) % BLOCKS
        return [
            remote(hsend.at[k], halo_in.at[side], h_s.at[k], h_r.at[side], (to * GROUP + k, g)) for k in range(GROUP)
        ]

    edge = [edge_copies(0), edge_copies(1)]

    @pl.when(final)
    def _():
        edge_sums(0)
        for cp in edge[0]:
            cp.start()

    @pl.when(first)
    def _():
        edge_sums(1)
        for cp in edge[1]:
            cp.start()

    for cp in planes:
        cp.start()

    def add_halo(side, summed):
        def body(t, carry):
            inv, rho = inv_t[t], pow_t[t, 1]
            for c in range(3):
                ahead = back = None
                for row in ROWS[side]:
                    x = (ext[1, REACH + row, :, cols(t)] * inv) * halo_taps(t, c, row, (side, 0))
                    part[c, row, :, cols(t)] = part[c, row, :, cols(t)] + x
                    if summed:
                        ahead = x if ahead is None else rho * ahead + x
                        x = pow_t[t, row] * x
                        back = x if back is None else back + x
                if summed:
                    if side == 0:
                        ahead = ahead * pow_t[t, PTS - REACH]
                    fb[t, c] = fb[t, c] - STEP_WEIGHT * ahead
                    fb[TILES + t, c] = fb[TILES + t, c] - STEP_WEIGHT * back
            return carry

        lax.fori_loop(0, TILES, body, 0)

    @pl.when(me != 0)
    def _():
        for cp in (halo_up[1], halo_up[0], halo_up[2]):
            cp.wait_recv()
        add_halo(0, True)

    @pl.when(me != GROUP - 1)
    def _():
        for cp in (halo_down[1], halo_down[0], halo_down[2]):
            cp.wait_recv()
        add_halo(1, True)

    mirror.wait_recv()
    for i in range(PTS // 4):
        lines = []
        for c in range(3):
            packed = mrecv[c, i]
            lines += [packed[:, :RT]] + [pltpu.roll(packed, LANES - RT * j, 1)[:, :RT] for j in range(1, 4)]
        more = dot3(jnp.concatenate(lines, axis=0), wh[pl.ds(NR, RT)], wl[pl.ds(NR, RT)]).reshape(3, 4, 8, NR)
        for t in range(TILES):
            here = slice(t * LANES, (t + 1) * LANES)
            for c in range(3):
                ahead, back = fb[t, c], fb[TILES + t, c]
                for j in range(4):
                    row = 4 * i + j
                    x = ext[0, REACH + row, :, here] * more[c, j, :, here]
                    part[c, row, :, here] = part[c, row, :, here] + x
                    x = -STEP_WEIGHT * x
                    ahead = ahead + pow_t[t, PTS - 1 - row] * x
                    back = back + pow_t[t, row] * x
                fb[t, c] = ahead
                fb[TILES + t, c] = back

    one, two, three = [], [], []
    for k in sorted(range(1, GROUP), key=lambda k: abs(k - GROUP // 2)):
        other = (me + k) % GROUP
        cp = remote(fb.at[other], up_in.at[me], p1_s.at[k - 1], p1_r.at[k - 1], (block * GROUP + other, g))
        cp.start()
        one.append(cp)
    up_in[me] = fb[me]

    def finish_term(c):
        def body(t, carry):
            rho = pow_t[t, 1]
            right = []
            left = []
            for i in range(PTS // 4):
                if c < 2:
                    far = unpack4([grecv[c, 3 * i + j, :, cols(t)] for j in range(3)], sub)
                else:
                    far = unpack4([erecv[3 * i + j, :, cols(t)] for j in range(3)], sub)
                for j in range(4):
                    row = 4 * i + j
                    grad = far[j]
                    if c == 2:
                        grad = axial_parts(grad, sub)[1]
                    else:
                        grad = jnp.where((sub == 3) | (sub == 4), 0.0, grad)
                    term = part[c, row, :, cols(t)] + ext[2, REACH + row, :, cols(t)] * grad
                    part[c, row, :, cols(t)] = term
                    right.append(ext[c, REACH + row, :, cols(t)] - STEP_WEIGHT * term)
                    left.append(right[row] if row == 0 else right[row] + rho * left[row - 1])
            run = None
            for row in range(PTS - 1, -1, -1):
                if run is None:
                    loc[c, row, :, cols(t)] = left[row]
                    run = right[row]
                else:
                    run = rho * run
                    loc[c, row, :, cols(t)] = left[row] + run
                    run = right[row] + run
            return carry

        lax.fori_loop(0, TILES, body, 0)

    def entry(k):
        return k + backward * (GROUP - 1 - 2 * k)

    pl.semaphore_wait(chain.at[2], 1)
    for cp in (*one, edge[0][0], edge[1][0]):
        cp.wait_recv()
    remote(ssend, sum_in, v_s.at[0], v_r.at[0], (p, 1 - g)).wait_recv()
    for k in range(GROUP):
        total = up_in[k] + sum_in[k]
        if k == 0:
            total = total + halo_in[0]
        if k == GROUP - 1:
            total = total + halo_in[1]
        up_in[k] = total
    w = w_t[my_tile]
    run = up_in[entry(0)]
    for k in range(1, GROUP):
        run = up_in[entry(k)] + w * run
    tot[block] = run
    for k in sorted(range(1, BLOCKS), key=lambda k: abs(k - BLOCKS // 2)):
        cp = remote(
            tot.at[block], tot.at[block], p2_s.at[k - 1], p2_r.at[k - 1],
            (((block + k) % BLOCKS) * GROUP + me, g),
        )
        cp.start()
        two.append(cp)


    for side in range(2):

        @pl.when(me == RELAY[side])
        def _(side=side):
            to_relay[side].wait_recv()
            relayed[side].start()

    for cp in two:
        cp.wait_recv()
    big = big_t[my_tile]
    run = tot[block]
    for m in range(BLOCKS - 1, 0, -1):
        run = tot[(block + (2 * backward - 1) * m + BLOCKS) % BLOCKS] + big * run
    run = run * inv_n[my_tile]
    for k in range(GROUP):
        ret[entry(k)] = run
        run = up_in[entry(k)] + w * run
    for k in sorted(range(1, GROUP), key=lambda k: abs(k - GROUP // 2)):
        other = (me + k) % GROUP
        cp = remote(ret.at[other], car.at[me], p3_s.at[k - 1], p3_r.at[k - 1], (block * GROUP + other, g))
        cp.start()
        three.append(cp)
    car[me] = ret[me]

    @pl.when(first)
    def _():
        relayed[0].wait_recv()
        halo_up[2].wait_recv()
        add_halo(0, False)

    @pl.when(final)
    def _():
        relayed[1].wait_recv()
        halo_down[2].wait_recv()
        add_halo(1, False)

    finish_term(2)
    for c in range(2):
        planes[c].wait_recv()
        finish_term(c)

    for cp in three:
        cp.wait_recv()

    for t in range(TILES):
        ends[t] = scale_t[t] * car[t]
        ends[TILES + t] = scale_t[t] * car[TILES + t]
    for cp in (planes_e, *halo_up[1:], *halo_down[1:], mirror, *sums, *planes, *one, *two, *three):
        cp.wait_send()

    @pl.when(me != GROUP - 1)
    def _():
        halo_up[0].wait_send()

    @pl.when(me != 0)
    def _():
        halo_down[0].wait_send()

    for side in range(2):

        @pl.when(me == RELAY[side])
        def _(side=side):
            relayed[side].wait_send()

    for side, here in ((0, final), (1, first)):

        @pl.when(here)
        def _(side=side):
            for cp in (*edge[side], to_relay[side]):
                cp.wait_send()


def write_out(loc, part, ends, pow_t, scale_t, new_out, non_out, new, sem):
    def copy(src, dst, k, c):
        cp = pltpu.make_async_copy(src.at[c], dst.at[c], sem.at[k, c])
        cp.start()
        return cp

    copies = [copy(part, non_out, 1, c) for c in range(3)]
    for c in range(3):
        for t in range(TILES):
            here = slice(t * LANES, (t + 1) * LANES)
            for row in range(PTS):
                new[c, row, :, here] = (
                    scale_t[t] * loc[c, row, :, here]
                    + pow_t[t, row + 1] * ends[t, c]
                    + pow_t[t, PTS - row] * ends[TILES + t, c]
                )
        copies.append(copy(new, new_out, 0, c))
    for cp in copies:
        cp.wait()


def local(velocity, radial_op, azimuth_stencil, viscous_factor):
    dma = pltpu.SemaphoreType.DMA
    block = velocity.shape
    any_space = pl.BlockSpec(memory_space=pl.ANY)
    in_place = [
        pltpu.with_memory_space_constraint(x, pltpu.HBM) for x in (velocity, radial_op.T, azimuth_stencil)
    ]
    tile = (8, LANES)
    kept = tuple(
        jax.ShapeDtypeStruct(shape, F32)
        for shape in (block, block, (GROUP, 3, *tile), (TILES, PTS + 1, *tile), (TILES, *tile))
    )
    outs = pl.pallas_call(
        kernel,
        name="substep",
        out_shape=kept,
        in_specs=[any_space] * 3 + [pl.BlockSpec(memory_space=pltpu.SMEM)],
        out_specs=(pl.BlockSpec(memory_space=pltpu.VMEM),) * len(kept),
        scratch_shapes=[
            pltpu.SMEM((2 * REACH + 1,), F32),
            pltpu.VMEM((3, PTS + 2 * REACH, 8, NR), F32),
            pltpu.VMEM((NR + RT, NR), F32),
            pltpu.VMEM((NR + RT, NR), BF16),
            pltpu.VMEM((NR + RT, NR), BF16),
            pltpu.VMEM((12, 8, NR), F32),
            pltpu.VMEM((12, 8, NR), F32),
            pltpu.VMEM((2, 12, 8, NR), F32),
            pltpu.VMEM((2, 12, 8, NR), F32),
            pltpu.VMEM((3, 4, *tile), F32),
            pltpu.VMEM((3, 4, *tile), F32),
            pltpu.VMEM(block, F32),
            pltpu.VMEM(block, F32),
            pltpu.VMEM((TILES, *tile), F32),
            pltpu.VMEM((TILES, *tile), F32),
            pltpu.VMEM((TILES, *tile), F32),
            pltpu.VMEM((TILES, *tile), F32),
            pltpu.VMEM((GROUP, 3, *tile), F32),
            pltpu.VMEM((GROUP, 3, *tile), F32),
            pltpu.VMEM((GROUP, 3, *tile), F32),
            pltpu.VMEM((2, 3, *tile), F32),
            pltpu.VMEM((GROUP, 3, *tile), F32),
            pltpu.VMEM((GROUP, 3, *tile), F32),
            pltpu.VMEM((GROUP, 3, *tile), F32),
            pltpu.VMEM((BLOCKS, 3, *tile), F32),
            pltpu.VMEM((GROUP, 3, *tile), F32),
            dma((4,)),
            dma((2,)), dma((2,)), dma((2, 3)), dma((2, 3)),
            dma((2, 2)), dma((GROUP,)), dma((1,)), dma((GROUP,)), dma((2,)),
            dma((GROUP - 1,)), dma((GROUP - 1,)),
            dma((BLOCKS - 1,)), dma((BLOCKS - 1,)),
            dma((GROUP - 1,)), dma((GROUP - 1,)),
            dma((2,)), dma((2,)),
            pltpu.VMEM((REACH, 8, NR), F32),
            pltpu.SemaphoreType.REGULAR((3,)),
        ],
        compiler_params=pltpu.CompilerParams(
            collective_id=0, has_side_effects=True, vmem_limit_bytes=40 << 20
        ),
    )(*in_place, viscous_factor)
    return pl.pallas_call(
        write_out,
        name="write_out",
        out_shape=(pltpu.HBM(block, F32), pltpu.HBM(block, F32)),
        in_specs=[pl.BlockSpec(memory_space=pltpu.VMEM)] * len(kept),
        out_specs=(any_space, any_space),
        scratch_shapes=[pltpu.VMEM(block, F32), dma((2, 3))],
    )(*[pltpu.with_memory_space_constraint(x, pltpu.VMEM) for x in outs])


def solution(mesh):
    spec = P(None, "theta", "gz", None)
    return jax.shard_map(
        local, mesh=mesh, in_specs=(spec, P(), P(), P()), out_specs=(spec, spec), check_vma=False
    )
```

```python
import jax
import jax.numpy as jnp
from jax import lax
from jax.experimental import pallas as pl
from jax.experimental.pallas import tpu as pltpu
from jax.sharding import PartitionSpec as P

AXIAL_WEIGHTS = (0.75, -0.15, 1.0 / 60.0)
STEP_WEIGHT = 0.2
MIRROR_SIGNS = (-1.0, -1.0, 1.0)
MESH = pl.DeviceIdType.MESH
F32 = jnp.float32
BF16 = jnp.bfloat16
REACH = 10
PTS = 16
NR = 512
RT = 32
LANES = 128
TILES = NR // LANES
GROUP = 8
SECTORS = 128
BLOCKS = SECTORS // GROUP
ROWS = (range(0, REACH), range(PTS - REACH, PTS))
RELAY = (5, 2)
PLAIN_DOT = (((1,), (0,)), ((), ()))


def split(x):
    high = x.astype(BF16)
    return high, (x - high.astype(F32)).astype(BF16)


def dot3(x, w_high, w_low):
    high, low = split(x)
    out = lax.dot_general(high, w_low, PLAIN_DOT, preferred_element_type=F32)
    out = out + lax.dot_general(low, w_high, PLAIN_DOT, preferred_element_type=F32)
    return out + lax.dot_general(high, w_high, PLAIN_DOT, preferred_element_type=F32)


def rows_of(shape):
    return lax.broadcasted_iota(jnp.int32, shape, len(shape) - 2)


def lane(shape):
    return lax.broadcasted_iota(jnp.int32, shape, len(shape) - 1)


def doubled(q):
    return q * (2.0 - q)


def pack4(x, sub):
    middle = (sub == 3) | (sub == 4)
    return (
        jnp.where(middle, pltpu.roll(x[3], 3, 0), x[0]),
        jnp.where(sub == 3, pltpu.roll(x[3], 1, 0), jnp.where(sub == 4, pltpu.roll(x[3], 7, 0), x[1])),
        jnp.where(middle, pltpu.roll(x[3], 5, 0), x[2]),
    )


def unpack4(y, sub):
    fourth = jnp.where(
        sub < 2,
        pltpu.roll(y[0], 5, 0),
        jnp.where(
            sub == 2,
            pltpu.roll(y[1], 7, 0),
            jnp.where(sub == 5, pltpu.roll(y[1], 1, 0), pltpu.roll(y[2], 3, 0)),
        ),
    )
    return (y[0], y[1], y[2], fourth)


def axial_parts(x, sub):
    own = far = None
    for m, weight in enumerate(AXIAL_WEIGHTS, 1):
        upper = weight * pltpu.roll(x, 8 - m, 0)
        lower = weight * pltpu.roll(x, m, 0)
        inside = jnp.where(sub < 8 - m, upper, 0.0) - jnp.where(sub >= m, lower, 0.0)
        outside = jnp.where(sub < 8 - m, 0.0, upper) - jnp.where(sub >= m, 0.0, lower)
        own = inside if own is None else own + inside
        far = outside if far is None else far + outside
    return own, far


def kernel(
    v_hbm, op_hbm, sten_hbm, visc, loc, part, ends, pow_t, scale_t,
    sten,
    ext, op_v, wh, wl, esend, erecv, gsend, grecv, msend, mrecv, own_ax, far_ax,
    inv_t, w_t, big_t, inv_n, ssend, sum_in, hsend, halo_in, fb, up_in, ret, tot, car,
    in_sem, e_sem, mir_sem, up_sem, down_sem, g_sem, v_s, v_r, h_s, h_r,
    p1_s, p1_r, p2_s, p2_r, p3_s, p3_r, relay_in, relay_out, passing, chain,
):
    p = lax.axis_index("theta")
    g = lax.axis_index("gz")
    me = p % GROUP
    block = p // GROUP
    backward = me // TILES
    my_tile = me % TILES
    sub = rows_of((8, LANES))

    reads = [
        pltpu.make_async_copy(v_hbm, ext.at[:, pl.ds(REACH, PTS)], in_sem.at[0]),
        pltpu.make_async_copy(op_hbm, op_v, in_sem.at[1]),
        pltpu.make_async_copy(sten_hbm, sten, in_sem.at[2]),
    ]
    for r in reads:
        r.start()

    after = (p + 1) % SECTORS
    before = (p + SECTORS - 1) % SECTORS
    across = (p + SECTORS // 2) % SECTORS
    barrier = pltpu.get_barrier_semaphore()
    greeted = [(after, g), (before, g)]
    greeted += [(block * GROUP + (me + k) % GROUP, g) for k in range(1, GROUP)]
    greeted += [(p, 1 - g)]
    hop = [((p + d) % SECTORS, g) for d in (2 * GROUP, SECTORS - 2 * GROUP, 4 * GROUP, SECTORS - 4 * GROUP)]
    side_block = (block + 1 - 2 * (block % 2)) * GROUP + me
    greeted += [*hop[:2], (side_block, g)]
    for who in greeted:
        pl.semaphore_signal(barrier, inc=1, device_id=who, device_id_type=MESH)

    def cols(t):
        return pl.ds(pl.multiple_of(t * LANES, LANES), LANES)

    reads[0].wait()

    def pack_axial(t, carry):
        for i in range(PTS // 4):
            x = [ext[2, REACH + 4 * i + j, :, cols(t)] for j in range(4)]
            for j, y in enumerate(pack4(x, sub)):
                esend[3 * i + j, :, cols(t)] = y
        return carry

    lax.fori_loop(0, TILES, pack_axial, 0)
    quarter = lane((8, LANES)) // RT
    for c in range(3):
        for i in range(PTS // 4):
            line = ext[c, REACH + 4 * i, :, :LANES]
            for j in range(1, 4):
                line = jnp.where(quarter == j, pltpu.roll(ext[c, REACH + 4 * i + j, :, :LANES], RT * j, 1), line)
            msend[c, i] = MIRROR_SIGNS[c] * line

    pl.semaphore_wait(barrier, len(greeted))

    def tell(stage, whom):
        for who in whom:
            pl.semaphore_signal(chain.at[stage], inc=1, device_id=who, device_id_type=MESH)

    tell(0, hop[:2])

    def remote(src, dst, s_sem, r_sem, who):
        return pltpu.make_async_remote_copy(
            src_ref=src, dst_ref=dst, send_sem=s_sem, recv_sem=r_sem, device_id=who, device_id_type=MESH
        )

    def pair(src, dst, sem, who):
        return remote(src, dst, sem.at[0], sem.at[1], who)

    planes_e = pair(esend, erecv, e_sem, (p, 1 - g))
    halo_up, halo_down = [], []
    for c in range(3):
        halo_up.append(
            remote(ext.at[c, pl.ds(PTS, REACH)], ext.at[c, pl.ds(0, REACH)], up_sem.at[0, c], up_sem.at[1, c], (after, g))
        )
        halo_down.append(
            remote(
                ext.at[c, pl.ds(REACH, REACH)], ext.at[c, pl.ds(REACH + PTS, REACH)],
                down_sem.at[0, c], down_sem.at[1, c], (before, g),
            )
        )
    next_block, last_block = (block + 1) % BLOCKS, (block + BLOCKS - 1) % BLOCKS
    halo_up_last, halo_down_last = ext.at[0, pl.ds(PTS, REACH)], ext.at[0, pl.ds(REACH, REACH)]
    to_relay = [
        pair(halo_up_last, passing, relay_in, (next_block * GROUP + RELAY[0], g)),
        pair(halo_down_last, passing, relay_in, (last_block * GROUP + RELAY[1], g)),
    ]
    relayed = [
        pair(passing, ext.at[0, pl.ds(0, REACH)], relay_out, (block * GROUP, g)),
        pair(passing, ext.at[0, pl.ds(REACH + PTS, REACH)], relay_out, (block * GROUP + GROUP - 1, g)),
    ]
    mirror = pair(msend, mrecv, mir_sem, (across, g))
    planes = [
        remote(gsend.at[c], grecv.at[c], g_sem.at[0, c], g_sem.at[1, c], (p, 1 - g)) for c in range(2)
    ]
    first, final = me == 0, me == GROUP - 1
    planes_e.start()
    halo_up[1].start()
    halo_down[1].start()

    @pl.when(me != GROUP - 1)
    def _():
        halo_up[0].start()
        halo_up[2].start()

    @pl.when(me != 0)
    def _():
        halo_down[0].start()
        halo_down[2].start()

    reads[2].wait()
    radius = lane((8, NR)).astype(F32) + 0.5
    inverse_r = 1.0 / radius
    coef = visc[0] * inverse_r * inverse_r
    half = 0.5 / coef
    gap = jnp.sqrt(half * (2.0 + half)) - half
    rho = 1.0 - gap
    scale = 1.0 / jnp.sqrt(1.0 + 4.0 * coef)
    gap16 = doubled(doubled(doubled(doubled(gap))))
    gap128 = doubled(doubled(doubled(gap16)))
    whole = doubled(doubled(doubled(doubled(gap128))))
    for t in range(TILES):
        here = slice(t * LANES, (t + 1) * LANES)
        inv_t[t] = inverse_r[:, here]
        scale_t[t] = scale[:, here]
        w_t[t] = 1.0 - gap16[:, here]
        big_t[t] = 1.0 - gap128[:, here]
        inv_n[t] = 1.0 / whole[:, here]
        power = jnp.ones((8, LANES), F32)
        for j in range(PTS + 1):
            pow_t[t, j] = power
            power = power * rho[:, here]

    pl.semaphore_wait(chain.at[0], 2)
    tell(1, hop[2:])

    def spread(t, carry):
        for c in range(3):
            for i in range(PTS // 4):
                far = []
                for j in range(4):
                    row = 4 * i + j
                    inside, outside = axial_parts(ext[c, REACH + row, :, cols(t)], sub)
                    own_ax[c, row, :, cols(t)] = inside
                    far_ax[c, row, :, cols(t)] = outside
                    far.append(outside)
                if c < 2:
                    for j, y in enumerate(pack4(far, sub)):
                        gsend[c, 3 * i + j, :, cols(t)] = y
        return carry

    lax.fori_loop(0, TILES, spread, 0)

    reads[1].wait()
    op_high, op_low = split(op_v[...])
    wh[...] = op_high
    wl[...] = op_low
    for c in range(3):
        lines = ext[c, pl.ds(REACH, PTS)].reshape(PTS * 8, NR)
        part[c] = dot3(lines, wh[pl.ds(0, NR)], wl[pl.ds(0, NR)]).reshape(PTS, 8, NR)

    pl.semaphore_wait(chain.at[1], 2)
    mirror.start()
    tell(2, [(side_block, g)])

    def azimuth(t, carry):
        inv = inv_t[t]
        for c in range(3):
            x = [ext[c, REACH + k, :, cols(t)] for k in range(PTS)]
            for row in range(PTS):
                grad = None
                for k in range(max(0, row - REACH), min(PTS, row + REACH + 1)):
                    tap = sten[k - row + REACH] * x[k]
                    grad = tap if grad is None else grad + tap
                a = ext[0, REACH + row, :, cols(t)]
                b = ext[1, REACH + row, :, cols(t)]
                e = ext[2, REACH + row, :, cols(t)]
                if c == 0:
                    grad = grad - b
                if c == 1:
                    grad = grad + a
                part[c, row, :, cols(t)] = (
                    a * part[c, row, :, cols(t)] + (b * inv) * grad + e * own_ax[c, row, :, cols(t)]
                )
        return carry

    lax.fori_loop(0, TILES, azimuth, 0)

    def local_sums(t, carry):
        rho = pow_t[t, 1]
        for c in range(3):
            ahead = back = None
            for row in range(PTS):
                right = ext[c, REACH + row, :, cols(t)] - STEP_WEIGHT * part[c, row, :, cols(t)]
                ahead = right if row == 0 else rho * ahead + right
                back = right if row == 0 else back + pow_t[t, row] * right
            fb[t, c] = ahead
            fb[TILES + t, c] = back
        return carry

    lax.fori_loop(0, TILES, local_sums, 0)

    @pl.when(final)
    def _():
        halo_down[1].wait_recv()
        to_relay[0].start()
        halo_up[2].start()

    @pl.when(first)
    def _():
        halo_up[1].wait_recv()
        to_relay[1].start()
        halo_down[2].start()

    planes_e.wait_recv()

    sums = []
    for turn in range(TILES):
        t = (my_tile + turn) % TILES
        rho = pow_t[t, 1]
        e = []
        for i in range(PTS // 4):
            e += unpack4([erecv[3 * i + j, :, cols(t)] for j in range(3)], sub)
        for c in range(3):
            ahead = back = None
            for row in range(PTS):
                x = e[row] * far_ax[c, row, :, cols(t)]
                ahead = x if row == 0 else rho * ahead + x
                back = x if row == 0 else back + pow_t[t, row] * x
            ssend[t, c] = -STEP_WEIGHT * ahead
            ssend[TILES + t, c] = -STEP_WEIGHT * back
        for k in (t, TILES + t):
            cp = remote(
                ssend.at[k], sum_in.at[me], v_s.at[len(sums)], v_r.at[0], (block * GROUP + k, 1 - g)
            )
            cp.start()
            sums.append(cp)

    def halo_taps(t, c, row, shift):
        span = range(row, REACH) if shift[0] == 0 else range(REACH + PTS, row + 2 * REACH + 1)
        grad = None
        for k in span:
            tap = sten[k - row] * ext[c, k + shift[1], :, cols(t)]
            grad = tap if grad is None else grad + tap
        return grad

    def edge_sums(side):
        shift = (side, PTS if side == 0 else -PTS)
        theirs = REACH + PTS if side == 0 else REACH - PTS

        def body(t, carry):
            inv, rho = inv_t[t], pow_t[t, 1]
            for c in range(3):
                ahead = back = None
                for row in ROWS[side]:
                    x = (ext[1, row + theirs, :, cols(t)] * inv) * halo_taps(t, c, row, shift)
                    ahead = x if ahead is None else rho * ahead + x
                    x = pow_t[t, row] * x
                    back = x if back is None else back + x
                if side == 0:
                    ahead = ahead * pow_t[t, PTS - REACH]
                hsend[t, c] = -STEP_WEIGHT * ahead
                hsend[TILES + t, c] = -STEP_WEIGHT * back
            return carry

        lax.fori_loop(0, TILES, body, 0)

    def edge_copies(side):
        to = (block + 1) % BLOCKS if side == 0 else (block + BLOCKS - 1) % BLOCKS
        return [
            remote(hsend.at[k], halo_in.at[side], h_s.at[k], h_r.at[side], (to * GROUP + k, g)) for k in range(GROUP)
        ]

    edge = [edge_copies(0), edge_copies(1)]

    @pl.when(final)
    def _():
        edge_sums(0)
        for cp in edge[0]:
            cp.start()

    @pl.when(first)
    def _():
        edge_sums(1)
        for cp in edge[1]:
            cp.start()

    planes[0].start()

    def add_halo(side, summed):
        def body(t, carry):
            inv, rho = inv_t[t], pow_t[t, 1]
            for c in range(3):
                ahead = back = None
                for row in ROWS[side]:
                    x = (ext[1, REACH + row, :, cols(t)] * inv) * halo_taps(t, c, row, (side, 0))
                    part[c, row, :, cols(t)] = part[c, row, :, cols(t)] + x
                    if summed:
                        ahead = x if ahead is None else rho * ahead + x
                        x = pow_t[t, row] * x
                        back = x if back is None else back + x
                if summed:
                    if side == 0:
                        ahead = ahead * pow_t[t, PTS - REACH]
                    fb[t, c] = fb[t, c] - STEP_WEIGHT * ahead
                    fb[TILES + t, c] = fb[TILES + t, c] - STEP_WEIGHT * back
            return carry

        lax.fori_loop(0, TILES, body, 0)

    @pl.when(me != 0)
    def _():
        for cp in (halo_up[1], halo_up[0], halo_up[2]):
            cp.wait_recv()
        add_halo(0, True)

    @pl.when(me != GROUP - 1)
    def _():
        for cp in (halo_down[1], halo_down[0], halo_down[2]):
            cp.wait_recv()
        add_halo(1, True)

    mirror.wait_recv()
    for i in range(PTS // 4):
        lines = []
        for c in range(3):
            packed = mrecv[c, i]
            lines += [packed[:, :RT]] + [pltpu.roll(packed, LANES - RT * j, 1)[:, :RT] for j in range(1, 4)]
        more = dot3(jnp.concatenate(lines, axis=0), wh[pl.ds(NR, RT)], wl[pl.ds(NR, RT)]).reshape(3, 4, 8, NR)
        for t in range(TILES):
            here = slice(t * LANES, (t + 1) * LANES)
            for c in range(3):
                ahead, back = fb[t, c], fb[TILES + t, c]
                for j in range(4):
                    row = 4 * i + j
                    x = ext[0, REACH + row, :, here] * more[c, j, :, here]
                    part[c, row, :, here] = part[c, row, :, here] + x
                    x = -STEP_WEIGHT * x
                    ahead = ahead + pow_t[t, PTS - 1 - row] * x
                    back = back + pow_t[t, row] * x
                fb[t, c] = ahead
                fb[TILES + t, c] = back

    one, two, three = [], [], []
    for k in sorted(range(1, GROUP), key=lambda k: abs(k - GROUP // 2)):
        other = (me + k) % GROUP
        cp = remote(fb.at[other], up_in.at[me], p1_s.at[k - 1], p1_r.at[k - 1], (block * GROUP + other, g))
        cp.start()
        one.append(cp)
    up_in[me] = fb[me]

    def finish_term(c):
        def body(t, carry):
            rho = pow_t[t, 1]
            right = []
            left = []
            for i in range(PTS // 4):
                if c < 2:
                    far = unpack4([grecv[c, 3 * i + j, :, cols(t)] for j in range(3)], sub)
                else:
                    far = unpack4([erecv[3 * i + j, :, cols(t)] for j in range(3)], sub)
                for j in range(4):
                    row = 4 * i + j
                    grad = far[j]
                    if c == 2:
                        grad = axial_parts(grad, sub)[1]
                    else:
                        grad = jnp.where((sub == 3) | (sub == 4), 0.0, grad)
                    term = part[c, row, :, cols(t)] + ext[2, REACH + row, :, cols(t)] * grad
                    part[c, row, :, cols(t)] = term
                    right.append(ext[c, REACH + row, :, cols(t)] - STEP_WEIGHT * term)
                    left.append(right[row] if row == 0 else right[row] + rho * left[row - 1])
            run = None
            for row in range(PTS - 1, -1, -1):
                if run is None:
                    loc[c, row, :, cols(t)] = left[row]
                    run = right[row]
                else:
                    run = rho * run
                    loc[c, row, :, cols(t)] = left[row] + run
                    run = right[row] + run
            return carry

        lax.fori_loop(0, TILES, body, 0)

    def entry(k):
        return k + backward * (GROUP - 1 - 2 * k)

    pl.semaphore_wait(chain.at[2], 1)
    for cp in (*one, edge[0][0], edge[1][0]):
        cp.wait_recv()
    remote(ssend, sum_in, v_s.at[0], v_r.at[0], (p, 1 - g)).wait_recv()
    for k in range(GROUP):
        total = up_in[k] + sum_in[k]
        if k == 0:
            total = total + halo_in[0]
        if k == GROUP - 1:
            total = total + halo_in[1]
        up_in[k] = total
    w = w_t[my_tile]
    run = up_in[entry(0)]
    for k in range(1, GROUP):
        run = up_in[entry(k)] + w * run
    tot[block] = run
    for k in sorted(range(1, BLOCKS), key=lambda k: abs(k - BLOCKS // 2)):
        cp = remote(
            tot.at[block], tot.at[block], p2_s.at[k - 1], p2_r.at[k - 1],
            (((block + k) % BLOCKS) * GROUP + me, g),
        )
        cp.start()
        two.append(cp)
    planes[1].start()


    for side in range(2):

        @pl.when(me == RELAY[side])
        def _(side=side):
            to_relay[side].wait_recv()
            relayed[side].start()

    for cp in two:
        cp.wait_recv()
    big = big_t[my_tile]
    run = tot[block]
    for m in range(BLOCKS - 1, 0, -1):
        run = tot[(block + (2 * backward - 1) * m + BLOCKS) % BLOCKS] + big * run
    run = run * inv_n[my_tile]
    for k in range(GROUP):
        ret[entry(k)] = run
        run = up_in[entry(k)] + w * run
    for k in sorted(range(1, GROUP), key=lambda k: abs(k - GROUP // 2)):
        other = (me + k) % GROUP
        cp = remote(ret.at[other], car.at[me], p3_s.at[k - 1], p3_r.at[k - 1], (block * GROUP + other, g))
        cp.start()
        three.append(cp)
    car[me] = ret[me]

    @pl.when(first)
    def _():
        relayed[0].wait_recv()
        halo_up[2].wait_recv()
        add_halo(0, False)

    @pl.when(final)
    def _():
        relayed[1].wait_recv()
        halo_down[2].wait_recv()
        add_halo(1, False)

    finish_term(2)
    for c in range(2):
        planes[c].wait_recv()
        finish_term(c)

    for cp in three:
        cp.wait_recv()

    for t in range(TILES):
        ends[t] = scale_t[t] * car[t]
        ends[TILES + t] = scale_t[t] * car[TILES + t]
    for cp in (planes_e, *halo_up[1:], *halo_down[1:], mirror, *sums, *planes, *one, *two, *three):
        cp.wait_send()

    @pl.when(me != GROUP - 1)
    def _():
        halo_up[0].wait_send()

    @pl.when(me != 0)
    def _():
        halo_down[0].wait_send()

    for side in range(2):

        @pl.when(me == RELAY[side])
        def _(side=side):
            relayed[side].wait_send()

    for side, here in ((0, final), (1, first)):

        @pl.when(here)
        def _(side=side):
            for cp in (*edge[side], to_relay[side]):
                cp.wait_send()


def write_out(loc, part, ends, pow_t, scale_t, new_out, non_out, new, sem):
    def copy(src, dst, k, c):
        cp = pltpu.make_async_copy(src.at[c], dst.at[c], sem.at[k, c])
        cp.start()
        return cp

    copies = [copy(part, non_out, 1, c) for c in range(3)]
    for c in range(3):
        for t in range(TILES):
            here = slice(t * LANES, (t + 1) * LANES)
            for row in range(PTS):
                new[c, row, :, here] = (
                    scale_t[t] * loc[c, row, :, here]
                    + pow_t[t, row + 1] * ends[t, c]
                    + pow_t[t, PTS - row] * ends[TILES + t, c]
                )
        copies.append(copy(new, new_out, 0, c))
    for cp in copies:
        cp.wait()


def local(velocity, radial_op, azimuth_stencil, viscous_factor):
    dma = pltpu.SemaphoreType.DMA
    block = velocity.shape
    any_space = pl.BlockSpec(memory_space=pl.ANY)
    in_place = [
        pltpu.with_memory_space_constraint(x, pltpu.HBM) for x in (velocity, radial_op.T, azimuth_stencil)
    ]
    tile = (8, LANES)
    kept = tuple(
        jax.ShapeDtypeStruct(shape, F32)
        for shape in (block, block, (GROUP, 3, *tile), (TILES, PTS + 1, *tile), (TILES, *tile))
    )
    outs = pl.pallas_call(
        kernel,
        name="substep",
        out_shape=kept,
        in_specs=[any_space] * 3 + [pl.BlockSpec(memory_space=pltpu.SMEM)],
        out_specs=(pl.BlockSpec(memory_space=pltpu.VMEM),) * len(kept),
        scratch_shapes=[
            pltpu.SMEM((2 * REACH + 1,), F32),
            pltpu.VMEM((3, PTS + 2 * REACH, 8, NR), F32),
            pltpu.VMEM((NR + RT, NR), F32),
            pltpu.VMEM((NR + RT, NR), BF16),
            pltpu.VMEM((NR + RT, NR), BF16),
            pltpu.VMEM((12, 8, NR), F32),
            pltpu.VMEM((12, 8, NR), F32),
            pltpu.VMEM((2, 12, 8, NR), F32),
            pltpu.VMEM((2, 12, 8, NR), F32),
            pltpu.VMEM((3, 4, *tile), F32),
            pltpu.VMEM((3, 4, *tile), F32),
            pltpu.VMEM(block, F32),
            pltpu.VMEM(block, F32),
            pltpu.VMEM((TILES, *tile), F32),
            pltpu.VMEM((TILES, *tile), F32),
            pltpu.VMEM((TILES, *tile), F32),
            pltpu.VMEM((TILES, *tile), F32),
            pltpu.VMEM((GROUP, 3, *tile), F32),
            pltpu.VMEM((GROUP, 3, *tile), F32),
            pltpu.VMEM((GROUP, 3, *tile), F32),
            pltpu.VMEM((2, 3, *tile), F32),
            pltpu.VMEM((GROUP, 3, *tile), F32),
            pltpu.VMEM((GROUP, 3, *tile), F32),
            pltpu.VMEM((GROUP, 3, *tile), F32),
            pltpu.VMEM((BLOCKS, 3, *tile), F32),
            pltpu.VMEM((GROUP, 3, *tile), F32),
            dma((4,)),
            dma((2,)), dma((2,)), dma((2, 3)), dma((2, 3)),
            dma((2, 2)), dma((GROUP,)), dma((1,)), dma((GROUP,)), dma((2,)),
            dma((GROUP - 1,)), dma((GROUP - 1,)),
            dma((BLOCKS - 1,)), dma((BLOCKS - 1,)),
            dma((GROUP - 1,)), dma((GROUP - 1,)),
            dma((2,)), dma((2,)),
            pltpu.VMEM((REACH, 8, NR), F32),
            pltpu.SemaphoreType.REGULAR((3,)),
        ],
        compiler_params=pltpu.CompilerParams(
            collective_id=0, has_side_effects=True, vmem_limit_bytes=40 << 20
        ),
    )(*in_place, viscous_factor)
    return pl.pallas_call(
        write_out,
        name="write_out",
        out_shape=(pltpu.HBM(block, F32), pltpu.HBM(block, F32)),
        in_specs=[pl.BlockSpec(memory_space=pltpu.VMEM)] * len(kept),
        out_specs=(any_space, any_space),
        scratch_shapes=[pltpu.VMEM(block, F32), dma((2, 3))],
    )(*[pltpu.with_memory_space_constraint(x, pltpu.VMEM) for x in outs])


def solution(mesh):
    spec = P(None, "theta", "gz", None)
    return jax.shard_map(
        local, mesh=mesh, in_specs=(spec, P(), P(), P()), out_specs=(spec, spec), check_vma=False
    )
```

```python
import jax
import jax.numpy as jnp
from jax import lax
from jax.experimental import pallas as pl
from jax.experimental.pallas import tpu as pltpu
from jax.sharding import PartitionSpec as P

AXIAL_WEIGHTS = (0.75, -0.15, 1.0 / 60.0)
STEP_WEIGHT = 0.2
MIRROR_SIGNS = (-1.0, -1.0, 1.0)
MESH = pl.DeviceIdType.MESH
F32 = jnp.float32
BF16 = jnp.bfloat16
REACH = 10
PTS = 16
NR = 512
RT = 32
LANES = 128
TILES = NR // LANES
GROUP = 8
SECTORS = 128
BLOCKS = SECTORS // GROUP
ROWS = (range(0, REACH), range(PTS - REACH, PTS))
RELAY = (5, 2)
PLAIN_DOT = (((1,), (0,)), ((), ()))


def split(x):
    high = x.astype(BF16)
    return high, (x - high.astype(F32)).astype(BF16)


def dot3(x, w_high, w_low):
    high, low = split(x)
    out = lax.dot_general(high, w_low, PLAIN_DOT, preferred_element_type=F32)
    out = out + lax.dot_general(low, w_high, PLAIN_DOT, preferred_element_type=F32)
    return out + lax.dot_general(high, w_high, PLAIN_DOT, preferred_element_type=F32)


def rows_of(shape):
    return lax.broadcasted_iota(jnp.int32, shape, len(shape) - 2)


def lane(shape):
    return lax.broadcasted_iota(jnp.int32, shape, len(shape) - 1)


def doubled(q):
    return q * (2.0 - q)


def pack4(x, sub):
    middle = (sub == 3) | (sub == 4)
    return (
        jnp.where(middle, pltpu.roll(x[3], 3, 0), x[0]),
        jnp.where(sub == 3, pltpu.roll(x[3], 1, 0), jnp.where(sub == 4, pltpu.roll(x[3], 7, 0), x[1])),
        jnp.where(middle, pltpu.roll(x[3], 5, 0), x[2]),
    )


def unpack4(y, sub):
    fourth = jnp.where(
        sub < 2,
        pltpu.roll(y[0], 5, 0),
        jnp.where(
            sub == 2,
            pltpu.roll(y[1], 7, 0),
            jnp.where(sub == 5, pltpu.roll(y[1], 1, 0), pltpu.roll(y[2], 3, 0)),
        ),
    )
    return (y[0], y[1], y[2], fourth)


def axial_parts(x, sub):
    own = far = None
    for m, weight in enumerate(AXIAL_WEIGHTS, 1):
        upper = weight * pltpu.roll(x, 8 - m, 0)
        lower = weight * pltpu.roll(x, m, 0)
        inside = jnp.where(sub < 8 - m, upper, 0.0) - jnp.where(sub >= m, lower, 0.0)
        outside = jnp.where(sub < 8 - m, 0.0, upper) - jnp.where(sub >= m, 0.0, lower)
        own = inside if own is None else own + inside
        far = outside if far is None else far + outside
    return own, far


def kernel(
    v_hbm, op_hbm, sten_hbm, visc, loc, part, ends, pow_t, scale_t,
    sten,
    ext, op_v, wh, wl, esend, erecv, gsend, grecv, msend, mrecv, own_ax, far_ax,
    inv_t, w_t, big_t, inv_n, ssend, sum_in, hsend, halo_in, fb, up_in, ret, tot, car,
    in_sem, e_sem, mir_sem, up_sem, down_sem, g_sem, v_s, v_r, h_s, h_r,
    p1_s, p1_r, p2_s, p2_r, p3_s, p3_r, relay_in, relay_out, passing, chain,
):
    p = lax.axis_index("theta")
    g = lax.axis_index("gz")
    me = p % GROUP
    block = p // GROUP
    backward = me // TILES
    my_tile = me % TILES
    sub = rows_of((8, LANES))

    reads = [
        pltpu.make_async_copy(v_hbm, ext.at[:, pl.ds(REACH, PTS)], in_sem.at[0]),
        pltpu.make_async_copy(op_hbm, op_v, in_sem.at[1]),
        pltpu.make_async_copy(sten_hbm, sten, in_sem.at[2]),
    ]
    for r in reads:
        r.start()

    after = (p + 1) % SECTORS
    before = (p + SECTORS - 1) % SECTORS
    across = (p + SECTORS // 2) % SECTORS
    barrier = pltpu.get_barrier_semaphore()
    greeted = [(after, g), (before, g)]
    greeted += [(block * GROUP + (me + k) % GROUP, g) for k in range(1, GROUP)]
    greeted += [(p, 1 - g)]
    hop = [((p + d) % SECTORS, g) for d in (2 * GROUP, SECTORS - 2 * GROUP, 4 * GROUP, SECTORS - 4 * GROUP)]
    side_block = (block + 1 - 2 * (block % 2)) * GROUP + me
    greeted += [*hop[:2], (side_block, g)]
    for who in greeted:
        pl.semaphore_signal(barrier, inc=1, device_id=who, device_id_type=MESH)

    def cols(t):
        return pl.ds(pl.multiple_of(t * LANES, LANES), LANES)

    reads[0].wait()

    def pack_axial(t, carry):
        for i in range(PTS // 4):
            x = [ext[2, REACH + 4 * i + j, :, cols(t)] for j in range(4)]
            for j, y in enumerate(pack4(x, sub)):
                esend[3 * i + j, :, cols(t)] = y
        return carry

    lax.fori_loop(0, TILES, pack_axial, 0)
    quarter = lane((8, LANES)) // RT
    for c in range(3):
        for i in range(PTS // 4):
            line = ext[c, REACH + 4 * i, :, :LANES]
            for j in range(1, 4):
                line = jnp.where(quarter == j, pltpu.roll(ext[c, REACH + 4 * i + j, :, :LANES], RT * j, 1), line)
            msend[c, i] = MIRROR_SIGNS[c] * line

    pl.semaphore_wait(barrier, len(greeted))

    def tell(stage, whom):
        for who in whom:
            pl.semaphore_signal(chain.at[stage], inc=1, device_id=who, device_id_type=MESH)

    tell(0, hop[:2])

    def remote(src, dst, s_sem, r_sem, who):
        return pltpu.make_async_remote_copy(
            src_ref=src, dst_ref=dst, send_sem=s_sem, recv_sem=r_sem, device_id=who, device_id_type=MESH
        )

    def pair(src, dst, sem, who):
        return remote(src, dst, sem.at[0], sem.at[1], who)

    planes_e = pair(esend, erecv, e_sem, (p, 1 - g))
    halo_up, halo_down = [], []
    for c in range(3):
        halo_up.append(
            remote(ext.at[c, pl.ds(PTS, REACH)], ext.at[c, pl.ds(0, REACH)], up_sem.at[0, c], up_sem.at[1, c], (after, g))
        )
        halo_down.append(
            remote(
                ext.at[c, pl.ds(REACH, REACH)], ext.at[c, pl.ds(REACH + PTS, REACH)],
                down_sem.at[0, c], down_sem.at[1, c], (before, g),
            )
        )
    next_block, last_block = (block + 1) % BLOCKS, (block + BLOCKS - 1) % BLOCKS
    halo_up_last, halo_down_last = ext.at[0, pl.ds(PTS, REACH)], ext.at[0, pl.ds(REACH, REACH)]
    to_relay = [
        pair(halo_up_last, passing, relay_in, (next_block * GROUP + RELAY[0], g)),
        pair(halo_down_last, passing, relay_in, (last_block * GROUP + RELAY[1], g)),
    ]
    relayed = [
        pair(passing, ext.at[0, pl.ds(0, REACH)], relay_out, (block * GROUP, g)),
        pair(passing, ext.at[0, pl.ds(REACH + PTS, REACH)], relay_out, (block * GROUP + GROUP - 1, g)),
    ]
    mirror = pair(msend, mrecv, mir_sem, (across, g))
    planes = [
        remote(gsend.at[c], grecv.at[c], g_sem.at[0, c], g_sem.at[1, c], (p, 1 - g)) for c in range(2)
    ]
    first, final = me == 0, me == GROUP - 1
    planes_e.start()
    halo_up[1].start()
    halo_down[1].start()

    @pl.when(me != GROUP - 1)
    def _():
        halo_up[0].start()
        halo_up[2].start()

    @pl.when(me != 0)
    def _():
        halo_down[0].start()
        halo_down[2].start()

    reads[2].wait()
    radius = lane((8, NR)).astype(F32) + 0.5
    inverse_r = 1.0 / radius
    coef = visc[0] * inverse_r * inverse_r
    half = 0.5 / coef
    gap = jnp.sqrt(half * (2.0 + half)) - half
    rho = 1.0 - gap
    scale = 1.0 / jnp.sqrt(1.0 + 4.0 * coef)
    gap16 = doubled(doubled(doubled(doubled(gap))))
    gap128 = doubled(doubled(doubled(gap16)))
    whole = doubled(doubled(doubled(doubled(gap128))))
    for t in range(TILES):
        here = slice(t * LANES, (t + 1) * LANES)
        inv_t[t] = inverse_r[:, here]
        scale_t[t] = scale[:, here]
        w_t[t] = 1.0 - gap16[:, here]
        big_t[t] = 1.0 - gap128[:, here]
        inv_n[t] = 1.0 / whole[:, here]
        power = jnp.ones((8, LANES), F32)
        for j in range(PTS + 1):
            pow_t[t, j] = power
            power = power * rho[:, here]

    pl.semaphore_wait(chain.at[0], 2)
    tell(1, hop[2:])

    def spread(t, carry):
        for c in range(3):
            for i in range(PTS // 4):
                far = []
                for j in range(4):
                    row = 4 * i + j
                    inside, outside = axial_parts(ext[c, REACH + row, :, cols(t)], sub)
                    own_ax[c, row, :, cols(t)] = inside
                    far_ax[c, row, :, cols(t)] = outside
                    far.append(outside)
                if c < 2:
                    for j, y in enumerate(pack4(far, sub)):
                        gsend[c, 3 * i + j, :, cols(t)] = y
        return carry

    lax.fori_loop(0, TILES, spread, 0)

    reads[1].wait()
    op_high, op_low = split(op_v[...])
    wh[...] = op_high
    wl[...] = op_low
    for c in range(3):
        lines = ext[c, pl.ds(REACH, PTS)].reshape(PTS * 8, NR)
        part[c] = dot3(lines, wh[pl.ds(0, NR)], wl[pl.ds(0, NR)]).reshape(PTS, 8, NR)

    pl.semaphore_wait(chain.at[1], 2)
    mirror.start()
    tell(2, [(side_block, g)])

    def azimuth(t, carry):
        inv = inv_t[t]
        for c in range(3):
            x = [ext[c, REACH + k, :, cols(t)] for k in range(PTS)]
            for row in range(PTS):
                grad = None
                for k in range(max(0, row - REACH), min(PTS, row + REACH + 1)):
                    tap = sten[k - row + REACH] * x[k]
                    grad = tap if grad is None else grad + tap
                a = ext[0, REACH + row, :, cols(t)]
                b = ext[1, REACH + row, :, cols(t)]
                e = ext[2, REACH + row, :, cols(t)]
                if c == 0:
                    grad = grad - b
                if c == 1:
                    grad = grad + a
                part[c, row, :, cols(t)] = (
                    a * part[c, row, :, cols(t)] + (b * inv) * grad + e * own_ax[c, row, :, cols(t)]
                )
        return carry

    lax.fori_loop(0, TILES, azimuth, 0)

    def local_sums(t, carry):
        rho = pow_t[t, 1]
        for c in range(3):
            ahead = back = None
            for row in range(PTS):
                right = ext[c, REACH + row, :, cols(t)] - STEP_WEIGHT * part[c, row, :, cols(t)]
                ahead = right if row == 0 else rho * ahead + right
                back = right if row == 0 else back + pow_t[t, row] * right
            fb[t, c] = ahead
            fb[TILES + t, c] = back
        return carry

    lax.fori_loop(0, TILES, local_sums, 0)

    @pl.when(final)
    def _():
        halo_down[1].wait_recv()
        to_relay[0].start()
        halo_up[2].start()

    @pl.when(first)
    def _():
        halo_up[1].wait_recv()
        to_relay[1].start()
        halo_down[2].start()

    planes_e.wait_recv()

    sums = []
    for turn in range(TILES):
        t = (my_tile + turn) % TILES
        rho = pow_t[t, 1]
        e = []
        for i in range(PTS // 4):
            e += unpack4([erecv[3 * i + j, :, cols(t)] for j in range(3)], sub)
        for c in range(3):
            ahead = back = None
            for row in range(PTS):
                x = e[row] * far_ax[c, row, :, cols(t)]
                ahead = x if row == 0 else rho * ahead + x
                back = x if row == 0 else back + pow_t[t, row] * x
            ssend[t, c] = -STEP_WEIGHT * ahead
            ssend[TILES + t, c] = -STEP_WEIGHT * back
        for k in (t, TILES + t):
            cp = remote(
                ssend.at[k], sum_in.at[me], v_s.at[len(sums)], v_r.at[0], (block * GROUP + k, 1 - g)
            )
            cp.start()
            sums.append(cp)

    def halo_taps(t, c, row, shift):
        span = range(row, REACH) if shift[0] == 0 else range(REACH + PTS, row + 2 * REACH + 1)
        grad = None
        for k in span:
            tap = sten[k - row] * ext[c, k + shift[1], :, cols(t)]
            grad = tap if grad is None else grad + tap
        return grad

    def edge_sums(side):
        shift = (side, PTS if side == 0 else -PTS)
        theirs = REACH + PTS if side == 0 else REACH - PTS

        def body(t, carry):
            inv, rho = inv_t[t], pow_t[t, 1]
            for c in range(3):
                ahead = back = None
                for row in ROWS[side]:
                    x = (ext[1, row + theirs, :, cols(t)] * inv) * halo_taps(t, c, row, shift)
                    ahead = x if ahead is None else rho * ahead + x
                    x = pow_t[t, row] * x
                    back = x if back is None else back + x
                if side == 0:
                    ahead = ahead * pow_t[t, PTS - REACH]
                hsend[t, c] = -STEP_WEIGHT * ahead
                hsend[TILES + t, c] = -STEP_WEIGHT * back
            return carry

        lax.fori_loop(0, TILES, body, 0)

    def edge_copies(side):
        to = (block + 1) % BLOCKS if side == 0 else (block + BLOCKS - 1) % BLOCKS
        return [
            remote(hsend.at[k], halo_in.at[side], h_s.at[k], h_r.at[side], (to * GROUP + k, g)) for k in range(GROUP)
        ]

    edge = [edge_copies(0), edge_copies(1)]

    @pl.when(final)
    def _():
        edge_sums(0)
        for cp in edge[0]:
            cp.start()

    @pl.when(first)
    def _():
        edge_sums(1)
        for cp in edge[1]:
            cp.start()

    def add_halo(side, summed):
        def body(t, carry):
            inv, rho = inv_t[t], pow_t[t, 1]
            for c in range(3):
                ahead = back = None
                for row in ROWS[side]:
                    x = (ext[1, REACH + row, :, cols(t)] * inv) * halo_taps(t, c, row, (side, 0))
                    part[c, row, :, cols(t)] = part[c, row, :, cols(t)] + x
                    if summed:
                        ahead = x if ahead is None else rho * ahead + x
                        x = pow_t[t, row] * x
                        back = x if back is None else back + x
                if summed:
                    if side == 0:
                        ahead = ahead * pow_t[t, PTS - REACH]
                    fb[t, c] = fb[t, c] - STEP_WEIGHT * ahead
                    fb[TILES + t, c] = fb[TILES + t, c] - STEP_WEIGHT * back
            return carry

        lax.fori_loop(0, TILES, body, 0)

    @pl.when(me != 0)
    def _():
        for cp in (halo_up[1], halo_up[0], halo_up[2]):
            cp.wait_recv()
        add_halo(0, True)

    @pl.when(me != GROUP - 1)
    def _():
        for cp in (halo_down[1], halo_down[0], halo_down[2]):
            cp.wait_recv()
        add_halo(1, True)

    mirror.wait_recv()
    for i in range(PTS // 4):
        lines = []
        for c in range(3):
            packed = mrecv[c, i]
            lines += [packed[:, :RT]] + [pltpu.roll(packed, LANES - RT * j, 1)[:, :RT] for j in range(1, 4)]
        more = dot3(jnp.concatenate(lines, axis=0), wh[pl.ds(NR, RT)], wl[pl.ds(NR, RT)]).reshape(3, 4, 8, NR)
        for t in range(TILES):
            here = slice(t * LANES, (t + 1) * LANES)
            for c in range(3):
                ahead, back = fb[t, c], fb[TILES + t, c]
                for j in range(4):
                    row = 4 * i + j
                    x = ext[0, REACH + row, :, here] * more[c, j, :, here]
                    part[c, row, :, here] = part[c, row, :, here] + x
                    x = -STEP_WEIGHT * x
                    ahead = ahead + pow_t[t, PTS - 1 - row] * x
                    back = back + pow_t[t, row] * x
                fb[t, c] = ahead
                fb[TILES + t, c] = back

    one, two, three = [], [], []
    for k in sorted(range(1, GROUP), key=lambda k: abs(k - GROUP // 2)):
        other = (me + k) % GROUP
        cp = remote(fb.at[other], up_in.at[me], p1_s.at[k - 1], p1_r.at[k - 1], (block * GROUP + other, g))
        cp.start()
        one.append(cp)
    up_in[me] = fb[me]
    planes[0].start()

    def finish_term(c):
        def body(t, carry):
            rho = pow_t[t, 1]
            right = []
            left = []
            for i in range(PTS // 4):
                if c < 2:
                    far = unpack4([grecv[c, 3 * i + j, :, cols(t)] for j in range(3)], sub)
                else:
                    far = unpack4([erecv[3 * i + j, :, cols(t)] for j in range(3)], sub)
                for j in range(4):
                    row = 4 * i + j
                    grad = far[j]
                    if c == 2:
                        grad = axial_parts(grad, sub)[1]
                    else:
                        grad = jnp.where((sub == 3) | (sub == 4), 0.0, grad)
                    term = part[c, row, :, cols(t)] + ext[2, REACH + row, :, cols(t)] * grad
                    part[c, row, :, cols(t)] = term
                    right.append(ext[c, REACH + row, :, cols(t)] - STEP_WEIGHT * term)
                    left.append(right[row] if row == 0 else right[row] + rho * left[row - 1])
            run = None
            for row in range(PTS - 1, -1, -1):
                if run is None:
                    loc[c, row, :, cols(t)] = left[row]
                    run = right[row]
                else:
                    run = rho * run
                    loc[c, row, :, cols(t)] = left[row] + run
                    run = right[row] + run
            return carry

        lax.fori_loop(0, TILES, body, 0)

    def entry(k):
        return k + backward * (GROUP - 1 - 2 * k)

    pl.semaphore_wait(chain.at[2], 1)
    for cp in (*one, edge[0][0], edge[1][0]):
        cp.wait_recv()
    remote(ssend, sum_in, v_s.at[0], v_r.at[0], (p, 1 - g)).wait_recv()
    for k in range(GROUP):
        total = up_in[k] + sum_in[k]
        if k == 0:
            total = total + halo_in[0]
        if k == GROUP - 1:
            total = total + halo_in[1]
        up_in[k] = total
    w = w_t[my_tile]
    run = up_in[entry(0)]
    for k in range(1, GROUP):
        run = up_in[entry(k)] + w * run
    tot[block] = run
    for k in sorted(range(1, BLOCKS), key=lambda k: abs(k - BLOCKS // 2)):
        cp = remote(
            tot.at[block], tot.at[block], p2_s.at[k - 1], p2_r.at[k - 1],
            (((block + k) % BLOCKS) * GROUP + me, g),
        )
        cp.start()
        two.append(cp)
    planes[1].start()


    for side in range(2):

        @pl.when(me == RELAY[side])
        def _(side=side):
            to_relay[side].wait_recv()
            relayed[side].start()

    for cp in two:
        cp.wait_recv()
    big = big_t[my_tile]
    run = tot[block]
    for m in range(BLOCKS - 1, 0, -1):
        run = tot[(block + (2 * backward - 1) * m + BLOCKS) % BLOCKS] + big * run
    run = run * inv_n[my_tile]
    for k in range(GROUP):
        ret[entry(k)] = run
        run = up_in[entry(k)] + w * run
    for k in sorted(range(1, GROUP), key=lambda k: abs(k - GROUP // 2)):
        other = (me + k) % GROUP
        cp = remote(ret.at[other], car.at[me], p3_s.at[k - 1], p3_r.at[k - 1], (block * GROUP + other, g))
        cp.start()
        three.append(cp)
    car[me] = ret[me]

    @pl.when(first)
    def _():
        relayed[0].wait_recv()
        halo_up[2].wait_recv()
        add_halo(0, False)

    @pl.when(final)
    def _():
        relayed[1].wait_recv()
        halo_down[2].wait_recv()
        add_halo(1, False)

    finish_term(2)
    for c in range(2):
        planes[c].wait_recv()
        finish_term(c)

    for cp in three:
        cp.wait_recv()

    for t in range(TILES):
        ends[t] = scale_t[t] * car[t]
        ends[TILES + t] = scale_t[t] * car[TILES + t]
    for cp in (planes_e, *halo_up[1:], *halo_down[1:], mirror, *sums, *planes, *one, *two, *three):
        cp.wait_send()

    @pl.when(me != GROUP - 1)
    def _():
        halo_up[0].wait_send()

    @pl.when(me != 0)
    def _():
        halo_down[0].wait_send()

    for side in range(2):

        @pl.when(me == RELAY[side])
        def _(side=side):
            relayed[side].wait_send()

    for side, here in ((0, final), (1, first)):

        @pl.when(here)
        def _(side=side):
            for cp in (*edge[side], to_relay[side]):
                cp.wait_send()


def write_out(loc, part, ends, pow_t, scale_t, new_out, non_out, new, sem):
    def copy(src, dst, k, c):
        cp = pltpu.make_async_copy(src.at[c], dst.at[c], sem.at[k, c])
        cp.start()
        return cp

    copies = [copy(part, non_out, 1, c) for c in range(3)]
    for c in range(3):
        for t in range(TILES):
            here = slice(t * LANES, (t + 1) * LANES)
            for row in range(PTS):
                new[c, row, :, here] = (
                    scale_t[t] * loc[c, row, :, here]
                    + pow_t[t, row + 1] * ends[t, c]
                    + pow_t[t, PTS - row] * ends[TILES + t, c]
                )
        copies.append(copy(new, new_out, 0, c))
    for cp in copies:
        cp.wait()


def local(velocity, radial_op, azimuth_stencil, viscous_factor):
    dma = pltpu.SemaphoreType.DMA
    block = velocity.shape
    any_space = pl.BlockSpec(memory_space=pl.ANY)
    in_place = [
        pltpu.with_memory_space_constraint(x, pltpu.HBM) for x in (velocity, radial_op.T, azimuth_stencil)
    ]
    tile = (8, LANES)
    kept = tuple(
        jax.ShapeDtypeStruct(shape, F32)
        for shape in (block, block, (GROUP, 3, *tile), (TILES, PTS + 1, *tile), (TILES, *tile))
    )
    outs = pl.pallas_call(
        kernel,
        name="substep",
        out_shape=kept,
        in_specs=[any_space] * 3 + [pl.BlockSpec(memory_space=pltpu.SMEM)],
        out_specs=(pl.BlockSpec(memory_space=pltpu.VMEM),) * len(kept),
        scratch_shapes=[
            pltpu.SMEM((2 * REACH + 1,), F32),
            pltpu.VMEM((3, PTS + 2 * REACH, 8, NR), F32),
            pltpu.VMEM((NR + RT, NR), F32),
            pltpu.VMEM((NR + RT, NR), BF16),
            pltpu.VMEM((NR + RT, NR), BF16),
            pltpu.VMEM((12, 8, NR), F32),
            pltpu.VMEM((12, 8, NR), F32),
            pltpu.VMEM((2, 12, 8, NR), F32),
            pltpu.VMEM((2, 12, 8, NR), F32),
            pltpu.VMEM((3, 4, *tile), F32),
            pltpu.VMEM((3, 4, *tile), F32),
            pltpu.VMEM(block, F32),
            pltpu.VMEM(block, F32),
            pltpu.VMEM((TILES, *tile), F32),
            pltpu.VMEM((TILES, *tile), F32),
            pltpu.VMEM((TILES, *tile), F32),
            pltpu.VMEM((TILES, *tile), F32),
            pltpu.VMEM((GROUP, 3, *tile), F32),
            pltpu.VMEM((GROUP, 3, *tile), F32),
            pltpu.VMEM((GROUP, 3, *tile), F32),
            pltpu.VMEM((2, 3, *tile), F32),
            pltpu.VMEM((GROUP, 3, *tile), F32),
            pltpu.VMEM((GROUP, 3, *tile), F32),
            pltpu.VMEM((GROUP, 3, *tile), F32),
            pltpu.VMEM((BLOCKS, 3, *tile), F32),
            pltpu.VMEM((GROUP, 3, *tile), F32),
            dma((4,)),
            dma((2,)), dma((2,)), dma((2, 3)), dma((2, 3)),
            dma((2, 2)), dma((GROUP,)), dma((1,)), dma((GROUP,)), dma((2,)),
            dma((GROUP - 1,)), dma((GROUP - 1,)),
            dma((BLOCKS - 1,)), dma((BLOCKS - 1,)),
            dma((GROUP - 1,)), dma((GROUP - 1,)),
            dma((2,)), dma((2,)),
            pltpu.VMEM((REACH, 8, NR), F32),
            pltpu.SemaphoreType.REGULAR((3,)),
        ],
        compiler_params=pltpu.CompilerParams(
            collective_id=0, has_side_effects=True, vmem_limit_bytes=40 << 20
        ),
    )(*in_place, viscous_factor)
    return pl.pallas_call(
        write_out,
        name="write_out",
        out_shape=(pltpu.HBM(block, F32), pltpu.HBM(block, F32)),
        in_specs=[pl.BlockSpec(memory_space=pltpu.VMEM)] * len(kept),
        out_specs=(any_space, any_space),
        scratch_shapes=[pltpu.VMEM(block, F32), dma((2, 3))],
    )(*[pltpu.with_memory_space_constraint(x, pltpu.VMEM) for x in outs])


def solution(mesh):
    spec = P(None, "theta", "gz", None)
    return jax.shard_map(
        local, mesh=mesh, in_specs=(spec, P(), P(), P()), out_specs=(spec, spec), check_vma=False
    )
```
